512 devices in a mesh: seq: 32 (over z, core), head: 16 (over y, x).
Axes of the slice: x: 4, y: 4, z: 16, core: 2. Of those that a mesh axis runs over, the one named last changes fastest.
Arguments:
- hidden_in: bfloat16 [8192, 4096], P('seq'), may hold values from -6 to 6
- w_qkv: bfloat16 [3, 4096, 4096], P(None, 'seq', 'head'), may hold values from -0.09375 to 0.09375
- doc_starts: int32 [9], replicated, may hold values from 0 to 8191, as said below
- beta_codes: int32 [8192, 32], P('seq', 'head'), may hold values from 0 to 4, as said below
- w_out: bfloat16 [4096, 4096], P('head', 'seq'), may hold values from -0.1875 to 0.1875
Outputs:
- layer_out: bfloat16 [8192, 4096], P('seq', 'head')
The draws below stay inside these ranges and needn't reach their ends.
Inputs may be any that keep to these rules, and one draw needn't show every extreme that they name: `doc_starts`: strictly rising; the first is 0 and the last is 8191, a one-token final document. `beta_codes`: integer codes of the write strength beta = 1.6 + 0.1 * code.
All inputs are finite; a program needn't handle non-finite values.
Results may differ from the reference program's by a relative error of at most 0.02.
Values may be sent and summed in bfloat16 or wider, within the bound.
No kernel may reach another device: no remote copies, remote signals or barrier semaphores. Data moves between devices by JAX's collectives and lax.ppermute only.
A program may use at most 64 MiB of HBM per device.

```python
import jax
import jax.numpy as jnp
from jax import lax

D = 4096
HEADS = 32
HD = 128
TOKENS = 8192
DOCS = 9


def draw_doc_starts(key, part):
    inner = jax.random.permutation(key, TOKENS - 2)[:DOCS - 2].astype(jnp.int32) + 1
    first = jnp.zeros((1,), jnp.int32)
    final = jnp.full((1,), TOKENS - 1, jnp.int32)
    return jnp.concatenate([first, jnp.sort(inner), final])


def draw_beta_codes(key, part):
    key_level, key_noise, key_pick = jax.random.split(jax.random.fold_in(key, 7), 3)
    level = jax.random.randint(key_level, (1, HEADS), 0, 5)
    noise = jax.random.randint(key_noise, (TOKENS, HEADS), 0, 5)
    picker = jax.random.randint(key_pick, (TOKENS, HEADS), 0, 4)
    return jnp.where(picker == 0, noise, level).astype(jnp.int32)


def raised(values, stream_key, source, target, blocks, factor):
    owner, partner = [(jnp.arange(values.shape[position]) // (values.shape[position] // blocks)).reshape([-1 if axis == position else 1 for axis in range(values.ndim)]) for position in (source, target)]
    chosen = jax.random.permutation(stream_key, blocks)[partner]
    strong = (owner == chosen) | (owner == (partner + blocks // 2) % blocks)
    return jnp.where(strong, factor * values, values)


def shard_levels(rng, dims, cuts, least, high):
    factor_of = 1.0
    for dim, parts in cuts:
        draws = jax.random.uniform(jax.random.fold_in(jax.random.fold_in(rng, 6), dim), (parts,), jnp.float32, least / len(cuts), high / len(cuts))
        factor_of = factor_of * jnp.repeat(jnp.exp(draws), dims[dim] // parts).reshape((-1,) + (1,) * (len(dims) - 1 - dim))
    return factor_of


def normal_values(stream_key, dims, spread, most, cuts=(), held_as=jnp.bfloat16):
    array = spread * jax.random.normal(stream_key, dims, jnp.float32)
    if cuts:
        array = array * shard_levels(stream_key, dims, cuts, -0.22, 0.18)
    return jnp.clip(array, -most, most).astype(held_as)


def gaussian_with(rng, shape, scale, reach, pieces, heavy, kind=jnp.bfloat16):
    values = scale * jax.random.normal(rng, shape, jnp.float32)
    if pieces:
        values = values * shard_levels(rng, shape, pieces, -0.22, 0.18)
    return jnp.clip(raised(values, jax.random.fold_in(rng, 3), *heavy), -reach, reach).astype(kind)


def setup_inputs(seed: int = 0) -> dict:
    seeds = jax.random.split(jax.random.key(seed), 6)
    return {
        "hidden_in": normal_values(seeds[0], (TOKENS, D), 1.0, 6.0, ((0, 32),)),
        "w_qkv": normal_values(seeds[1], (3, D, HEADS * HD), D ** -0.5, 0.09375, ((1, 32), (2, 16))),
        "doc_starts": draw_doc_starts(jax.random.fold_in(seeds[5], 71), 0),
        "beta_codes": draw_beta_codes(jax.random.fold_in(seeds[5], 71), 0),
        "w_out": gaussian_with(seeds[4], (HEADS * HD, D), (HEADS * HD) ** -0.5, 0.1875, ((0, 16), (1, 32)), (0, 1, 32, 2.75)),
    }


highest_accuracy = lax.Precision.HIGHEST

def unit_rows(matrix):
    return matrix * lax.rsqrt(lax.optimization_barrier(jnp.sum(matrix * matrix, axis=-1, keepdims=True)) + 1e-06)

def recur_step(state_matrix, inputs):
    step_query, step_key, value_t, beta_t, keep_t = inputs
    state_matrix = state_matrix * keep_t
    retrieved_value = jnp.einsum('of,ofg->og', step_key, state_matrix, precision=highest_accuracy)
    state_matrix = state_matrix + beta_t[:, None, None] * step_key[:, :, None] * (value_t - retrieved_value)[:, None, :]
    step_output = jnp.einsum('of,ofg->og', step_query, state_matrix, precision=highest_accuracy)
    return (state_matrix, step_output)

def reference(hidden_in, w_qkv, doc_starts, beta_codes, w_out):
    projected = []
    for which in range(3):
        partial_projection = jnp.dot(hidden_in, w_qkv[which], preferred_element_type=jnp.float32).astype(jnp.bfloat16)
        projected.append(partial_projection.astype(jnp.float32).reshape(TOKENS, HEADS, HD))
    queries = unit_rows(projected[0])
    keys_all = unit_rows(projected[1])
    values_all = projected[2]
    betas = 1.6 + 0.1 * beta_codes.astype(jnp.float32)
    positions = jnp.arange(TOKENS, dtype=jnp.int32)
    is_start = jnp.any(positions[:, None] == doc_starts[None, :], axis=1)
    keep_mask = 1.0 - is_start.astype(jnp.float32)
    state_zero = jnp.zeros((HEADS, HD, HD), jnp.float32)
    final_state, outputs = lax.scan(recur_step, state_zero, (queries, keys_all, values_all, betas, keep_mask))
    normed = outputs * lax.rsqrt(lax.optimization_barrier(jnp.mean(outputs * outputs, axis=-1, keepdims=True)) + 1e-05)
    normed = normed.astype(jnp.bfloat16).reshape(TOKENS, HEADS * HD)
    return jnp.dot(normed, w_out, preferred_element_type=jnp.float32).astype(jnp.bfloat16)
```

```python
import jax
import jax.numpy as jnp
import numpy as np
from jax import lax
from jax.experimental import pallas as pl
from jax.experimental.pallas import tpu as pltpu
from jax.sharding import Mesh
from jax.sharding import PartitionSpec as P

F32 = jnp.float32
BF16 = jnp.bfloat16
F16 = jnp.float16
HD = 128
TOK = 512
W_SCALE = 2.0**19
L_SCALE = 2.0**-6
NN = (((1,), (0,)), ((), ()))


def split(a):
    hi = a.astype(BF16)
    return hi, (a - hi.astype(F32)).astype(BF16)


def dot(a, b):
    return lax.dot_general(a, b, NN, preferred_element_type=F32)


def mm3s(a, b):
    (ah, al), (bh, bl) = a, b
    return dot(
        jnp.concatenate([ah, ah, al], axis=1), jnp.concatenate([bh, bl, bh], axis=0)
    )


def mm3(a, b):
    return mm3s(split(a), split(b))


def unit_rows(m):
    return m * lax.rsqrt(jnp.sum(m * m, axis=-1, keepdims=True) + 1e-06)


def count_le(ds_ref, pos):
    total = jnp.zeros(jnp.shape(pos), jnp.int32)
    for j in range(ds_ref.shape[0]):
        total = total + (ds_ref[j] <= pos).astype(jnp.int32)
    return total


def local_kernel(meta_ref, ds_ref, own_ref, sib_ref, beta_ref, tl_ref, b_ref):
    pos0 = meta_ref[0] * TOK
    first = meta_ref[1] == 0
    half = TOK // 2

    def tokens(p):
        own = own_ref[p].astype(F32)
        sib = sib_ref[p].astype(F32)
        return jnp.concatenate(
            [jnp.where(first, own, sib), jnp.where(first, sib, own)], axis=0
        )

    query = unit_rows(tokens(0))
    key = unit_rows(tokens(1))
    value = tokens(2)
    beta = 1.6 + 0.1 * beta_ref[...]
    doc_col = count_le(ds_ref, pos0 + lax.broadcasted_iota(jnp.int32, (TOK, 1), 0))
    doc_row = count_le(ds_ref, pos0 + lax.broadcasted_iota(jnp.int32, (1, TOK), 1))
    prev_doc = count_le(ds_ref, pos0 - 1)
    last_doc = count_le(ds_ref, pos0 + TOK - 1)
    carry_in = (doc_col == prev_doc).astype(F32)
    tail_row = (doc_row == last_doc).astype(F32)
    last_keep = (last_doc == prev_doc).astype(F32)

    key_s = split(key)
    key_t = jnp.transpose(key)
    key_ts = split(key_t)

    def part(pair, rows, cols):
        return pair[0][rows, cols], pair[1][rows, cols]

    every = slice(None)

    def system(rows, cols, inclusive=False, left=None, scale=None):
        gram = mm3s(part(left, rows, every), part(key_ts, every, cols))
        shape = gram.shape
        r = lax.broadcasted_iota(jnp.int32, shape, 0) + rows.start
        c = lax.broadcasted_iota(jnp.int32, shape, 1) + cols.start
        keep = (c <= r) if inclusive else (c < r)
        keep = keep & (doc_col[rows] == doc_row[:, cols])
        if scale is not None:
            gram = scale[rows] * gram
        return jnp.where(keep, gram, 0.0)

    quarter = [slice(128 * i, 128 * i + 128) for i in range(4)]
    rows128 = lax.broadcasted_iota(jnp.int32, (128, 128), 0)
    cols128 = lax.broadcasted_iota(jnp.int32, (128, 128), 1)
    eye128 = (rows128 == cols128).astype(F32)
    diag = [system(s, s, left=key_s, scale=beta) for s in quarter]
    inv = []
    for a in diag:
        m = ((rows128 >> 1) == (cols128 >> 1)) & (rows128 != cols128)
        inv.append(eye128 - jnp.where(m, a, 0.0))
    for lev in range(1, 7):
        m = ((rows128 >> (lev + 1)) == (cols128 >> (lev + 1))) & (
            (rows128 >> lev) != (cols128 >> lev)
        )
        xs = [split(x) for x in inv]
        ys = [mm3s(x, split(jnp.where(m, a, 0.0))) for x, a in zip(xs, diag)]
        inv = [x - mm3s(split(y), s) for x, y, s in zip(inv, ys, xs)]
    pair_inv = []
    for i in (0, 2):
        off = system(quarter[i + 1], quarter[i], left=key_s, scale=beta)
        low = -mm3(mm3(inv[i + 1], off), inv[i])
        top = jnp.concatenate([inv[i], jnp.zeros((128, 128), F32)], axis=1)
        bottom = jnp.concatenate([low, inv[i + 1]], axis=1)
        pair_inv.append(jnp.concatenate([top, bottom], axis=0))
    lo, hi = slice(0, half), slice(half, TOK)
    right = beta * jnp.concatenate([carry_in * key, value], axis=1)
    cross = system(hi, lo, left=key_s, scale=beta)
    wu_lo = mm3(pair_inv[0], right[lo])
    wu_lo_s = split(wu_lo)
    wu_hi = mm3(pair_inv[1], right[hi] - mm3s(split(cross), wu_lo_s))
    wu_s = (
        jnp.concatenate([wu_lo_s[0], split(wu_hi)[0]], axis=0),
        jnp.concatenate([wu_lo_s[1], split(wu_hi)[1]], axis=0),
    )
    tail = split(tail_row * key_t)
    tl = mm3s(tail, wu_s)
    trans = last_keep * eye128 - tl[:, :HD]
    tl_ref[0:HD, :] = trans
    tl_ref[HD : 2 * HD, :] = tl[:, HD:] * L_SCALE

    query_s = split(query)
    p_ll = split(system(lo, lo, inclusive=True, left=query_s))
    p_h = split(
        jnp.concatenate(
            [
                mm_masked
                for mm_masked in (
                    system(hi, lo, inclusive=True, left=query_s),
                    system(hi, hi, inclusive=True, left=query_s),
                )
            ],
            axis=1,
        )
    )
    out_lo = mm3s(p_ll, part(wu_s, lo, every))
    out_hi = mm3s(p_h, wu_s)
    b_ref[0, lo, :] = carry_in[lo] * query[lo] - out_lo[:, :HD]
    b_ref[0, hi, :] = carry_in[hi] * query[hi] - out_hi[:, :HD]
    b_ref[1, lo, :] = out_lo[:, HD:]
    b_ref[1, hi, :] = out_hi[:, HD:]


def finish_kernel(meta_ref, ds_ref, tl_ref, b_ref, out_ref):
    here = meta_ref[0]
    start = jnp.int32(0)
    for j in range(ds_ref.shape[0]):
        pos = ds_ref[j]
        start = jnp.where(pos < here * TOK, jnp.maximum(start, pos // TOK), start)

    def fold(j, state):
        block = tl_ref[j]
        sh, sl = split(state)
        left = block[:HD]
        add = block[HD:].astype(F32) * (1.0 / L_SCALE)
        return dot(jnp.concatenate([left, left], axis=1), jnp.concatenate([sh, sl], axis=0)) + add

    state = lax.fori_loop(start, here, fold, jnp.zeros((HD, HD), F32))
    out = mm3(b_ref[0], state) + b_ref[1]
    out = out * lax.rsqrt(jnp.mean(out * out, axis=-1, keepdims=True) + 1e-05)
    out_ref[...] = out.astype(BF16)


SMEM = pl.BlockSpec(memory_space=pltpu.SMEM)
VMEM = pl.BlockSpec(memory_space=pltpu.VMEM)


def local_terms(meta, doc_starts, own, sib, beta):
    return pl.pallas_call(
        local_kernel,
        out_shape=(
            jax.ShapeDtypeStruct((2 * HD, HD), F32),
            jax.ShapeDtypeStruct((2, TOK, HD), F32),
        ),
        in_specs=[SMEM, SMEM, VMEM, VMEM, VMEM],
        out_specs=(VMEM, VMEM),
        compiler_params=pltpu.CompilerParams(vmem_limit_bytes=48 << 20),
    )(meta, doc_starts, own, sib, beta)


def finish(meta, doc_starts, tl, b):
    return pl.pallas_call(
        finish_kernel,
        out_shape=jax.ShapeDtypeStruct((TOK, HD), BF16),
        in_specs=[SMEM, SMEM, VMEM, VMEM],
        out_specs=VMEM,
        compiler_params=pltpu.CompilerParams(vmem_limit_bytes=32 << 20),
    )(meta, doc_starts, tl, b)


def swap(value):
    return lax.ppermute(value, "c", [(0, 1), (1, 0)])


def per_device(hidden_in, w_qkv, doc_starts, beta_codes, w_out):
    z = lax.axis_index("z")
    c = lax.axis_index("c")
    first = c == 0
    half = hidden_in.shape[0]
    meta = jnp.stack([z, c]).astype(jnp.int32)

    def pick(array, axis, index):
        return lax.dynamic_slice_in_dim(array, index * HD, HD, axis=axis)

    codes = beta_codes.astype(BF16)
    give = jnp.concatenate(
        [
            pick(w_qkv, 2, 1 - c).reshape(3 * HD, HD),
            pick(w_out, 0, 1 - c),
            lax.dynamic_slice_in_dim(codes, 1 - c, 1, axis=1).reshape(half // HD, HD),
            jnp.zeros((16 - half // HD, HD), BF16),
        ],
        axis=0,
    )
    got = swap(give)
    hidden_sib = swap(hidden_in)

    def ordered(mine, other, axis=0):
        return jnp.concatenate(
            [jnp.where(first, mine, other), jnp.where(first, other, mine)], axis=axis
        )

    w_mine = pick(w_qkv, 2, c).reshape(1, 3, HD, HD)
    w_chip = ordered(w_mine, got[: 3 * HD].reshape(1, 3, HD, HD))
    w_f16 = (w_chip.astype(F32) * W_SCALE).astype(F16)
    w_all = lax.all_gather(w_f16, "z", axis=0)
    w_all = (w_all.astype(F32) * (1.0 / W_SCALE)).astype(BF16)

    wo_chip = ordered(pick(w_out, 0, c), got[3 * HD : 4 * HD], axis=1)
    wo_rows = lax.all_gather(wo_chip, "z", axis=0)
    wo_cols = lax.all_to_all(wo_rows, "h", 0, 0)

    beta_mine = lax.dynamic_slice_in_dim(codes, c, 1, axis=1)
    beta = ordered(beta_mine, got[4 * HD : 4 * HD + half // HD].reshape(half, 1)).astype(F32)

    def project(hid):
        return jnp.einsum(
            "tzcd,zcpde->pte",
            hid.reshape(half, w_all.shape[0], 2, HD),
            w_all,
            preferred_element_type=F32,
        ).astype(BF16)

    tl, b = local_terms(meta, doc_starts, project(hidden_in), project(hidden_sib), beta)
    tl_all = lax.all_gather(tl.astype(F16), "z", axis=0).astype(BF16)
    normed = finish(meta, doc_starts, tl_all, b)
    normed_all = lax.all_gather(normed.astype(F16), "h", axis=0).astype(BF16)
    terms = jnp.einsum("htf,hfn->tn", normed_all, wo_cols, preferred_element_type=F32)
    mine = lax.dynamic_slice_in_dim(terms, c * half, half, axis=0)
    other = lax.dynamic_slice_in_dim(terms, (1 - c) * half, half, axis=0)
    return (mine + swap(other)).astype(BF16)


def solution(mesh):
    seq, head = mesh.devices.shape
    fine = Mesh(mesh.devices.reshape(seq // 2, 2, head), ("z", "c", "h"))
    tokens = ("z", "c")
    in_specs = (P(tokens, None), P(None, tokens, "h"), P(), P(tokens, "h"), P("h", tokens))
    return jax.shard_map(
        per_device, mesh=fine, in_specs=in_specs, out_specs=P(tokens, "h"), check_vma=False
    )
```

```python
import jax
import jax.numpy as jnp
from jax import lax
from jax.experimental import pallas as pl
from jax.experimental.pallas import tpu as pltpu
from jax.sharding import Mesh
from jax.sharding import PartitionSpec as P

F32 = jnp.float32
BF16 = jnp.bfloat16
F16 = jnp.float16
HD = 128
TOK = 512
W_SCALE = 2.0**19
N_SCALE = 2.0**12
NN = (((1,), (0,)), ((), ()))


def split(a):
    hi = a.astype(BF16)
    return hi, (a - hi.astype(F32)).astype(BF16)


def dot(a, b):
    return lax.dot_general(a, b, NN, preferred_element_type=F32)


def mm3s(a, b):
    (ah, al), (bh, bl) = a, b
    return dot(
        jnp.concatenate([ah, ah, al], axis=1), jnp.concatenate([bh, bl, bh], axis=0)
    )


def mm3(a, b):
    return mm3s(split(a), split(b))


def unit_rows(m):
    return m * lax.rsqrt(jnp.sum(m * m, axis=-1, keepdims=True) + 1e-06)


def count_le(ds_ref, pos):
    total = jnp.zeros(jnp.shape(pos), jnp.int32)
    for j in range(ds_ref.shape[0]):
        total = total + (ds_ref[j] <= pos).astype(jnp.int32)
    return total


def doc_info(meta_ref, ds_ref):
    pos0 = meta_ref[0] * TOK
    doc_col = count_le(ds_ref, pos0 + lax.broadcasted_iota(jnp.int32, (TOK, 1), 0))
    doc_row = count_le(ds_ref, pos0 + lax.broadcasted_iota(jnp.int32, (1, TOK), 1))
    return doc_col, doc_row, count_le(ds_ref, pos0 - 1), count_le(ds_ref, pos0 + TOK - 1)


def in_order(first, own, sib):
    return jnp.concatenate([jnp.where(first, own, sib), jnp.where(first, sib, own)], axis=0)


def part(pair, rows, cols):
    return pair[0][rows, cols], pair[1][rows, cols]


EVERY = slice(None)


def masked_gram(left, right_t, doc_col, doc_row, rows, cols, inclusive=False, scale=None):
    gram = mm3s(part(left, rows, EVERY), part(right_t, EVERY, cols))
    r = lax.broadcasted_iota(jnp.int32, gram.shape, 0) + rows.start
    c = lax.broadcasted_iota(jnp.int32, gram.shape, 1) + cols.start
    keep = (c <= r) if inclusive else (c < r)
    keep = keep & (doc_col[rows] == doc_row[:, cols])
    if scale is not None:
        gram = scale[rows] * gram
    return jnp.where(keep, gram, 0.0)


def pack_kernel(meta_ref, w_ref, wo_ref, codes_ref, give_ref, mine_ref):
    first = meta_ref[1] == 0

    def halves(x):
        left, right = x[:, :HD], x[:, HD:]
        return jnp.where(first, left, right), jnp.where(first, right, left)

    for p in range(3):
        mine, other = halves(w_ref[p].astype(F32))
        mine_ref[:, HD * p : HD * p + HD] = mine.astype(BF16)
        give_ref[:, HD * p : HD * p + HD] = other.astype(BF16)
    top, bottom = wo_ref[:HD].astype(F32), wo_ref[HD:].astype(F32)
    mine_ref[:, 3 * HD :] = jnp.where(first, top, bottom).astype(BF16)
    give_ref[:, 3 * HD : 4 * HD] = jnp.where(first, bottom, top).astype(BF16)
    codes = codes_ref[...].astype(F32)
    other = jnp.where(first, codes[:, 1:2], codes[:, 0:1])
    lane = lax.broadcasted_iota(jnp.int32, (HD, HD), 1)
    give_ref[:, 4 * HD :] = jnp.where(lane == 0, other[:HD], other[HD:]).astype(BF16)


def local_kernel(meta_ref, ds_ref, own_ref, sib_ref, codes_ref, got_ref, tl_ref, wu_ref, kt_ref):
    first = meta_ref[1] == 0
    half = TOK // 2
    kv = in_order(first, own_ref[...].astype(F32), sib_ref[...].astype(F32))
    key = unit_rows(kv[:, :HD])
    value = kv[:, HD:]
    codes = codes_ref[...].astype(F32)
    own_codes = jnp.where(first, codes[:, 0:1], codes[:, 1:2])
    got = got_ref[:, 4 * HD :].astype(F32)
    sib_codes = jnp.concatenate([got[:, 0:1], got[:, 1:2]], axis=0)
    beta = 1.6 + 0.1 * in_order(first, own_codes, sib_codes)
    doc_col, doc_row, prev_doc, last_doc = doc_info(meta_ref, ds_ref)
    carry_in = (doc_col == prev_doc).astype(F32)
    tail_row = (doc_row == last_doc).astype(F32)
    last_keep = (last_doc == prev_doc).astype(F32)

    key_s = split(key)
    key_t = jnp.transpose(key)
    kt_ref[...] = key_t
    key_ts = split(key_t)

    def system(rows, cols):
        return masked_gram(key_s, key_ts, doc_col, doc_row, rows, cols, scale=beta)

    quarter = [slice(128 * i, 128 * i + 128) for i in range(4)]
    rows128 = lax.broadcasted_iota(jnp.int32, (128, 128), 0)
    cols128 = lax.broadcasted_iota(jnp.int32, (128, 128), 1)
    eye128 = (rows128 == cols128).astype(F32)
    diag = [system(s, s) for s in quarter]
    inv = []
    for a in diag:
        m = ((rows128 >> 1) == (cols128 >> 1)) & (rows128 != cols128)
        inv.append(eye128 - jnp.where(m, a, 0.0))
    for lev in range(1, 7):
        m = ((rows128 >> (lev + 1)) == (cols128 >> (lev + 1))) & (
            (rows128 >> lev) != (cols128 >> lev)
        )
        xs = [split(x) for x in inv]
        ys = [mm3s(x, split(jnp.where(m, a, 0.0))) for x, a in zip(xs, diag)]
        inv = [x - mm3s(split(y), s) for x, y, s in zip(inv, ys, xs)]
    pair_inv = []
    for i in (0, 2):
        off = system(quarter[i + 1], quarter[i])
        low = -mm3(mm3(inv[i + 1], off), inv[i])
        top = jnp.concatenate([inv[i], jnp.zeros((128, 128), F32)], axis=1)
        bottom = jnp.concatenate([low, inv[i + 1]], axis=1)
        pair_inv.append(jnp.concatenate([top, bottom], axis=0))
    lo, hi = slice(0, half), slice(half, TOK)
    right = beta * jnp.concatenate([carry_in * key, value], axis=1)
    cross = system(hi, lo)
    wu_lo = mm3(pair_inv[0], right[lo])
    wu_lo_s = split(wu_lo)
    wu_hi = mm3(pair_inv[1], right[hi] - mm3s(split(cross), wu_lo_s))
    wu_hi_s = split(wu_hi)
    wu_ref[lo, :] = wu_lo
    wu_ref[hi, :] = wu_hi
    wu_s = tuple(jnp.concatenate([x, y], axis=0) for x, y in zip(wu_lo_s, wu_hi_s))
    tl = mm3s(split(tail_row * key_t), wu_s)
    tl_ref[0:HD, :] = (last_keep * eye128 - tl[:, :HD]).astype(BF16)
    tl_ref[HD:, :] = tl[:, HD:].astype(BF16)


def query_kernel(meta_ref, ds_ref, own_ref, sib_ref, kt_ref, wu_ref, b_ref):
    first = meta_ref[1] == 0
    half = TOK // 2
    query = unit_rows(in_order(first, own_ref[...].astype(F32), sib_ref[...].astype(F32)))
    doc_col, doc_row, prev_doc, _ = doc_info(meta_ref, ds_ref)
    carry_in = (doc_col == prev_doc).astype(F32)
    query_s = split(query)
    key_ts = split(kt_ref[...])
    wu_s = split(wu_ref[...])
    lo, hi = slice(0, half), slice(half, TOK)

    def probs(rows, cols):
        return masked_gram(query_s, key_ts, doc_col, doc_row, rows, cols, inclusive=True)

    out_lo = mm3s(split(probs(lo, lo)), part(wu_s, lo, EVERY))
    out_hi = mm3s(split(probs(hi, slice(0, TOK))), wu_s)
    b_ref[0, lo, :] = carry_in[lo] * query[lo] - out_lo[:, :HD]
    b_ref[0, hi, :] = carry_in[hi] * query[hi] - out_hi[:, :HD]
    b_ref[1, lo, :] = out_lo[:, HD:]
    b_ref[1, hi, :] = out_hi[:, HD:]


def apply_block(block, state):
    hi, lo = split(state)
    left = block[:HD]
    return dot(jnp.concatenate([left, left], axis=1), jnp.concatenate([hi, lo], axis=0))


def group_kernel(meta_ref, tl_ref, comp_ref, pre_ref):
    place = meta_ref[0] & 3
    eye = (
        lax.broadcasted_iota(jnp.int32, (HD, HD), 0)
        == lax.broadcasted_iota(jnp.int32, (HD, HD), 1)
    ).astype(F32)
    zero = jnp.zeros((HD, HD), F32)
    comp = jnp.concatenate([eye, zero], axis=1)
    pre = comp
    for j in range(4):
        pre = jnp.where(place == j, comp, pre)
        add = jnp.concatenate([zero, tl_ref[j, HD:].astype(F32)], axis=1)
        comp = apply_block(tl_ref[j], comp) + add
    pre_ref[...] = pre
    comp_b = jnp.concatenate([comp[:, :HD], comp[:, HD:]], axis=0).astype(BF16)
    for j in range(4):
        comp_ref[j] = comp_b


def finish_kernel(meta_ref, comp_ref, pre_ref, b_ref, out_ref):
    group = meta_ref[0] >> 2
    first = meta_ref[1] == 0
    half = TOK // 2
    state = jnp.zeros((HD, HD), F32)
    for j in range(3):
        new = apply_block(comp_ref[j], state) + comp_ref[j, HD:].astype(F32)
        state = jnp.where(j < group, new, state)
    state = mm3(pre_ref[:, :HD], state) + pre_ref[:, HD:]
    out = mm3(b_ref[0], state) + b_ref[1]
    out = out * lax.rsqrt(jnp.mean(out * out, axis=-1, keepdims=True) + 1e-05)
    low, high = out[:half], out[half:]
    out_ref[:half, :] = jnp.where(first, high, low).astype(BF16)
    out_ref[half:, :] = jnp.where(first, low, high).astype(BF16)


SMEM = pl.BlockSpec(memory_space=pltpu.SMEM)
VMEM = pl.BlockSpec(memory_space=pltpu.VMEM)


def call(kernel, scalars, arrays, outs, flops):
    return pl.pallas_call(
        kernel,
        out_shape=tuple(jax.ShapeDtypeStruct(s, d) for s, d in outs),
        in_specs=[SMEM] * len(scalars) + [VMEM] * len(arrays),
        out_specs=(VMEM,) * len(outs),
        compiler_params=pltpu.CompilerParams(vmem_limit_bytes=40 << 20),
        cost_estimate=pl.CostEstimate(flops=flops, bytes_accessed=1 << 20, transcendentals=0),
    )(*scalars, *arrays)


def swap(value):
    return lax.ppermute(value, "c", [(0, 1), (1, 0)])


def exchange(blocks, groups):
    return lax.all_to_all(blocks, "z", 0, 0, axis_index_groups=groups)


def per_device(hidden_in, w_qkv, doc_starts, beta_codes, w_out):
    z = lax.axis_index("z")
    c = lax.axis_index("c")
    first = c == 0
    chips = lax.axis_size("z")
    half, width = hidden_in.shape
    meta = jnp.stack([z, c]).astype(jnp.int32)
    near = [[4 * i + j for j in range(4)] for i in range(chips // 4)]
    far = [[4 * i + j for i in range(4)] for j in range(chips // 4)]

    give, mine = call(
        pack_kernel,
        (meta,),
        (w_qkv, w_out, beta_codes),
        [((HD, 5 * HD), BF16), ((HD, 4 * HD), BF16)],
        1 << 20,
    )
    got = swap(give)
    hidden_sib = swap(hidden_in)

    def ordered(a, b, axis=0):
        return jnp.concatenate([jnp.where(first, a, b), jnp.where(first, b, a)], axis=axis)

    w_chip = ordered(mine[:, : 3 * HD], got[:, : 3 * HD])
    w_f16 = (w_chip.astype(F32) * W_SCALE).astype(F16)
    w_all = lax.all_gather(w_f16, "z", axis=0, tiled=True)
    w_all = (w_all.astype(F32) * (1.0 / W_SCALE)).astype(BF16)

    wo_chip = ordered(mine[:, 3 * HD :], got[:, 3 * HD : 4 * HD], axis=1)
    wo_rows = lax.all_gather(wo_chip, "z", axis=0)
    wo_cols = lax.all_to_all(wo_rows, "h", 0, 0)

    def project(hid, cols):
        return jnp.dot(hid, w_all[:, cols], preferred_element_type=F32).astype(BF16)

    q_cols, kv_cols = slice(0, HD), slice(HD, 3 * HD)
    tl, wu, key_t = call(
        local_kernel,
        (meta, doc_starts),
        (project(hidden_in, kv_cols), project(hidden_sib, kv_cols), beta_codes, got),
        [((2 * HD, HD), BF16), ((TOK, 2 * HD), F32), ((HD, TOK), F32)],
        3 << 30,
    )
    near_all = exchange(jnp.broadcast_to(tl[None], (4, 2 * HD, HD)), near)
    comp, pre = call(
        group_kernel,
        (meta,),
        (near_all,),
        [((4, 2 * HD, HD), BF16), ((HD, 2 * HD), F32)],
        1 << 28,
    )
    far_all = exchange(comp, far)
    (b,) = call(
        query_kernel,
        (meta, doc_starts),
        (project(hidden_in, q_cols), project(hidden_sib, q_cols), key_t, wu),
        [((2, TOK, HD), F32)],
        3 << 30,
    )
    (normed,) = call(
        finish_kernel,
        (meta,),
        (far_all, pre, b),
        [((TOK, HD), BF16)],
        1 << 28,
    )
    normed = (normed.astype(F32) * N_SCALE).astype(F16)
    normed_all = lax.all_gather(normed, "h", axis=0)
    normed_all = (normed_all.astype(F32) * (1.0 / N_SCALE)).astype(BF16)

    def output(rows):
        return jnp.einsum("htf,hfn->tn", rows, wo_cols, preferred_element_type=F32)

    sent = swap(output(normed_all[:, :half]))
    return (output(normed_all[:, half:]) + sent).astype(BF16)


def solution(mesh):
    seq, head = mesh.devices.shape
    fine = Mesh(mesh.devices.reshape(seq // 2, 2, head), ("z", "c", "h"))
    tokens = ("z", "c")
    in_specs = (P(tokens, None), P(None, tokens, "h"), P(), P(tokens, "h"), P("h", tokens))
    return jax.shard_map(
        per_device, mesh=fine, in_specs=in_specs, out_specs=P(tokens, "h"), check_vma=False
    )
```

```python
import jax
import jax.numpy as jnp
from jax import lax
from jax.experimental import pallas as pl
from jax.experimental.pallas import tpu as pltpu
from jax.sharding import Mesh
from jax.sharding import PartitionSpec as P

F32 = jnp.float32
BF16 = jnp.bfloat16
F16 = jnp.float16
HD = 128
TOK = 512
W_SCALE = 2.0**19
NN = (((1,), (0,)), ((), ()))


def split(a):
    hi = a.astype(BF16)
    return hi, (a - hi.astype(F32)).astype(BF16)


def dot(a, b):
    return lax.dot_general(a, b, NN, preferred_element_type=F32)


def mm3s(a, b):
    (ah, al), (bh, bl) = a, b
    return dot(
        jnp.concatenate([ah, ah, al], axis=1), jnp.concatenate([bh, bl, bh], axis=0)
    )


def mm3(a, b):
    return mm3s(split(a), split(b))


def unit_rows(m):
    return m * lax.rsqrt(jnp.sum(m * m, axis=-1, keepdims=True) + 1e-06)


def count_le(ds_ref, pos):
    total = jnp.zeros(jnp.shape(pos), jnp.int32)
    for j in range(ds_ref.shape[0]):
        total = total + (ds_ref[j] <= pos).astype(jnp.int32)
    return total


def doc_info(meta_ref, ds_ref):
    pos0 = meta_ref[0] * TOK
    doc_col = count_le(ds_ref, pos0 + lax.broadcasted_iota(jnp.int32, (TOK, 1), 0))
    doc_row = count_le(ds_ref, pos0 + lax.broadcasted_iota(jnp.int32, (1, TOK), 1))
    return doc_col, doc_row, count_le(ds_ref, pos0 - 1), count_le(ds_ref, pos0 + TOK - 1)


def in_order(first, own, sib):
    return jnp.concatenate([jnp.where(first, own, sib), jnp.where(first, sib, own)], axis=0)


def part(pair, rows, cols):
    return pair[0][rows, cols], pair[1][rows, cols]


EVERY = slice(None)


def masked_gram(left, right_t, doc_col, doc_row, rows, cols, inclusive=False, scale=None):
    gram = mm3s(part(left, rows, EVERY), part(right_t, EVERY, cols))
    r = lax.broadcasted_iota(jnp.int32, gram.shape, 0) + rows.start
    c = lax.broadcasted_iota(jnp.int32, gram.shape, 1) + cols.start
    keep = (c <= r) if inclusive else (c < r)
    keep = keep & (doc_col[rows] == doc_row[:, cols])
    if scale is not None:
        gram = scale[rows] * gram
    return jnp.where(keep, gram, 0.0)


def pack_kernel(meta_ref, w_ref, codes_ref, give_ref, mine_ref):
    first = meta_ref[1] == 0
    for place, p in enumerate((1, 2, 0)):
        left = w_ref[p, :, :HD].astype(F32)
        right = w_ref[p, :, HD:].astype(F32)
        cols = slice(HD * place, HD * place + HD)
        mine_ref[:, cols] = jnp.where(first, left, right).astype(BF16)
        give_ref[:, cols] = jnp.where(first, right, left).astype(BF16)
    codes = codes_ref[...].astype(F32)
    other = jnp.where(first, codes[1:2], codes[0:1])
    row = lax.broadcasted_iota(jnp.int32, (HD, HD), 0)
    give_ref[:, 3 * HD :] = jnp.where(row == 0, other[:, :HD], other[:, HD:]).astype(BF16)


def local_kernel(meta_ref, ds_ref, own_ref, sib_ref, codes_ref, got_ref, tl_ref, wu_ref, kt_ref):
    first = meta_ref[1] == 0
    half = TOK // 2
    kv = in_order(first, own_ref[...].astype(F32), sib_ref[...].astype(F32))
    key = unit_rows(kv[:, :HD])
    value = kv[:, HD:]
    codes = codes_ref[...].astype(F32)
    own_codes = jnp.where(first, codes[0:1], codes[1:2])
    got = got_ref[0:8, 3 * HD :].astype(F32)
    sib_codes = jnp.concatenate([got[0:1], got[1:2]], axis=1)
    codes = jnp.concatenate(
        [jnp.where(first, own_codes, sib_codes), jnp.where(first, sib_codes, own_codes)], axis=1
    )
    beta = 1.6 + 0.1 * jnp.transpose(jnp.broadcast_to(codes, (8, TOK)))[:, 0:1]
    doc_col, doc_row, prev_doc, last_doc = doc_info(meta_ref, ds_ref)
    carry_in = (doc_col == prev_doc).astype(F32)
    tail_row = (doc_row == last_doc).astype(F32)
    last_keep = (last_doc == prev_doc).astype(F32)

    key_s = split(key)
    key_t = jnp.transpose(key)
    kt_ref[...] = key_t
    key_ts = split(key_t)

    def system(rows, cols):
        return masked_gram(key_s, key_ts, doc_col, doc_row, rows, cols, scale=beta)

    quarter = [slice(128 * i, 128 * i + 128) for i in range(4)]
    rows128 = lax.broadcasted_iota(jnp.int32, (128, 128), 0)
    cols128 = lax.broadcasted_iota(jnp.int32, (128, 128), 1)
    eye128 = (rows128 == cols128).astype(F32)
    diag = [system(s, s) for s in quarter]
    inv = []
    for a in diag:
        m = ((rows128 >> 1) == (cols128 >> 1)) & (rows128 != cols128)
        inv.append(eye128 - jnp.where(m, a, 0.0))
    for lev in range(1, 7):
        m = ((rows128 >> (lev + 1)) == (cols128 >> (lev + 1))) & (
            (rows128 >> lev) != (cols128 >> lev)
        )
        xs = [split(x) for x in inv]
        ys = [mm3s(x, split(jnp.where(m, a, 0.0))) for x, a in zip(xs, diag)]
        inv = [x - mm3s(split(y), s) for x, y, s in zip(inv, ys, xs)]
    pair_inv = []
    for i in (0, 2):
        off = system(quarter[i + 1], quarter[i])
        low = -mm3(mm3(inv[i + 1], off), inv[i])
        top = jnp.concatenate([inv[i], jnp.zeros((128, 128), F32)], axis=1)
        bottom = jnp.concatenate([low, inv[i + 1]], axis=1)
        pair_inv.append(jnp.concatenate([top, bottom], axis=0))
    lo, hi = slice(0, half), slice(half, TOK)
    right = beta * jnp.concatenate([carry_in * key, value], axis=1)
    cross = system(hi, lo)
    wu_lo = mm3(pair_inv[0], right[lo])
    wu_lo_s = split(wu_lo)
    wu_hi = mm3(pair_inv[1], right[hi] - mm3s(split(cross), wu_lo_s))
    wu_hi_s = split(wu_hi)
    wu_ref[lo, :] = wu_lo
    wu_ref[hi, :] = wu_hi
    wu_s = tuple(jnp.concatenate([x, y], axis=0) for x, y in zip(wu_lo_s, wu_hi_s))
    tl = mm3s(split(tail_row * key_t), wu_s)
    tl_ref[0:HD, :] = (last_keep * eye128 - tl[:, :HD]).astype(BF16)
    tl_ref[HD:, :] = tl[:, HD:].astype(BF16)


def query_kernel(meta_ref, ds_ref, own_ref, sib_ref, kt_ref, wu_ref, b_ref):
    first = meta_ref[1] == 0
    half = TOK // 2
    query = unit_rows(in_order(first, own_ref[...].astype(F32), sib_ref[...].astype(F32)))
    doc_col, doc_row, prev_doc, _ = doc_info(meta_ref, ds_ref)
    carry_in = (doc_col == prev_doc).astype(F32)
    query_s = split(query)
    key_ts = split(kt_ref[...])
    wu_s = split(wu_ref[...])
    lo, hi = slice(0, half), slice(half, TOK)

    def probs(rows, cols):
        return masked_gram(query_s, key_ts, doc_col, doc_row, rows, cols, inclusive=True)

    out_lo = mm3s(split(probs(lo, lo)), part(wu_s, lo, EVERY))
    out_hi = mm3s(split(probs(hi, slice(0, TOK))), wu_s)
    b_ref[0, lo, :] = carry_in[lo] * query[lo] - out_lo[:, :HD]
    b_ref[0, hi, :] = carry_in[hi] * query[hi] - out_hi[:, :HD]
    b_ref[1, lo, :] = out_lo[:, HD:]
    b_ref[1, hi, :] = out_hi[:, HD:]


def apply_block(block, state):
    hi, lo = split(state)
    left = block[:HD]
    return dot(jnp.concatenate([left, left], axis=1), jnp.concatenate([hi, lo], axis=0))


def group_kernel(meta_ref, tl_ref, comp_ref, pre_ref):
    place = meta_ref[0] & 3
    eye = (
        lax.broadcasted_iota(jnp.int32, (HD, HD), 0)
        == lax.broadcasted_iota(jnp.int32, (HD, HD), 1)
    ).astype(F32)
    zero = jnp.zeros((HD, HD), F32)
    comp = jnp.concatenate([eye, zero], axis=1)
    pre = comp
    for j in range(4):
        pre = jnp.where(place == j, comp, pre)
        add = jnp.concatenate([zero, tl_ref[j, HD:].astype(F32)], axis=1)
        comp = apply_block(tl_ref[j], comp) + add
    pre_ref[...] = pre
    comp_b = jnp.concatenate([comp[:, :HD], comp[:, HD:]], axis=0).astype(BF16)
    for j in range(4):
        comp_ref[j] = comp_b


def finish_kernel(meta_ref, comp_ref, pre_ref, b_ref, out_ref):
    group = meta_ref[0] >> 2
    first = meta_ref[1] == 0
    half = TOK // 2
    state = jnp.zeros((HD, HD), F32)
    for j in range(3):
        new = apply_block(comp_ref[j], state) + comp_ref[j, HD:].astype(F32)
        state = jnp.where(j < group, new, state)
    state = mm3(pre_ref[:, :HD], state) + pre_ref[:, HD:]
    out = mm3(b_ref[0], state) + b_ref[1]
    out = out * lax.rsqrt(jnp.mean(out * out, axis=-1, keepdims=True) + 1e-05)
    low, high = out[:half], out[half:]
    out_ref[:half, :] = jnp.where(first, high, low).astype(BF16)
    out_ref[half:, :] = jnp.where(first, low, high).astype(BF16)


def terms_kernel(meta_ref, own_ref, got_ref, own_w_ref, sib_w_ref, out_ref):
    first = meta_ref[1] == 0
    own = own_ref[TOK // 2 :].astype(F32)
    got = got_ref[...].astype(F32)
    rows = jnp.concatenate(
        [jnp.where(first, own, got), jnp.where(first, got, own)], axis=1
    ).astype(BF16)
    for j in range(own_w_ref.shape[0]):
        mine = dot(rows, own_w_ref[j])
        other = dot(rows, sib_w_ref[j])
        out_ref[j, :, :HD] = jnp.where(first, mine, other).astype(BF16)
        out_ref[j, :, HD:] = jnp.where(first, other, mine).astype(BF16)


SMEM = pl.BlockSpec(memory_space=pltpu.SMEM)
VMEM = pl.BlockSpec(memory_space=pltpu.VMEM)


def call(kernel, scalars, arrays, outs, flops):
    return pl.pallas_call(
        kernel,
        out_shape=tuple(jax.ShapeDtypeStruct(s, d) for s, d in outs),
        in_specs=[SMEM] * len(scalars) + [VMEM] * len(arrays),
        out_specs=(VMEM,) * len(outs),
        compiler_params=pltpu.CompilerParams(vmem_limit_bytes=16 << 20),
        cost_estimate=pl.CostEstimate(flops=flops, bytes_accessed=1 << 20, transcendentals=0),
    )(*scalars, *arrays)


def swap(value):
    return lax.ppermute(value, "c", [(0, 1), (1, 0)])


def exchange(blocks, groups):
    return lax.all_to_all(blocks, "z", 0, 0, axis_index_groups=groups)


def per_device(hidden_in, w_qkv, doc_starts, beta_codes, w_out):
    z = lax.axis_index("z")
    c = lax.axis_index("c")
    first = c == 0
    chips = lax.axis_size("z")
    half, width = hidden_in.shape
    meta = jnp.stack([z, c]).astype(jnp.int32)
    near = [[4 * i + j for j in range(4)] for i in range(chips // 4)]
    far = [[4 * i + j for i in range(4)] for j in range(chips // 4)]

    codes = beta_codes.T
    give, mine = call(
        pack_kernel,
        (meta,),
        (w_qkv, codes),
        [((HD, 4 * HD), BF16), ((HD, 3 * HD), BF16)],
        1 << 20,
    )
    got = swap(give)
    hidden_sib = swap(hidden_in)

    def chip(cols):
        a, b = mine[:, cols], got[:, cols]
        return jnp.concatenate([jnp.where(first, a, b), jnp.where(first, b, a)], axis=0)

    kv_f16 = (chip(slice(0, 2 * HD)).astype(F32) * W_SCALE).astype(F16)
    qo = jnp.concatenate([chip(slice(2 * HD, 3 * HD)), w_out], axis=1)
    kv_f16, qo = lax.optimization_barrier((kv_f16, qo))
    qo_all = lax.all_gather(qo, "z", axis=0, tiled=True)
    kv_all = lax.all_gather(kv_f16, "z", axis=0, tiled=True)
    kv_all = (kv_all.astype(F32) * (1.0 / W_SCALE)).astype(BF16)

    def project(hid, weights):
        return jnp.dot(hid, weights, preferred_element_type=F32).astype(BF16)

    tl, wu, key_t = call(
        local_kernel,
        (meta, doc_starts),
        (project(hidden_in, kv_all), project(hidden_sib, kv_all), codes, got),
        [((2 * HD, HD), BF16), ((TOK, 2 * HD), F32), ((HD, TOK), F32)],
        3 << 30,
    )
    near_all = exchange(jnp.broadcast_to(tl[None], (4, 2 * HD, HD)), near)
    comp, pre = call(
        group_kernel,
        (meta,),
        (near_all,),
        [((4, 2 * HD, HD), BF16), ((HD, 2 * HD), F32)],
        1 << 28,
    )
    far_all = exchange(comp, far)
    qo_all, _ = lax.optimization_barrier((qo_all, comp))
    q_all = qo_all[:, :HD]
    wo_own = qo_all[:, HD:].reshape(chips, 2 * HD, HD)
    wo_sib = swap(wo_own)
    (b,) = call(
        query_kernel,
        (meta, doc_starts),
        (project(hidden_in, q_all), project(hidden_sib, q_all), key_t, wu),
        [((2, TOK, HD), F32)],
        3 << 30,
    )
    (normed,) = call(
        finish_kernel,
        (meta,),
        (far_all, pre, b),
        [((TOK, HD), BF16)],
        1 << 28,
    )
    (terms,) = call(
        terms_kernel,
        (meta,),
        (normed, swap(normed[:half]), wo_own, wo_sib),
        [((chips, half, 2 * HD), BF16)],
        1 << 29,
    )
    shares = lax.all_to_all(terms, "h", 0, 0)
    return jnp.sum(shares.astype(F32), axis=0).astype(BF16)


def solution(mesh):
    seq, head = mesh.devices.shape
    fine = Mesh(mesh.devices.reshape(seq // 2, 2, head), ("z", "c", "h"))
    tokens = ("z", "c")
    in_specs = (P(tokens, None), P(None, tokens, "h"), P(), P(tokens, "h"), P("h", tokens))
    return jax.shard_map(
        per_device, mesh=fine, in_specs=in_specs, out_specs=P(tokens, "h"), check_vma=False
    )
```

```python
import jax
import jax.numpy as jnp
from jax import lax
from jax.experimental import pallas as pl
from jax.experimental.pallas import tpu as pltpu
from jax.sharding import Mesh
from jax.sharding import PartitionSpec as P

F32 = jnp.float32
BF16 = jnp.bfloat16
F16 = jnp.float16
HD = 128
TOK = 512
W_SCALE = 2.0**19
WO_SCALE = 2.0**18
L_SCALE = 2.0**-6
N_SCALE = 2.0**12
NN = (((1,), (0,)), ((), ()))


def split(a):
    hi = a.astype(BF16)
    return hi, (a - hi.astype(F32)).astype(BF16)


def dot(a, b):
    return lax.dot_general(a, b, NN, preferred_element_type=F32)


def mm3s(a, b):
    (ah, al), (bh, bl) = a, b
    return dot(
        jnp.concatenate([ah, ah, al], axis=1), jnp.concatenate([bh, bl, bh], axis=0)
    )


def mm3(a, b):
    return mm3s(split(a), split(b))


def unit_rows(m):
    return m * lax.rsqrt(jnp.sum(m * m, axis=-1, keepdims=True) + 1e-06)


def count_le(ds_ref, pos):
    total = jnp.zeros(jnp.shape(pos), jnp.int32)
    for j in range(ds_ref.shape[0]):
        total = total + (ds_ref[j] <= pos).astype(jnp.int32)
    return total


def doc_info(meta_ref, ds_ref):
    pos0 = meta_ref[0] * TOK
    doc_col = count_le(ds_ref, pos0 + lax.broadcasted_iota(jnp.int32, (TOK, 1), 0))
    doc_row = count_le(ds_ref, pos0 + lax.broadcasted_iota(jnp.int32, (1, TOK), 1))
    return doc_col, doc_row, count_le(ds_ref, pos0 - 1), count_le(ds_ref, pos0 + TOK - 1)


def in_order(first, own, sib):
    return jnp.concatenate([jnp.where(first, own, sib), jnp.where(first, sib, own)], axis=0)


def part(pair, rows, cols):
    return pair[0][rows, cols], pair[1][rows, cols]


EVERY = slice(None)


def masked_gram(left, right_t, doc_col, doc_row, rows, cols, inclusive=False, scale=None):
    gram = mm3s(part(left, rows, EVERY), part(right_t, EVERY, cols))
    r = lax.broadcasted_iota(jnp.int32, gram.shape, 0) + rows.start
    c = lax.broadcasted_iota(jnp.int32, gram.shape, 1) + cols.start
    keep = (c <= r) if inclusive else (c < r)
    keep = keep & (doc_col[rows] == doc_row[:, cols])
    if scale is not None:
        gram = scale[rows] * gram
    return jnp.where(keep, gram, 0.0)


def pack_kernel(meta_ref, w_ref, wo_ref, codes_ref, give_ref, mine_ref):
    first = meta_ref[1] == 0

    def put(place, mine, other):
        cols = slice(HD * place, HD * place + HD)
        mine_ref[:, cols] = jnp.where(first, mine, other).astype(BF16)
        give_ref[:, cols] = jnp.where(first, other, mine).astype(BF16)

    for p in range(3):
        put(p, w_ref[p, :, :HD].astype(F32), w_ref[p, :, HD:].astype(F32))
    put(3, wo_ref[:HD].astype(F32), wo_ref[HD:].astype(F32))
    codes = codes_ref[...].astype(F32)
    other = jnp.where(first, codes[1:2], codes[0:1])
    row = lax.broadcasted_iota(jnp.int32, (HD, HD), 0)
    give_ref[:, 4 * HD :] = jnp.where(row == 0, other[:, :HD], other[:, HD:]).astype(BF16)


def local_kernel(meta_ref, ds_ref, own_ref, sib_ref, codes_ref, got_ref, tl_ref, b_ref):
    first = meta_ref[1] == 0
    half = TOK // 2
    qkv = in_order(first, own_ref[...].astype(F32), sib_ref[...].astype(F32))
    query = unit_rows(qkv[:, :HD])
    key = unit_rows(qkv[:, HD : 2 * HD])
    value = qkv[:, 2 * HD :]
    codes = codes_ref[...].astype(F32)
    own_codes = jnp.where(first, codes[0:1], codes[1:2])
    got = got_ref[0:8, 4 * HD :].astype(F32)
    sib_codes = jnp.concatenate([got[0:1], got[1:2]], axis=1)
    codes = jnp.concatenate(
        [jnp.where(first, own_codes, sib_codes), jnp.where(first, sib_codes, own_codes)], axis=1
    )
    beta = 1.6 + 0.1 * jnp.transpose(jnp.broadcast_to(codes, (8, TOK)))[:, 0:1]
    doc_col, doc_row, prev_doc, last_doc = doc_info(meta_ref, ds_ref)
    carry_in = (doc_col == prev_doc).astype(F32)
    tail_row = (doc_row == last_doc).astype(F32)
    last_keep = (last_doc == prev_doc).astype(F32)

    key_s = split(key)
    key_t = jnp.transpose(key)
    key_ts = split(key_t)

    def system(rows, cols):
        return masked_gram(key_s, key_ts, doc_col, doc_row, rows, cols, scale=beta)

    quarter = [slice(128 * i, 128 * i + 128) for i in range(4)]
    rows128 = lax.broadcasted_iota(jnp.int32, (128, 128), 0)
    cols128 = lax.broadcasted_iota(jnp.int32, (128, 128), 1)
    eye128 = (rows128 == cols128).astype(F32)
    diag = [system(s, s) for s in quarter]
    inv = []
    for a in diag:
        m = ((rows128 >> 1) == (cols128 >> 1)) & (rows128 != cols128)
        inv.append(eye128 - jnp.where(m, a, 0.0))
    for lev in range(1, 7):
        m = ((rows128 >> (lev + 1)) == (cols128 >> (lev + 1))) & (
            (rows128 >> lev) != (cols128 >> lev)
        )
        xs = [split(x) for x in inv]
        ys = [mm3s(x, split(jnp.where(m, a, 0.0))) for x, a in zip(xs, diag)]
        inv = [x - mm3s(split(y), s) for x, y, s in zip(inv, ys, xs)]
    pair_inv = []
    for i in (0, 2):
        off = system(quarter[i + 1], quarter[i])
        low = -mm3(mm3(inv[i + 1], off), inv[i])
        top = jnp.concatenate([inv[i], jnp.zeros((128, 128), F32)], axis=1)
        bottom = jnp.concatenate([low, inv[i + 1]], axis=1)
        pair_inv.append(jnp.concatenate([top, bottom], axis=0))
    lo, hi = slice(0, half), slice(half, TOK)
    right = beta * jnp.concatenate([carry_in * key, value], axis=1)
    cross = system(hi, lo)
    wu_lo = mm3(pair_inv[0], right[lo])
    wu_lo_s = split(wu_lo)
    wu_hi = mm3(pair_inv[1], right[hi] - mm3s(split(cross), wu_lo_s))
    wu_hi_s = split(wu_hi)
    wu_s = tuple(jnp.concatenate([x, y], axis=0) for x, y in zip(wu_lo_s, wu_hi_s))
    tl = mm3s(split(tail_row * key_t), wu_s)
    tl_ref[:, :HD] = last_keep * eye128 - tl[:, :HD]
    tl_ref[:, HD:] = tl[:, HD:] * L_SCALE

    query_s = split(query)

    def probs(rows, cols):
        return masked_gram(query_s, key_ts, doc_col, doc_row, rows, cols, inclusive=True)

    out_lo = mm3s(split(probs(lo, lo)), part(wu_s, lo, EVERY))
    out_hi = mm3s(split(probs(hi, slice(0, TOK))), wu_s)
    b_ref[0, lo, :] = carry_in[lo] * query[lo] - out_lo[:, :HD]
    b_ref[0, hi, :] = carry_in[hi] * query[hi] - out_hi[:, :HD]
    b_ref[1, lo, :] = out_lo[:, HD:]
    b_ref[1, hi, :] = out_hi[:, HD:]


def finish_kernel(meta_ref, ds_ref, tl_ref, b_ref, out_ref):
    here = meta_ref[0]
    first = meta_ref[1] == 0
    half = TOK // 2
    start = jnp.int32(0)
    for j in range(ds_ref.shape[0]):
        pos = ds_ref[j]
        start = jnp.where(pos < here * TOK, jnp.maximum(start, pos // TOK), start)

    def fold(j, state):
        block = tl_ref[j]
        hi, lo = split(state)
        left = block[:, :HD]
        add = block[:, HD:].astype(F32) * (1.0 / L_SCALE)
        return dot(jnp.concatenate([left, left], axis=1), jnp.concatenate([hi, lo], axis=0)) + add

    state = lax.fori_loop(start, here, fold, jnp.zeros((HD, HD), F32))
    out = mm3(b_ref[0], state) + b_ref[1]
    out = out * lax.rsqrt(jnp.mean(out * out, axis=-1, keepdims=True) + 1e-05)
    low, high = out[:half], out[half:]
    out_ref[:half, :] = jnp.where(first, high, low).astype(BF16)
    out_ref[half:, :] = jnp.where(first, low, high).astype(BF16)


SMEM = pl.BlockSpec(memory_space=pltpu.SMEM)
VMEM = pl.BlockSpec(memory_space=pltpu.VMEM)


def call(kernel, scalars, arrays, outs, flops):
    return pl.pallas_call(
        kernel,
        out_shape=tuple(jax.ShapeDtypeStruct(s, d) for s, d in outs),
        in_specs=[SMEM] * len(scalars) + [VMEM] * len(arrays),
        out_specs=(VMEM,) * len(outs),
        compiler_params=pltpu.CompilerParams(vmem_limit_bytes=16 << 20),
        cost_estimate=pl.CostEstimate(flops=flops, bytes_accessed=1 << 20, transcendentals=0),
    )(*scalars, *arrays)


def swap(value):
    return lax.ppermute(value, "c", [(0, 1), (1, 0)])


def to_f16(value, scale):
    return (value.astype(F32) * scale).astype(F16)


def from_f16(value, scale):
    return (value.astype(F32) * (1.0 / scale)).astype(BF16)


def per_device(hidden_in, w_qkv, doc_starts, beta_codes, w_out):
    z = lax.axis_index("z")
    c = lax.axis_index("c")
    first = c == 0
    chips = lax.axis_size("z")
    heads = lax.axis_size("h")
    half = hidden_in.shape[0]
    meta = jnp.stack([z, c]).astype(jnp.int32)
    codes = beta_codes.T

    give, mine = call(
        pack_kernel,
        (meta,),
        (w_qkv, w_out, codes),
        [((HD, 5 * HD), BF16), ((HD, 4 * HD), BF16)],
        1 << 20,
    )
    got = swap(give)
    hidden_sib = swap(hidden_in)

    def chip(cols, axis):
        a, b = mine[:, cols], got[:, cols]
        return jnp.concatenate([jnp.where(first, a, b), jnp.where(first, b, a)], axis=axis)

    w_all = lax.all_gather(to_f16(chip(slice(0, 3 * HD), 0), W_SCALE), "z", axis=0, tiled=True)
    w_all = from_f16(w_all, W_SCALE)
    turned = [(i * heads + j, j * heads + i) for i in range(chips) for j in range(heads)]
    wo = lax.ppermute(chip(slice(3 * HD, 4 * HD), 1), ("z", "h"), turned)

    def project(hid):
        return jnp.dot(hid, w_all, preferred_element_type=F32).astype(BF16)

    tl, b = call(
        local_kernel,
        (meta, doc_starts),
        (project(hidden_in), project(hidden_sib), codes, got),
        [((HD, 2 * HD), F32), ((2, TOK, HD), F32)],
        3 << 30,
    )
    both = jnp.concatenate([tl.astype(F16), to_f16(wo, WO_SCALE)], axis=0)
    both = lax.all_gather(both, "z", axis=0)
    (normed,) = call(
        finish_kernel,
        (meta, doc_starts),
        (both[:, :HD].astype(BF16), b),
        [((TOK, HD), BF16)],
        1 << 28,
    )
    normed_all = from_f16(lax.all_gather(to_f16(normed, N_SCALE), "h", axis=0), N_SCALE)
    wo_cols = from_f16(both[:, HD:], WO_SCALE)

    def output(rows):
        return jnp.einsum("htf,hfn->tn", rows, wo_cols, preferred_element_type=F32)

    sent = swap(output(normed_all[:, :half]))
    return (output(normed_all[:, half:]) + sent).astype(BF16)


def solution(mesh):
    seq, head = mesh.devices.shape
    fine = Mesh(mesh.devices.reshape(seq // 2, 2, head), ("z", "c", "h"))
    tokens = ("z", "c")
    in_specs = (P(tokens, None), P(None, tokens, "h"), P(), P(tokens, "h"), P("h", tokens))
    return jax.shard_map(
        per_device, mesh=fine, in_specs=in_specs, out_specs=P(tokens, "h"), check_vma=False
    )
```

```python
import jax
import jax.numpy as jnp
from jax import lax
from jax.experimental import pallas as pl
from jax.experimental.pallas import tpu as pltpu
from jax.sharding import Mesh
from jax.sharding import PartitionSpec as P

F32 = jnp.float32
BF16 = jnp.bfloat16
F16 = jnp.float16
HD = 128
TOK = 512
W_SCALE = 2.0**19
WO_SCALE = 2.0**18
N_SCALE = 2.0**12
NN = (((1,), (0,)), ((), ()))


def split(a):
    hi = a.astype(BF16)
    return hi, (a - hi.astype(F32)).astype(BF16)


def dot(a, b):
    return lax.dot_general(a, b, NN, preferred_element_type=F32)


def mm3s(a, b):
    (ah, al), (bh, bl) = a, b
    return dot(
        jnp.concatenate([ah, ah, al], axis=1), jnp.concatenate([bh, bl, bh], axis=0)
    )


def mm3(a, b):
    return mm3s(split(a), split(b))


def unit_rows(m):
    return m * lax.rsqrt(jnp.sum(m * m, axis=-1, keepdims=True) + 1e-06)


def count_le(ds_ref, pos):
    total = jnp.zeros(jnp.shape(pos), jnp.int32)
    for j in range(ds_ref.shape[0]):
        total = total + (ds_ref[j] <= pos).astype(jnp.int32)
    return total


def doc_info(meta_ref, ds_ref):
    pos0 = meta_ref[0] * TOK
    doc_col = count_le(ds_ref, pos0 + lax.broadcasted_iota(jnp.int32, (TOK, 1), 0))
    doc_row = count_le(ds_ref, pos0 + lax.broadcasted_iota(jnp.int32, (1, TOK), 1))
    return doc_col, doc_row, count_le(ds_ref, pos0 - 1), count_le(ds_ref, pos0 + TOK - 1)


def in_order(first, own, sib):
    return jnp.concatenate([jnp.where(first, own, sib), jnp.where(first, sib, own)], axis=0)


def part(pair, rows, cols):
    return pair[0][rows, cols], pair[1][rows, cols]


EVERY = slice(None)


def masked_gram(left, right_t, doc_col, doc_row, rows, cols, inclusive=False, scale=None):
    gram = mm3s(part(left, rows, EVERY), part(right_t, EVERY, cols))
    r = lax.broadcasted_iota(jnp.int32, gram.shape, 0) + rows.start
    c = lax.broadcasted_iota(jnp.int32, gram.shape, 1) + cols.start
    keep = (c <= r) if inclusive else (c < r)
    keep = keep & (doc_col[rows] == doc_row[:, cols])
    if scale is not None:
        gram = scale[rows] * gram
    return jnp.where(keep, gram, 0.0)


def pack_kernel(meta_ref, w_ref, wo_ref, codes_ref, give_ref, mine_ref):
    first = meta_ref[1] == 0

    def put(place, mine, other):
        cols = slice(HD * place, HD * place + HD)
        mine_ref[:, cols] = jnp.where(first, mine, other).astype(BF16)
        give_ref[:, cols] = jnp.where(first, other, mine).astype(BF16)

    for p in range(3):
        put(p, w_ref[p, :, :HD].astype(F32), w_ref[p, :, HD:].astype(F32))
    put(3, wo_ref[:HD].astype(F32), wo_ref[HD:].astype(F32))
    codes = codes_ref[...].astype(F32)
    other = jnp.where(first, codes[1:2], codes[0:1])
    row = lax.broadcasted_iota(jnp.int32, (HD, HD), 0)
    give_ref[:, 4 * HD :] = jnp.where(row == 0, other[:, :HD], other[:, HD:]).astype(BF16)


def local_kernel(
    meta_ref, ds_ref, own_ref, sib_ref, codes_ref, got_ref, tl_ref, tl16_ref, b_ref
):
    first = meta_ref[1] == 0
    half = TOK // 2
    qkv = in_order(first, own_ref[...].astype(F32), sib_ref[...].astype(F32))
    query = unit_rows(qkv[:, :HD])
    key = unit_rows(qkv[:, HD : 2 * HD])
    value = qkv[:, 2 * HD :]
    codes = codes_ref[...].astype(F32)
    own_codes = jnp.where(first, codes[0:1], codes[1:2])
    got = got_ref[0:8, 4 * HD :].astype(F32)
    sib_codes = jnp.concatenate([got[0:1], got[1:2]], axis=1)
    codes = jnp.concatenate(
        [jnp.where(first, own_codes, sib_codes), jnp.where(first, sib_codes, own_codes)], axis=1
    )
    beta = 1.6 + 0.1 * jnp.transpose(jnp.broadcast_to(codes, (8, TOK)))[:, 0:1]
    doc_col, doc_row, prev_doc, last_doc = doc_info(meta_ref, ds_ref)
    carry_in = (doc_col == prev_doc).astype(F32)
    tail_row = (doc_row == last_doc).astype(F32)
    last_keep = (last_doc == prev_doc).astype(F32)

    key_s = split(key)
    key_t = jnp.transpose(key)
    key_ts = split(key_t)

    def system(rows, cols):
        return masked_gram(key_s, key_ts, doc_col, doc_row, rows, cols, scale=beta)

    quarter = [slice(128 * i, 128 * i + 128) for i in range(4)]
    rows128 = lax.broadcasted_iota(jnp.int32, (128, 128), 0)
    cols128 = lax.broadcasted_iota(jnp.int32, (128, 128), 1)
    eye128 = (rows128 == cols128).astype(F32)
    diag = [system(s, s) for s in quarter]
    inv = []
    for a in diag:
        m = ((rows128 >> 1) == (cols128 >> 1)) & (rows128 != cols128)
        inv.append(eye128 - jnp.where(m, a, 0.0))
    for lev in range(1, 7):
        m = ((rows128 >> (lev + 1)) == (cols128 >> (lev + 1))) & (
            (rows128 >> lev) != (cols128 >> lev)
        )
        xs = [split(x) for x in inv]
        ys = [mm3s(x, split(jnp.where(m, a, 0.0))) for x, a in zip(xs, diag)]
        inv = [x - mm3s(split(y), s) for x, y, s in zip(inv, ys, xs)]
    pair_inv = []
    for i in (0, 2):
        off = system(quarter[i + 1], quarter[i])
        low = -mm3(mm3(inv[i + 1], off), inv[i])
        top = jnp.concatenate([inv[i], jnp.zeros((128, 128), F32)], axis=1)
        bottom = jnp.concatenate([low, inv[i + 1]], axis=1)
        pair_inv.append(jnp.concatenate([top, bottom], axis=0))
    lo, hi = slice(0, half), slice(half, TOK)
    right = beta * jnp.concatenate([carry_in * key, value], axis=1)
    cross = system(hi, lo)
    wu_lo = mm3(pair_inv[0], right[lo])
    wu_lo_s = split(wu_lo)
    wu_hi = mm3(pair_inv[1], right[hi] - mm3s(split(cross), wu_lo_s))
    wu_hi_s = split(wu_hi)
    wu_s = tuple(jnp.concatenate([x, y], axis=0) for x, y in zip(wu_lo_s, wu_hi_s))
    tl = mm3s(split(tail_row * key_t), wu_s)
    tl_ref[:, :HD] = last_keep * eye128 - tl[:, :HD]
    tl_ref[:, HD:] = tl[:, HD:]
    tl16_ref[...] = tl_ref[...].astype(BF16)

    query_s = split(query)

    def probs(rows, cols):
        return masked_gram(query_s, key_ts, doc_col, doc_row, rows, cols, inclusive=True)

    out_lo = mm3s(split(probs(lo, lo)), part(wu_s, lo, EVERY))
    out_hi = mm3s(split(probs(hi, slice(0, TOK))), wu_s)
    b_ref[0, lo, :] = carry_in[lo] * query[lo] - out_lo[:, :HD]
    b_ref[0, hi, :] = carry_in[hi] * query[hi] - out_hi[:, :HD]
    b_ref[1, lo, :] = out_lo[:, HD:]
    b_ref[1, hi, :] = out_hi[:, HD:]


def after(later, earlier):
    product = mm3(later[:, :HD], earlier)
    return jnp.concatenate([product[:, :HD], product[:, HD:] + later[:, HD:]], axis=1)


def pair_kernel(tl_ref, one_ref, two_ref):
    two_ref[...] = after(tl_ref[...], one_ref[...].astype(F32)).astype(BF16)


def window_kernel(tl_ref, one_ref, two_ref, pre_ref, four_t_ref, four_l_ref):
    pre = after(one_ref[...].astype(F32), two_ref[...].astype(F32))
    pre_ref[...] = pre
    four = after(tl_ref[...], pre).astype(BF16)
    four_t_ref[...] = four[:, :HD]
    four_l_ref[...] = four[:, HD:]


def finish_kernel(meta_ref, pre_ref, four_ref, extra_ref, b_ref, out_ref):
    first = meta_ref[1] == 0
    half = TOK // 2
    state = four_ref[...].astype(F32) + extra_ref[...]
    state = mm3(pre_ref[:, :HD], state) + pre_ref[:, HD:]
    out = mm3(b_ref[0], state) + b_ref[1]
    out = out * lax.rsqrt(jnp.mean(out * out, axis=-1, keepdims=True) + 1e-05)
    low, high = out[:half], out[half:]
    out_ref[:half, :] = jnp.where(first, high, low).astype(BF16)
    out_ref[half:, :] = jnp.where(first, low, high).astype(BF16)


SMEM = pl.BlockSpec(memory_space=pltpu.SMEM)
VMEM = pl.BlockSpec(memory_space=pltpu.VMEM)


def call(kernel, scalars, arrays, outs, flops):
    return pl.pallas_call(
        kernel,
        out_shape=tuple(jax.ShapeDtypeStruct(s, d) for s, d in outs),
        in_specs=[SMEM] * len(scalars) + [VMEM] * len(arrays),
        out_specs=(VMEM,) * len(outs),
        compiler_params=pltpu.CompilerParams(vmem_limit_bytes=16 << 20),
        cost_estimate=pl.CostEstimate(flops=flops, bytes_accessed=1 << 20, transcendentals=0),
    )(*scalars, *arrays)


def swap(value):
    return lax.ppermute(value, "c", [(0, 1), (1, 0)])


def ahead(value, steps):
    chips = lax.axis_size("z")
    return lax.ppermute(value, "z", [(i, i + steps) for i in range(chips - steps)])


def to_f16(value, scale):
    return (value.astype(F32) * scale).astype(F16)


def from_f16(value, scale):
    return (value.astype(F32) * (1.0 / scale)).astype(BF16)


def per_device(hidden_in, w_qkv, doc_starts, beta_codes, w_out):
    z = lax.axis_index("z")
    c = lax.axis_index("c")
    first = c == 0
    chips = lax.axis_size("z")
    heads = lax.axis_size("h")
    half = hidden_in.shape[0]
    meta = jnp.stack([z, c]).astype(jnp.int32)
    codes = beta_codes.T

    give, mine = call(
        pack_kernel,
        (meta,),
        (w_qkv, w_out, codes),
        [((HD, 5 * HD), BF16), ((HD, 4 * HD), BF16)],
        1 << 20,
    )
    got = swap(give)
    hidden_sib = swap(hidden_in)

    def chip(cols, axis):
        a, b = mine[:, cols], got[:, cols]
        return jnp.concatenate([jnp.where(first, a, b), jnp.where(first, b, a)], axis=axis)

    turned = [(i * heads + j, j * heads + i) for i in range(chips) for j in range(heads)]
    wo = lax.ppermute(chip(slice(3 * HD, 4 * HD), 1), ("z", "h"), turned)
    wo = jnp.concatenate([wo[:, :HD], wo[:, HD:]], axis=0)
    both = jnp.concatenate(
        [to_f16(chip(slice(0, 3 * HD), 0), W_SCALE), to_f16(wo, WO_SCALE)], axis=1
    )
    both = lax.all_gather(both, "z", axis=0, tiled=True)
    w_all = from_f16(both[:, : 3 * HD], W_SCALE)

    def project(hid):
        return jnp.dot(hid, w_all, preferred_element_type=F32).astype(BF16)

    tl, tl16, b = call(
        local_kernel,
        (meta, doc_starts),
        (project(hidden_in), project(hidden_sib), codes, got),
        [((HD, 2 * HD), F32), ((HD, 2 * HD), BF16), ((2, TOK, HD), F32)],
        3 << 30,
    )
    one = ahead(tl16, 1)
    (two,) = call(pair_kernel, (), (tl, one), [((HD, 2 * HD), BF16)], 1 << 26)
    two = ahead(two, 2)
    pre, four_t, four_l = call(
        window_kernel,
        (),
        (tl, one, two),
        [((HD, 2 * HD), F32), ((HD, HD), BF16), ((HD, HD), BF16)],
        1 << 26,
    )

    here = jnp.arange(chips, dtype=jnp.int32)[:, None]
    starts = doc_starts[None, :]
    since = jnp.max(jnp.where(starts < here * TOK, starts // TOK, 0), axis=1)
    reach_back = jnp.any(here[:, 0] - since > 7)

    def fetch_far(t, add):
        eight_t, eight_l, twelve = ahead(t, 8), ahead(add, 8), ahead(add, 12)
        state = jnp.dot(eight_t, twelve, preferred_element_type=F32) + eight_l.astype(F32)
        return jnp.dot(ahead(t, 4).astype(F32), state, precision=lax.Precision.HIGHEST)

    extra = lax.cond(
        reach_back, fetch_far, lambda t, add: jnp.zeros((HD, HD), F32), four_t, four_l
    )
    (normed,) = call(
        finish_kernel,
        (meta,),
        (pre, ahead(four_l, 4), extra, b),
        [((TOK, HD), BF16)],
        1 << 28,
    )
    normed_all = from_f16(lax.all_gather(to_f16(normed, N_SCALE), "h", axis=0), N_SCALE)
    wo_cols = from_f16(both[:, 3 * HD :], WO_SCALE).reshape(chips, 2, HD, HD)
    wo_cols = wo_cols.transpose(0, 2, 1, 3).reshape(chips, HD, 2 * HD)

    def output(rows):
        return jnp.einsum("htf,hfn->tn", rows, wo_cols, preferred_element_type=F32)

    sent = swap(output(normed_all[:, :half]))
    return (output(normed_all[:, half:]) + sent).astype(BF16)


def solution(mesh):
    seq, head = mesh.devices.shape
    fine = Mesh(mesh.devices.reshape(seq // 2, 2, head), ("z", "c", "h"))
    tokens = ("z", "c")
    in_specs = (P(tokens, None), P(None, tokens, "h"), P(), P(tokens, "h"), P("h", tokens))
    return jax.shard_map(
        per_device, mesh=fine, in_specs=in_specs, out_specs=P(tokens, "h"), check_vma=False
    )
```

```python
import jax
import jax.numpy as jnp
from jax import lax
from jax.experimental import pallas as pl
from jax.experimental.pallas import tpu as pltpu
from jax.sharding import Mesh
from jax.sharding import PartitionSpec as P

F32 = jnp.float32
BF16 = jnp.bfloat16
F16 = jnp.float16
HD = 128
TOK = 512
W_SCALE = 2.0**19
WO_SCALE = 2.0**18
N_SCALE = 2.0**12
NN = (((1,), (0,)), ((), ()))


def split(a):
    hi = a.astype(BF16)
    return hi, (a - hi.astype(F32)).astype(BF16)


def dot(a, b):
    return lax.dot_general(a, b, NN, preferred_element_type=F32)


def mm3s(a, b):
    (ah, al), (bh, bl) = a, b
    return dot(
        jnp.concatenate([ah, ah, al], axis=1), jnp.concatenate([bh, bl, bh], axis=0)
    )


def mm3(a, b):
    return mm3s(split(a), split(b))


def unit_rows(m):
    return m * lax.rsqrt(jnp.sum(m * m, axis=-1, keepdims=True) + 1e-06)


def count_le(ds_ref, pos):
    total = jnp.zeros(jnp.shape(pos), jnp.int32)
    for j in range(ds_ref.shape[0]):
        total = total + (ds_ref[j] <= pos).astype(jnp.int32)
    return total


def doc_info(meta_ref, ds_ref):
    pos0 = meta_ref[0] * TOK
    doc_col = count_le(ds_ref, pos0 + lax.broadcasted_iota(jnp.int32, (TOK, 1), 0))
    doc_row = count_le(ds_ref, pos0 + lax.broadcasted_iota(jnp.int32, (1, TOK), 1))
    return doc_col, doc_row, count_le(ds_ref, pos0 - 1), count_le(ds_ref, pos0 + TOK - 1)


def in_order(first, own, sib):
    return jnp.concatenate([jnp.where(first, own, sib), jnp.where(first, sib, own)], axis=0)


def part(pair, rows, cols):
    return pair[0][rows, cols], pair[1][rows, cols]


EVERY = slice(None)


def masked_gram(left, right_t, doc_col, doc_row, rows, cols, inclusive=False, scale=None):
    gram = mm3s(part(left, rows, EVERY), part(right_t, EVERY, cols))
    r = lax.broadcasted_iota(jnp.int32, gram.shape, 0) + rows.start
    c = lax.broadcasted_iota(jnp.int32, gram.shape, 1) + cols.start
    keep = (c <= r) if inclusive else (c < r)
    keep = keep & (doc_col[rows] == doc_row[:, cols])
    if scale is not None:
        gram = scale[rows] * gram
    return jnp.where(keep, gram, 0.0)


def pack_kernel(
    meta_ref, w_hbm, wo_hbm, codes_hbm, give_ref, mine_ref, w_ref, wo_ref, codes_ref, sems
):
    first = meta_ref[1] == 0
    copies = [
        pltpu.make_async_copy(source, target, sems.at[i])
        for i, (source, target) in enumerate(
            ((codes_hbm, codes_ref), (w_hbm, w_ref), (wo_hbm, wo_ref))
        )
    ]
    for copy in copies:
        copy.start()

    def put(place, mine, other):
        cols = slice(HD * place, HD * place + HD)
        mine_ref[:, cols] = jnp.where(first, mine, other).astype(BF16)
        give_ref[:, cols] = jnp.where(first, other, mine).astype(BF16)

    copies[0].wait()
    codes = codes_ref[...].astype(F32)
    other = jnp.where(first, codes[1:2], codes[0:1])
    row = lax.broadcasted_iota(jnp.int32, (HD, HD), 0)
    give_ref[:, 4 * HD :] = jnp.where(row == 0, other[:, :HD], other[:, HD:]).astype(BF16)
    copies[1].wait()
    for p in range(3):
        put(p, w_ref[p, :, :HD].astype(F32), w_ref[p, :, HD:].astype(F32))
    copies[2].wait()
    put(3, wo_ref[:HD].astype(F32), wo_ref[HD:].astype(F32))


def local_kernel(
    meta_ref, ds_ref, own_ref, sib_ref, codes_ref, got_ref, tl_ref, tl16_ref, b_ref
):
    first = meta_ref[1] == 0
    half = TOK // 2
    qkv = in_order(first, own_ref[...].astype(F32), sib_ref[...].astype(F32))
    query = unit_rows(qkv[:, :HD])
    key = unit_rows(qkv[:, HD : 2 * HD])
    value = qkv[:, 2 * HD :]
    codes = codes_ref[...].astype(F32)
    own_codes = jnp.where(first, codes[0:1], codes[1:2])
    got = got_ref[0:8, 4 * HD :].astype(F32)
    sib_codes = jnp.concatenate([got[0:1], got[1:2]], axis=1)
    codes = jnp.concatenate(
        [jnp.where(first, own_codes, sib_codes), jnp.where(first, sib_codes, own_codes)], axis=1
    )
    beta = 1.6 + 0.1 * jnp.transpose(jnp.broadcast_to(codes, (8, TOK)))[:, 0:1]
    doc_col, doc_row, prev_doc, last_doc = doc_info(meta_ref, ds_ref)
    carry_in = (doc_col == prev_doc).astype(F32)
    tail_row = (doc_row == last_doc).astype(F32)
    last_keep = (last_doc == prev_doc).astype(F32)

    key_s = split(key)
    key_t = jnp.transpose(key)
    key_ts = split(key_t)

    def system(rows, cols):
        return masked_gram(key_s, key_ts, doc_col, doc_row, rows, cols, scale=beta)

    quarter = [slice(128 * i, 128 * i + 128) for i in range(4)]
    rows128 = lax.broadcasted_iota(jnp.int32, (128, 128), 0)
    cols128 = lax.broadcasted_iota(jnp.int32, (128, 128), 1)
    eye128 = (rows128 == cols128).astype(F32)
    diag = [system(s, s) for s in quarter]
    inv = []
    for a in diag:
        m = ((rows128 >> 1) == (cols128 >> 1)) & (rows128 != cols128)
        inv.append(eye128 - jnp.where(m, a, 0.0))
    for lev in range(1, 7):
        m = ((rows128 >> (lev + 1)) == (cols128 >> (lev + 1))) & (
            (rows128 >> lev) != (cols128 >> lev)
        )
        xs = [split(x) for x in inv]
        ys = [mm3s(x, split(jnp.where(m, a, 0.0))) for x, a in zip(xs, diag)]
        inv = [x - mm3s(split(y), s) for x, y, s in zip(inv, ys, xs)]
    pair_inv = []
    for i in (0, 2):
        off = system(quarter[i + 1], quarter[i])
        low = -mm3(mm3(inv[i + 1], off), inv[i])
        top = jnp.concatenate([inv[i], jnp.zeros((128, 128), F32)], axis=1)
        bottom = jnp.concatenate([low, inv[i + 1]], axis=1)
        pair_inv.append(jnp.concatenate([top, bottom], axis=0))
    lo, hi = slice(0, half), slice(half, TOK)
    right = beta * jnp.concatenate([carry_in * key, value], axis=1)
    cross = system(hi, lo)
    wu_lo = mm3(pair_inv[0], right[lo])
    wu_lo_s = split(wu_lo)
    wu_hi = mm3(pair_inv[1], right[hi] - mm3s(split(cross), wu_lo_s))
    wu_hi_s = split(wu_hi)
    wu_s = tuple(jnp.concatenate([x, y], axis=0) for x, y in zip(wu_lo_s, wu_hi_s))
    tl = mm3s(split(tail_row * key_t), wu_s)
    tl_ref[:, :HD] = last_keep * eye128 - tl[:, :HD]
    tl_ref[:, HD:] = tl[:, HD:]
    tl16_ref[...] = tl_ref[...].astype(BF16)

    query_s = split(query)

    def probs(rows, cols):
        return masked_gram(query_s, key_ts, doc_col, doc_row, rows, cols, inclusive=True)

    out_lo = mm3s(split(probs(lo, lo)), part(wu_s, lo, EVERY))
    out_hi = mm3s(split(probs(hi, slice(0, TOK))), wu_s)
    b_ref[0, lo, :] = carry_in[lo] * query[lo] - out_lo[:, :HD]
    b_ref[0, hi, :] = carry_in[hi] * query[hi] - out_hi[:, :HD]
    b_ref[1, lo, :] = out_lo[:, HD:]
    b_ref[1, hi, :] = out_hi[:, HD:]


def after(later, earlier):
    product = mm3(later[:, :HD], earlier)
    return jnp.concatenate([product[:, :HD], product[:, HD:] + later[:, HD:]], axis=1)


def pair_kernel(tl_ref, one_ref, two_ref):
    two_ref[...] = after(tl_ref[...], one_ref[...].astype(F32)).astype(BF16)


def window_kernel(tl_ref, one_ref, two_ref, pre_ref, four_t_ref, four_l_ref):
    pre = after(one_ref[...].astype(F32), two_ref[...].astype(F32))
    pre_ref[...] = pre
    four = after(tl_ref[...], pre).astype(BF16)
    four_t_ref[...] = four[:, :HD]
    four_l_ref[...] = four[:, HD:]


def finish_kernel(meta_ref, pre_ref, four_ref, extra_ref, b_ref, out_ref):
    first = meta_ref[1] == 0
    half = TOK // 2
    state = four_ref[...].astype(F32) + extra_ref[...]
    state = mm3(pre_ref[:, :HD], state) + pre_ref[:, HD:]
    out = mm3(b_ref[0], state) + b_ref[1]
    out = out * lax.rsqrt(jnp.mean(out * out, axis=-1, keepdims=True) + 1e-05)
    low, high = out[:half], out[half:]
    out_ref[:half, :] = jnp.where(first, high, low).astype(BF16)
    out_ref[half:, :] = jnp.where(first, low, high).astype(BF16)


SMEM = pl.BlockSpec(memory_space=pltpu.SMEM)
VMEM = pl.BlockSpec(memory_space=pltpu.VMEM)


def call(kernel, scalars, arrays, outs, flops):
    return pl.pallas_call(
        kernel,
        out_shape=tuple(jax.ShapeDtypeStruct(s, d) for s, d in outs),
        in_specs=[SMEM] * len(scalars) + [VMEM] * len(arrays),
        out_specs=(VMEM,) * len(outs),
        compiler_params=pltpu.CompilerParams(vmem_limit_bytes=16 << 20),
        cost_estimate=pl.CostEstimate(flops=flops, bytes_accessed=1 << 20, transcendentals=0),
    )(*scalars, *arrays)


def swap(value):
    return lax.ppermute(value, "c", [(0, 1), (1, 0)])


def ahead(value, steps):
    chips = lax.axis_size("z")
    return lax.ppermute(value, "z", [(i, i + steps) for i in range(chips - steps)])


def to_f16(value, scale):
    return (value.astype(F32) * scale).astype(F16)


def from_f16(value, scale):
    return (value.astype(F32) * (1.0 / scale)).astype(BF16)


def per_device(hidden_in, w_qkv, doc_starts, beta_codes, w_out):
    z = lax.axis_index("z")
    c = lax.axis_index("c")
    first = c == 0
    chips = lax.axis_size("z")
    heads = lax.axis_size("h")
    half = hidden_in.shape[0]
    meta = jnp.stack([z, c]).astype(jnp.int32)
    codes = beta_codes.T

    whole = pl.BlockSpec(memory_space=pltpu.HBM)
    give, mine = pl.pallas_call(
        pack_kernel,
        out_shape=(
            jax.ShapeDtypeStruct((HD, 5 * HD), BF16),
            jax.ShapeDtypeStruct((HD, 4 * HD), BF16),
        ),
        in_specs=[SMEM, whole, whole, whole],
        out_specs=(VMEM, VMEM),
        scratch_shapes=[
            pltpu.VMEM(w_qkv.shape, BF16),
            pltpu.VMEM(w_out.shape, BF16),
            pltpu.VMEM(codes.shape, jnp.int32),
            pltpu.SemaphoreType.DMA((3,)),
        ],
        compiler_params=pltpu.CompilerParams(vmem_limit_bytes=8 << 20),
    )(meta, w_qkv, w_out, codes)
    got = swap(give)
    hidden_sib = swap(hidden_in)

    def chip(cols, axis):
        a, b = mine[:, cols], got[:, cols]
        return jnp.concatenate([jnp.where(first, a, b), jnp.where(first, b, a)], axis=axis)

    turned = [(i * heads + j, j * heads + i) for i in range(chips) for j in range(heads)]
    wo = lax.ppermute(chip(slice(3 * HD, 4 * HD), 1), ("z", "h"), turned)
    wo = jnp.concatenate([wo[:, :HD], wo[:, HD:]], axis=0)
    both = jnp.concatenate(
        [to_f16(chip(slice(0, 3 * HD), 0), W_SCALE), to_f16(wo, WO_SCALE)], axis=1
    )
    both = lax.all_gather(both, "z", axis=0, tiled=True)
    w_all = from_f16(both[:, : 3 * HD], W_SCALE)

    def project(hid):
        return jnp.dot(hid, w_all, preferred_element_type=F32).astype(BF16)

    tl, tl16, b = call(
        local_kernel,
        (meta, doc_starts),
        (project(hidden_in), project(hidden_sib), codes, got),
        [((HD, 2 * HD), F32), ((HD, 2 * HD), BF16), ((2, TOK, HD), F32)],
        3 << 30,
    )
    one = ahead(tl16, 1)
    (two,) = call(pair_kernel, (), (tl, one), [((HD, 2 * HD), BF16)], 1 << 26)
    two = ahead(two, 2)
    pre, four_t, four_l = call(
        window_kernel,
        (),
        (tl, one, two),
        [((HD, 2 * HD), F32), ((HD, HD), BF16), ((HD, HD), BF16)],
        1 << 26,
    )

    here = jnp.arange(chips, dtype=jnp.int32)[:, None]
    starts = doc_starts[None, :]
    since = jnp.max(jnp.where(starts < here * TOK, starts // TOK, 0), axis=1)
    reach_back = jnp.any(here[:, 0] - since > 7)

    def fetch_far(t, add):
        eight_t, eight_l, twelve = ahead(t, 8), ahead(add, 8), ahead(add, 12)
        state = jnp.dot(eight_t, twelve, preferred_element_type=F32) + eight_l.astype(F32)
        return jnp.dot(ahead(t, 4).astype(F32), state, precision=lax.Precision.HIGHEST)

    extra = lax.cond(
        reach_back, fetch_far, lambda t, add: jnp.zeros((HD, HD), F32), four_t, four_l
    )
    (normed,) = call(
        finish_kernel,
        (meta,),
        (pre, ahead(four_l, 4), extra, b),
        [((TOK, HD), BF16)],
        1 << 28,
    )
    normed_all = lax.all_gather(to_f16(normed, N_SCALE), "h", axis=0)
    wo_cols = from_f16(both[:, 3 * HD :], WO_SCALE).reshape(chips, 2, HD, HD)
    wo_cols = wo_cols.transpose(0, 2, 1, 3).reshape(chips, HD, 2 * HD)

    def output(rows):
        rows = from_f16(rows, N_SCALE)
        return jnp.einsum("htf,hfn->tn", rows, wo_cols, preferred_element_type=F32)

    sent = swap(output(normed_all[:, :half]))
    return (output(normed_all[:, half:]) + sent).astype(BF16)


def solution(mesh):
    seq, head = mesh.devices.shape
    fine = Mesh(mesh.devices.reshape(seq // 2, 2, head), ("z", "c", "h"))
    tokens = ("z", "c")
    in_specs = (P(tokens, None), P(None, tokens, "h"), P(), P(tokens, "h"), P("h", tokens))
    return jax.shard_map(
        per_device, mesh=fine, in_specs=in_specs, out_specs=P(tokens, "h"), check_vma=False
    )
```

```python
import jax
import jax.numpy as jnp
from jax import lax
from jax.experimental import pallas as pl
from jax.experimental.pallas import tpu as pltpu
from jax.sharding import Mesh
from jax.sharding import PartitionSpec as P

F32 = jnp.float32
BF16 = jnp.bfloat16
F16 = jnp.float16
HD = 128
TOK = 512
W_SCALE = 2.0**19
WO_SCALE = 2.0**18
N_SCALE = 2.0**12
NN = (((1,), (0,)), ((), ()))


def split(a):
    hi = a.astype(BF16)
    return hi, (a - hi.astype(F32)).astype(BF16)


def dot(a, b):
    return lax.dot_general(a, b, NN, preferred_element_type=F32)


def mm3s(a, b):
    (ah, al), (bh, bl) = a, b
    return dot(
        jnp.concatenate([ah, ah, al], axis=1), jnp.concatenate([bh, bl, bh], axis=0)
    )


def mm3(a, b):
    return mm3s(split(a), split(b))


def unit_rows(m):
    return m * lax.rsqrt(jnp.sum(m * m, axis=-1, keepdims=True) + 1e-06)


def count_le(ds_ref, pos):
    total = jnp.zeros(jnp.shape(pos), jnp.int32)
    for j in range(ds_ref.shape[0]):
        total = total + (ds_ref[j] <= pos).astype(jnp.int32)
    return total


def doc_info(meta_ref, ds_ref):
    pos0 = meta_ref[0] * TOK
    doc_col = count_le(ds_ref, pos0 + lax.broadcasted_iota(jnp.int32, (TOK, 1), 0))
    doc_row = count_le(ds_ref, pos0 + lax.broadcasted_iota(jnp.int32, (1, TOK), 1))
    return doc_col, doc_row, count_le(ds_ref, pos0 - 1), count_le(ds_ref, pos0 + TOK - 1)


def in_order(first, own, sib):
    return jnp.concatenate([jnp.where(first, own, sib), jnp.where(first, sib, own)], axis=0)


def part(pair, rows, cols):
    return pair[0][rows, cols], pair[1][rows, cols]


EVERY = slice(None)


def masked_gram(left, right_t, doc_col, doc_row, rows, cols, inclusive=False, scale=None):
    gram = mm3s(part(left, rows, EVERY), part(right_t, EVERY, cols))
    r = lax.broadcasted_iota(jnp.int32, gram.shape, 0) + rows.start
    c = lax.broadcasted_iota(jnp.int32, gram.shape, 1) + cols.start
    keep = (c <= r) if inclusive else (c < r)
    keep = keep & (doc_col[rows] == doc_row[:, cols])
    if scale is not None:
        gram = scale[rows] * gram
    return jnp.where(keep, gram, 0.0)


def pack_kernel(meta_ref, w_hbm, codes_hbm, give_ref, mine_ref, w_ref, codes_ref, sems):
    first = meta_ref[1] == 0
    copies = [
        pltpu.make_async_copy(codes_hbm, codes_ref, sems.at[0]),
        pltpu.make_async_copy(w_hbm, w_ref, sems.at[1]),
    ]
    for copy in copies:
        copy.start()
    copies[0].wait()
    codes = codes_ref[...].astype(F32)
    other = jnp.where(first, codes[1:2], codes[0:1])
    row = lax.broadcasted_iota(jnp.int32, (HD, HD), 0)
    give_ref[:, 3 * HD :] = jnp.where(row == 0, other[:, :HD], other[:, HD:]).astype(BF16)
    copies[1].wait()
    for p in range(3):
        cols = slice(HD * p, HD * p + HD)
        left = w_ref[p, :, :HD].astype(F32)
        right = w_ref[p, :, HD:].astype(F32)
        mine_ref[:, cols] = jnp.where(first, left, right).astype(BF16)
        give_ref[:, cols] = jnp.where(first, right, left).astype(BF16)


def local_kernel(
    meta_ref, ds_ref, own_ref, sib_ref, codes_ref, got_ref, tl_ref, tl16_ref, b_ref
):
    first = meta_ref[1] == 0
    half = TOK // 2
    qkv = in_order(first, own_ref[...].astype(F32), sib_ref[...].astype(F32))
    query = unit_rows(qkv[:, :HD])
    key = unit_rows(qkv[:, HD : 2 * HD])
    value = qkv[:, 2 * HD :]
    codes = codes_ref[...].astype(F32)
    own_codes = jnp.where(first, codes[0:1], codes[1:2])
    got = got_ref[0:8, 3 * HD :].astype(F32)
    sib_codes = jnp.concatenate([got[0:1], got[1:2]], axis=1)
    codes = jnp.concatenate(
        [jnp.where(first, own_codes, sib_codes), jnp.where(first, sib_codes, own_codes)], axis=1
    )
    beta = 1.6 + 0.1 * jnp.transpose(jnp.broadcast_to(codes, (8, TOK)))[:, 0:1]
    doc_col, doc_row, prev_doc, last_doc = doc_info(meta_ref, ds_ref)
    carry_in = (doc_col == prev_doc).astype(F32)
    tail_row = (doc_row == last_doc).astype(F32)
    last_keep = (last_doc == prev_doc).astype(F32)

    key_s = split(key)
    key_t = jnp.transpose(key)
    key_ts = split(key_t)

    def system(rows, cols):
        return masked_gram(key_s, key_ts, doc_col, doc_row, rows, cols, scale=beta)

    quarter = [slice(128 * i, 128 * i + 128) for i in range(4)]
    rows128 = lax.broadcasted_iota(jnp.int32, (128, 128), 0)
    cols128 = lax.broadcasted_iota(jnp.int32, (128, 128), 1)
    eye128 = (rows128 == cols128).astype(F32)
    diag = [system(s, s) for s in quarter]
    inv = []
    for a in diag:
        m = ((rows128 >> 1) == (cols128 >> 1)) & (rows128 != cols128)
        inv.append(eye128 - jnp.where(m, a, 0.0))
    for lev in range(1, 7):
        m = ((rows128 >> (lev + 1)) == (cols128 >> (lev + 1))) & (
            (rows128 >> lev) != (cols128 >> lev)
        )
        xs = [split(x) for x in inv]
        ys = [mm3s(x, split(jnp.where(m, a, 0.0))) for x, a in zip(xs, diag)]
        inv = [x - mm3s(split(y), s) for x, y, s in zip(inv, ys, xs)]
    pair_inv = []
    for i in (0, 2):
        off = system(quarter[i + 1], quarter[i])
        low = -mm3(mm3(inv[i + 1], off), inv[i])
        top = jnp.concatenate([inv[i], jnp.zeros((128, 128), F32)], axis=1)
        bottom = jnp.concatenate([low, inv[i + 1]], axis=1)
        pair_inv.append(jnp.concatenate([top, bottom], axis=0))
    lo, hi = slice(0, half), slice(half, TOK)
    right = beta * jnp.concatenate([carry_in * key, value], axis=1)
    cross = system(hi, lo)
    wu_lo = mm3(pair_inv[0], right[lo])
    wu_lo_s = split(wu_lo)
    wu_hi = mm3(pair_inv[1], right[hi] - mm3s(split(cross), wu_lo_s))
    wu_hi_s = split(wu_hi)
    wu_s = tuple(jnp.concatenate([x, y], axis=0) for x, y in zip(wu_lo_s, wu_hi_s))
    tl = mm3s(split(tail_row * key_t), wu_s)
    tl_ref[:, :HD] = last_keep * eye128 - tl[:, :HD]
    tl_ref[:, HD:] = tl[:, HD:]
    tl16_ref[...] = tl_ref[...].astype(BF16)

    query_s = split(query)

    def probs(rows, cols):
        return masked_gram(query_s, key_ts, doc_col, doc_row, rows, cols, inclusive=True)

    out_lo = mm3s(split(probs(lo, lo)), part(wu_s, lo, EVERY))
    out_hi = mm3s(split(probs(hi, slice(0, TOK))), wu_s)
    b_ref[0, lo, :] = carry_in[lo] * query[lo] - out_lo[:, :HD]
    b_ref[0, hi, :] = carry_in[hi] * query[hi] - out_hi[:, :HD]
    b_ref[1, lo, :] = out_lo[:, HD:]
    b_ref[1, hi, :] = out_hi[:, HD:]


def after(later, earlier):
    product = mm3(later[:, :HD], earlier)
    return jnp.concatenate([product[:, :HD], product[:, HD:] + later[:, HD:]], axis=1)


def pair_kernel(tl_ref, one_ref, two_ref):
    two_ref[...] = after(tl_ref[...], one_ref[...].astype(F32)).astype(BF16)


def window_kernel(tl_ref, one_ref, two_ref, pre_ref, four_t_ref, four_l_ref):
    pre = after(one_ref[...].astype(F32), two_ref[...].astype(F32))
    pre_ref[...] = pre
    four = after(tl_ref[...], pre).astype(BF16)
    four_t_ref[...] = four[:, :HD]
    four_l_ref[...] = four[:, HD:]


def finish_kernel(meta_ref, pre_ref, four_ref, extra_ref, b_ref, out_ref):
    first = meta_ref[1] == 0
    half = TOK // 2
    state = four_ref[...].astype(F32) + extra_ref[...]
    state = mm3(pre_ref[:, :HD], state) + pre_ref[:, HD:]
    out = mm3(b_ref[0], state) + b_ref[1]
    out = out * lax.rsqrt(jnp.mean(out * out, axis=-1, keepdims=True) + 1e-05)
    low, high = out[:half], out[half:]
    out_ref[:half, :] = jnp.where(first, high, low).astype(BF16)
    out_ref[half:, :] = jnp.where(first, low, high).astype(BF16)


SMEM = pl.BlockSpec(memory_space=pltpu.SMEM)
VMEM = pl.BlockSpec(memory_space=pltpu.VMEM)


def call(kernel, scalars, arrays, outs, flops):
    return pl.pallas_call(
        kernel,
        out_shape=tuple(jax.ShapeDtypeStruct(s, d) for s, d in outs),
        in_specs=[SMEM] * len(scalars) + [VMEM] * len(arrays),
        out_specs=(VMEM,) * len(outs),
        compiler_params=pltpu.CompilerParams(vmem_limit_bytes=16 << 20),
        cost_estimate=pl.CostEstimate(flops=flops, bytes_accessed=1 << 20, transcendentals=0),
    )(*scalars, *arrays)


def swap(value):
    return lax.ppermute(value, "c", [(0, 1), (1, 0)])


def ahead(value, steps):
    chips = lax.axis_size("z")
    return lax.ppermute(value, "z", [(i, i + steps) for i in range(chips - steps)])


def to_f16(value, scale):
    return (value.astype(F32) * scale).astype(F16)


def from_f16(value, scale):
    return (value.astype(F32) * (1.0 / scale)).astype(BF16)


def per_device(hidden_in, w_qkv, doc_starts, beta_codes, w_out):
    z = lax.axis_index("z")
    c = lax.axis_index("c")
    first = c == 0
    chips = lax.axis_size("z")
    heads = lax.axis_size("h")
    half = hidden_in.shape[0]
    meta = jnp.stack([z, c]).astype(jnp.int32)
    codes = beta_codes.T

    def turned(core):
        pairs = [
            ((i * 2 + k) * heads + j, (j * 2 + (k ^ core)) * heads + i)
            for i in range(chips)
            for k in range(2)
            for j in range(heads)
        ]
        rows = lax.ppermute(w_out, ("z", "c", "h"), pairs)
        return jnp.where(first, rows[:HD], rows[HD:])

    wo_same, wo_cross = turned(0), turned(1)
    wo = jnp.concatenate(
        [jnp.where(first, wo_same, wo_cross), jnp.where(first, wo_cross, wo_same)], axis=0
    )
    whole = pl.BlockSpec(memory_space=pl.ANY)
    give, mine = pl.pallas_call(
        pack_kernel,
        out_shape=(
            jax.ShapeDtypeStruct((HD, 4 * HD), BF16),
            jax.ShapeDtypeStruct((HD, 3 * HD), BF16),
        ),
        in_specs=[SMEM, whole, whole],
        out_specs=(VMEM, VMEM),
        scratch_shapes=[
            pltpu.VMEM(w_qkv.shape, BF16),
            pltpu.VMEM(codes.shape, jnp.int32),
            pltpu.SemaphoreType.DMA((2,)),
        ],
        compiler_params=pltpu.CompilerParams(vmem_limit_bytes=60 << 20),
    )(meta, w_qkv, codes)
    got = swap(give)
    hidden_sib = swap(hidden_in)

    other = got[:, : 3 * HD]
    w_chip = jnp.concatenate(
        [jnp.where(first, mine, other), jnp.where(first, other, mine)], axis=0
    )
    both = jnp.concatenate(
        [to_f16(w_chip, W_SCALE), to_f16(wo, WO_SCALE)], axis=1
    )
    both = lax.all_gather(both, "z", axis=0, tiled=True)
    w_all = from_f16(both[:, : 3 * HD], W_SCALE)

    def project(hid):
        return jnp.dot(hid, w_all, preferred_element_type=F32).astype(BF16)

    tl, tl16, b = call(
        local_kernel,
        (meta, doc_starts),
        (project(hidden_in), project(hidden_sib), codes, got),
        [((HD, 2 * HD), F32), ((HD, 2 * HD), BF16), ((2, TOK, HD), F32)],
        3 << 30,
    )
    one = ahead(tl16, 1)
    (two,) = call(pair_kernel, (), (tl, one), [((HD, 2 * HD), BF16)], 1 << 26)
    two = ahead(two, 2)
    pre, four_t, four_l = call(
        window_kernel,
        (),
        (tl, one, two),
        [((HD, 2 * HD), F32), ((HD, HD), BF16), ((HD, HD), BF16)],
        1 << 26,
    )

    here = jnp.arange(chips, dtype=jnp.int32)[:, None]
    starts = doc_starts[None, :]
    since = jnp.max(jnp.where(starts < here * TOK, starts // TOK, 0), axis=1)
    reach_back = jnp.any(here[:, 0] - since > 7)

    def fetch_far(t, add):
        eight_t, eight_l, twelve = ahead(t, 8), ahead(add, 8), ahead(add, 12)
        state = jnp.dot(eight_t, twelve, preferred_element_type=F32) + eight_l.astype(F32)
        return jnp.dot(ahead(t, 4).astype(F32), state, precision=lax.Precision.HIGHEST)

    extra = lax.cond(
        reach_back, fetch_far, lambda t, add: jnp.zeros((HD, HD), F32), four_t, four_l
    )
    (normed,) = call(
        finish_kernel,
        (meta,),
        (pre, ahead(four_l, 4), extra, b),
        [((TOK, HD), BF16)],
        1 << 28,
    )
    normed_all = lax.all_gather(to_f16(normed, N_SCALE), "h", axis=0)
    wo_cols = from_f16(both[:, 3 * HD :], WO_SCALE).reshape(chips, 2, HD, HD)
    wo_cols = wo_cols.transpose(0, 2, 1, 3).reshape(chips, HD, 2 * HD)

    def output(rows):
        rows = from_f16(rows, N_SCALE)
        return jnp.einsum("htf,hfn->tn", rows, wo_cols, preferred_element_type=F32)

    sent = swap(output(normed_all[:, :half]))
    return (output(normed_all[:, half:]) + sent).astype(BF16)


def solution(mesh):
    seq, head = mesh.devices.shape
    fine = Mesh(mesh.devices.reshape(seq // 2, 2, head), ("z", "c", "h"))
    tokens = ("z", "c")
    in_specs = (P(tokens, None), P(None, tokens, "h"), P(), P(tokens, "h"), P("h", tokens))
    return jax.shard_map(
        per_device, mesh=fine, in_specs=in_specs, out_specs=P(tokens, "h"), check_vma=False
    )
```

```python
import jax
import jax.numpy as jnp
from jax import lax
from jax.experimental import pallas as pl
from jax.experimental.pallas import tpu as pltpu
from jax.sharding import Mesh
from jax.sharding import PartitionSpec as P

F32 = jnp.float32
BF16 = jnp.bfloat16
F16 = jnp.float16
HD = 128
TOK = 512
W_SCALE = 2.0**19
WO_SCALE = 2.0**18
N_SCALE = 2.0**12
NN = (((1,), (0,)), ((), ()))


def split(a):
    hi = a.astype(BF16)
    return hi, (a - hi.astype(F32)).astype(BF16)


def dot(a, b):
    return lax.dot_general(a, b, NN, preferred_element_type=F32)


def mm3s(a, b):
    (ah, al), (bh, bl) = a, b
    return dot(
        jnp.concatenate([ah, ah, al], axis=1), jnp.concatenate([bh, bl, bh], axis=0)
    )


def mm3(a, b):
    return mm3s(split(a), split(b))


def unit_rows(m):
    return m * lax.rsqrt(jnp.sum(m * m, axis=-1, keepdims=True) + 1e-06)


def count_le(ds_ref, pos):
    total = jnp.zeros(jnp.shape(pos), jnp.int32)
    for j in range(ds_ref.shape[0]):
        total = total + (ds_ref[j] <= pos).astype(jnp.int32)
    return total


def doc_info(meta_ref, ds_ref):
    pos0 = meta_ref[0] * TOK
    doc_col = count_le(ds_ref, pos0 + lax.broadcasted_iota(jnp.int32, (TOK, 1), 0))
    doc_row = count_le(ds_ref, pos0 + lax.broadcasted_iota(jnp.int32, (1, TOK), 1))
    return doc_col, doc_row, count_le(ds_ref, pos0 - 1), count_le(ds_ref, pos0 + TOK - 1)


def in_order(first, own, sib):
    return jnp.concatenate([jnp.where(first, own, sib), jnp.where(first, sib, own)], axis=0)


def part(pair, rows, cols):
    return pair[0][rows, cols], pair[1][rows, cols]


EVERY = slice(None)


def masked_gram(left, right_t, doc_col, doc_row, rows, cols, inclusive=False, scale=None):
    gram = mm3s(part(left, rows, EVERY), part(right_t, EVERY, cols))
    r = lax.broadcasted_iota(jnp.int32, gram.shape, 0) + rows.start
    c = lax.broadcasted_iota(jnp.int32, gram.shape, 1) + cols.start
    keep = (c <= r) if inclusive else (c < r)
    keep = keep & (doc_col[rows] == doc_row[:, cols])
    if scale is not None:
        gram = scale[rows] * gram
    return jnp.where(keep, gram, 0.0)


def pack_kernel(meta_ref, w_ref, codes_ref, give_ref, mine_ref):
    first = meta_ref[1] == 0
    codes = codes_ref[...].astype(F32)
    other = jnp.where(first, codes[1:2], codes[0:1])
    row = lax.broadcasted_iota(jnp.int32, (HD, HD), 0)
    give_ref[:, 3 * HD :] = jnp.where(row == 0, other[:, :HD], other[:, HD:]).astype(BF16)
    for p in range(3):
        cols = slice(HD * p, HD * p + HD)
        left = w_ref[p, :, :HD].astype(F32)
        right = w_ref[p, :, HD:].astype(F32)
        mine_ref[:, cols] = jnp.where(first, left, right).astype(BF16)
        give_ref[:, cols] = jnp.where(first, right, left).astype(BF16)


def local_kernel(
    meta_ref, ds_ref, own_ref, sib_ref, codes_ref, got_ref, tl_ref, tl16_ref, b_ref
):
    first = meta_ref[1] == 0
    half = TOK // 2
    qkv = in_order(first, own_ref[...].astype(F32), sib_ref[...].astype(F32))
    query = unit_rows(qkv[:, :HD])
    key = unit_rows(qkv[:, HD : 2 * HD])
    value = qkv[:, 2 * HD :]
    codes = codes_ref[...].astype(F32)
    own_codes = jnp.where(first, codes[0:1], codes[1:2])
    got = got_ref[0:8, 3 * HD :].astype(F32)
    sib_codes = jnp.concatenate([got[0:1], got[1:2]], axis=1)
    codes = jnp.concatenate(
        [jnp.where(first, own_codes, sib_codes), jnp.where(first, sib_codes, own_codes)], axis=1
    )
    beta = 1.6 + 0.1 * jnp.transpose(jnp.broadcast_to(codes, (8, TOK)))[:, 0:1]
    doc_col, doc_row, prev_doc, last_doc = doc_info(meta_ref, ds_ref)
    carry_in = (doc_col == prev_doc).astype(F32)
    tail_row = (doc_row == last_doc).astype(F32)
    last_keep = (last_doc == prev_doc).astype(F32)

    key_s = split(key)
    key_t = jnp.transpose(key)
    key_ts = split(key_t)

    def system(rows, cols):
        return masked_gram(key_s, key_ts, doc_col, doc_row, rows, cols, scale=beta)

    quarter = [slice(128 * i, 128 * i + 128) for i in range(4)]
    rows128 = lax.broadcasted_iota(jnp.int32, (128, 128), 0)
    cols128 = lax.broadcasted_iota(jnp.int32, (128, 128), 1)
    eye128 = (rows128 == cols128).astype(F32)
    diag = [system(s, s) for s in quarter]
    inv = []
    for a in diag:
        m = ((rows128 >> 1) == (cols128 >> 1)) & (rows128 != cols128)
        inv.append(eye128 - jnp.where(m, a, 0.0))
    for lev in range(1, 7):
        m = ((rows128 >> (lev + 1)) == (cols128 >> (lev + 1))) & (
            (rows128 >> lev) != (cols128 >> lev)
        )
        xs = [split(x) for x in inv]
        ys = [mm3s(x, split(jnp.where(m, a, 0.0))) for x, a in zip(xs, diag)]
        inv = [x - mm3s(split(y), s) for x, y, s in zip(inv, ys, xs)]
    pair_inv = []
    for i in (0, 2):
        off = system(quarter[i + 1], quarter[i])
        low = -mm3(mm3(inv[i + 1], off), inv[i])
        top = jnp.concatenate([inv[i], jnp.zeros((128, 128), F32)], axis=1)
        bottom = jnp.concatenate([low, inv[i + 1]], axis=1)
        pair_inv.append(jnp.concatenate([top, bottom], axis=0))
    lo, hi = slice(0, half), slice(half, TOK)
    right = beta * jnp.concatenate([carry_in * key, value], axis=1)
    cross = system(hi, lo)
    wu_lo = mm3(pair_inv[0], right[lo])
    wu_lo_s = split(wu_lo)
    wu_hi = mm3(pair_inv[1], right[hi] - mm3s(split(cross), wu_lo_s))
    wu_hi_s = split(wu_hi)
    wu_s = tuple(jnp.concatenate([x, y], axis=0) for x, y in zip(wu_lo_s, wu_hi_s))
    tl = mm3s(split(tail_row * key_t), wu_s)
    tl_ref[:, :HD] = last_keep * eye128 - tl[:, :HD]
    tl_ref[:, HD:] = tl[:, HD:]
    tl16_ref[...] = tl_ref[...].astype(BF16)

    query_s = split(query)

    def probs(rows, cols):
        return masked_gram(query_s, key_ts, doc_col, doc_row, rows, cols, inclusive=True)

    out_lo = mm3s(split(probs(lo, lo)), part(wu_s, lo, EVERY))
    out_hi = mm3s(split(probs(hi, slice(0, TOK))), wu_s)
    b_ref[0, lo, :] = carry_in[lo] * query[lo] - out_lo[:, :HD]
    b_ref[0, hi, :] = carry_in[hi] * query[hi] - out_hi[:, :HD]
    b_ref[1, lo, :] = out_lo[:, HD:]
    b_ref[1, hi, :] = out_hi[:, HD:]


def after(later, earlier):
    product = mm3(later[:, :HD], earlier)
    return jnp.concatenate([product[:, :HD], product[:, HD:] + later[:, HD:]], axis=1)


def pair_kernel(tl_ref, one_ref, two_ref):
    two_ref[...] = after(tl_ref[...], one_ref[...].astype(F32)).astype(BF16)


def window_kernel(tl_ref, one_ref, two_ref, pre_ref, four_t_ref, four_l_ref):
    pre = after(one_ref[...].astype(F32), two_ref[...].astype(F32))
    pre_ref[...] = pre
    four = after(tl_ref[...], pre).astype(BF16)
    four_t_ref[...] = four[:, :HD]
    four_l_ref[...] = four[:, HD:]


def finish_kernel(meta_ref, pre_ref, four_ref, extra_ref, b_ref, out_ref):
    first = meta_ref[1] == 0
    half = TOK // 2
    state = four_ref[...].astype(F32) + extra_ref[...]
    state = mm3(pre_ref[:, :HD], state) + pre_ref[:, HD:]
    out = mm3(b_ref[0], state) + b_ref[1]
    out = out * lax.rsqrt(jnp.mean(out * out, axis=-1, keepdims=True) + 1e-05)
    low, high = out[:half], out[half:]
    out_ref[:half, :] = jnp.where(first, high, low).astype(BF16)
    out_ref[half:, :] = jnp.where(first, low, high).astype(BF16)


SMEM = pl.BlockSpec(memory_space=pltpu.SMEM)
VMEM = pl.BlockSpec(memory_space=pltpu.VMEM)


def call(kernel, scalars, arrays, outs, flops):
    return pl.pallas_call(
        kernel,
        out_shape=tuple(jax.ShapeDtypeStruct(s, d) for s, d in outs),
        in_specs=[SMEM] * len(scalars) + [VMEM] * len(arrays),
        out_specs=(VMEM,) * len(outs),
        compiler_params=pltpu.CompilerParams(vmem_limit_bytes=16 << 20),
        cost_estimate=pl.CostEstimate(flops=flops, bytes_accessed=1 << 20, transcendentals=0),
    )(*scalars, *arrays)


def swap(value):
    return lax.ppermute(value, "c", [(0, 1), (1, 0)])


def ahead(value, steps):
    chips = lax.axis_size("z")
    return lax.ppermute(value, "z", [(i, i + steps) for i in range(chips - steps)])


def to_f16(value, scale):
    return (value.astype(F32) * scale).astype(F16)


def from_f16(value, scale):
    return (value.astype(F32) * (1.0 / scale)).astype(BF16)


def per_device(hidden_in, w_qkv, doc_starts, beta_codes, w_out):
    z = lax.axis_index("z")
    c = lax.axis_index("c")
    first = c == 0
    chips = lax.axis_size("z")
    heads = lax.axis_size("h")
    half = hidden_in.shape[0]
    meta = jnp.stack([z, c]).astype(jnp.int32)
    codes = beta_codes.T

    turned = [
        ((i * 2 + k) * heads + j, (j * 2 + k) * heads + i)
        for i in range(chips)
        for k in range(2)
        for j in range(heads)
    ]
    wo = lax.ppermute(w_out, ("z", "c", "h"), turned)
    give, mine = call(
        pack_kernel,
        (meta,),
        (w_qkv, codes),
        [((HD, 4 * HD), BF16), ((HD, 3 * HD), BF16)],
        1 << 20,
    )
    got = swap(give)
    hidden_sib = swap(hidden_in)

    other = got[:, : 3 * HD]
    w_chip = jnp.concatenate(
        [jnp.where(first, mine, other), jnp.where(first, other, mine)], axis=0
    )
    both = jnp.concatenate(
        [to_f16(w_chip, W_SCALE), to_f16(wo, WO_SCALE)], axis=1
    )
    both = lax.all_gather(both, "z", axis=0, tiled=True)
    w_all, wo_all = from_f16(both[:, : 3 * HD], W_SCALE), both[:, 3 * HD :]

    def project(hid):
        return jnp.dot(hid, w_all, preferred_element_type=F32).astype(BF16)

    tl, tl16, b = call(
        local_kernel,
        (meta, doc_starts),
        (project(hidden_in), project(hidden_sib), codes, got),
        [((HD, 2 * HD), F32), ((HD, 2 * HD), BF16), ((2, TOK, HD), F32)],
        3 << 30,
    )
    one = ahead(tl16, 1)
    (two,) = call(pair_kernel, (), (tl, one), [((HD, 2 * HD), BF16)], 1 << 26)
    two = ahead(two, 2)
    wo_all, _ = lax.optimization_barrier((wo_all, one))
    wo_all = wo_all.reshape(chips, 2, HD, HD)
    wo_keep = from_f16(jnp.where(first, wo_all[:, 0], wo_all[:, 1]), WO_SCALE)
    wo_sent = from_f16(jnp.where(first, wo_all[:, 1], wo_all[:, 0]), WO_SCALE)
    wo_got = swap(wo_sent)
    wo_cols = jnp.concatenate(
        [jnp.where(first, wo_keep, wo_got), jnp.where(first, wo_got, wo_keep)], axis=2
    )
    pre, four_t, four_l = call(
        window_kernel,
        (),
        (tl, one, two),
        [((HD, 2 * HD), F32), ((HD, HD), BF16), ((HD, HD), BF16)],
        1 << 26,
    )

    here = jnp.arange(chips, dtype=jnp.int32)[:, None]
    starts = doc_starts[None, :]
    since = jnp.max(jnp.where(starts < here * TOK, starts // TOK, 0), axis=1)
    reach_back = jnp.any(here[:, 0] - since > 7)

    def fetch_far(t, add):
        eight_t, eight_l, twelve = ahead(t, 8), ahead(add, 8), ahead(add, 12)
        state = jnp.dot(eight_t, twelve, preferred_element_type=F32) + eight_l.astype(F32)
        return jnp.dot(ahead(t, 4).astype(F32), state, precision=lax.Precision.HIGHEST)

    extra = lax.cond(
        reach_back, fetch_far, lambda t, add: jnp.zeros((HD, HD), F32), four_t, four_l
    )
    (normed,) = call(
        finish_kernel,
        (meta,),
        (pre, ahead(four_l, 4), extra, b),
        [((TOK, HD), BF16)],
        1 << 28,
    )
    normed_all = lax.all_gather(to_f16(normed, N_SCALE), "h", axis=0)
    def output(rows):
        rows = from_f16(rows, N_SCALE)
        return jnp.einsum("htf,hfn->tn", rows, wo_cols, preferred_element_type=F32)

    sent = swap(output(normed_all[:, :half]))
    return (output(normed_all[:, half:]) + sent).astype(BF16)


def solution(mesh):
    seq, head = mesh.devices.shape
    fine = Mesh(mesh.devices.reshape(seq // 2, 2, head), ("z", "c", "h"))
    tokens = ("z", "c")
    in_specs = (P(tokens, None), P(None, tokens, "h"), P(), P(tokens, "h"), P("h", tokens))
    return jax.shard_map(
        per_device, mesh=fine, in_specs=in_specs, out_specs=P(tokens, "h"), check_vma=False
    )
```

```python
import functools

import jax
import jax.numpy as jnp
from jax import lax
from jax.experimental import pallas as pl
from jax.experimental.pallas import tpu as pltpu
from jax.sharding import Mesh
from jax.sharding import PartitionSpec as P

F32 = jnp.float32
BF16 = jnp.bfloat16
F16 = jnp.float16
HD = 128
VMEM_LIMIT = 12 << 20
TOK_BITS = 9
TOK = 1 << TOK_BITS
W_SCALE = 2.0**19
WO_SCALE = 2.0**18
N_SCALE = 2.0**12
NN = (((1,), (0,)), ((), ()))


def split(a):
    hi = a.astype(BF16)
    return hi, (a - hi.astype(F32)).astype(BF16)


def dot(a, b):
    return lax.dot_general(a, b, NN, preferred_element_type=F32)


def mm3s(a, b):
    (ah, al), (bh, bl) = a, b
    return dot(
        jnp.concatenate([ah, ah, al], axis=1), jnp.concatenate([bh, bl, bh], axis=0)
    )


def mm3(a, b):
    return mm3s(split(a), split(b))


def unit_rows(m):
    return m * lax.rsqrt(jnp.sum(m * m, axis=-1, keepdims=True) + 1e-06)


def count_le(ds_ref, pos):
    total = jnp.zeros(jnp.shape(pos), jnp.int32)
    for j in range(ds_ref.shape[0]):
        total = total + (ds_ref[j] <= pos).astype(jnp.int32)
    return total


def doc_info(meta_ref, ds_ref):
    pos0 = meta_ref[0] * TOK
    doc_col = count_le(ds_ref, pos0 + lax.broadcasted_iota(jnp.int32, (TOK, 1), 0))
    doc_row = count_le(ds_ref, pos0 + lax.broadcasted_iota(jnp.int32, (1, TOK), 1))
    return doc_col, doc_row, count_le(ds_ref, pos0 - 1), count_le(ds_ref, pos0 + TOK - 1)


def in_order(first, own, sib):
    return jnp.concatenate([jnp.where(first, own, sib), jnp.where(first, sib, own)], axis=0)


def part(pair, rows, cols):
    return pair[0][rows, cols], pair[1][rows, cols]


EVERY = slice(None)


def masked_gram(left, right_t, doc_col, doc_row, rows, cols, inclusive=False, scale=None):
    gram = mm3s(part(left, rows, EVERY), part(right_t, EVERY, cols))
    r = lax.broadcasted_iota(jnp.int32, gram.shape, 0) + rows.start
    c = lax.broadcasted_iota(jnp.int32, gram.shape, 1) + cols.start
    keep = (c <= r) if inclusive else (c < r)
    keep = keep & (doc_col[rows] == doc_row[:, cols])
    if scale is not None:
        gram = scale[rows] * gram
    return jnp.where(keep, gram, 0.0)


def pack_kernel(meta_ref, w_ref, codes_ref, give_ref, mine_ref):
    first = meta_ref[1] == 0
    codes = codes_ref[...].astype(F32)
    other = jnp.where(first, codes[1:2], codes[0:1])
    row = lax.broadcasted_iota(jnp.int32, (HD, HD), 0)
    give_ref[:, 3 * HD :] = jnp.where(row == 0, other[:, :HD], other[:, HD:]).astype(BF16)
    for p in range(3):
        cols = slice(HD * p, HD * p + HD)
        left = w_ref[p, :, :HD].astype(F32)
        right = w_ref[p, :, HD:].astype(F32)
        mine_ref[:, cols] = jnp.where(first, left, right).astype(BF16)
        give_ref[:, cols] = jnp.where(first, right, left).astype(BF16)


def far_reach(ds_ref, chips):
    reach = jnp.int32(0)
    for z in range(8, chips):
        since = jnp.int32(0)
        for j in range(ds_ref.shape[0]):
            pos = ds_ref[j]
            since = jnp.where(pos < z * TOK, jnp.maximum(since, pos >> TOK_BITS), since)
        reach = jnp.maximum(reach, (z - since > 7).astype(jnp.int32))
    return reach


def local_kernel(
    chips, meta_ref, ds_ref, own_ref, sib_ref, codes_ref, got_ref, tl_ref, tl16_ref, b_ref, far_ref
):
    far_ref[0] = far_reach(ds_ref, chips)
    first = meta_ref[1] == 0
    half = TOK // 2
    qkv = in_order(first, own_ref[...].astype(F32), sib_ref[...].astype(F32))
    query = unit_rows(qkv[:, :HD])
    key = unit_rows(qkv[:, HD : 2 * HD])
    value = qkv[:, 2 * HD :]
    codes = codes_ref[...].astype(F32)
    own_codes = jnp.where(first, codes[0:1], codes[1:2])
    got = got_ref[0:8, 3 * HD :].astype(F32)
    sib_codes = jnp.concatenate([got[0:1], got[1:2]], axis=1)
    codes = jnp.concatenate(
        [jnp.where(first, own_codes, sib_codes), jnp.where(first, sib_codes, own_codes)], axis=1
    )
    beta = 1.6 + 0.1 * jnp.transpose(jnp.broadcast_to(codes, (8, TOK)))[:, 0:1]
    doc_col, doc_row, prev_doc, last_doc = doc_info(meta_ref, ds_ref)
    carry_in = (doc_col == prev_doc).astype(F32)
    tail_row = (doc_row == last_doc).astype(F32)
    last_keep = (last_doc == prev_doc).astype(F32)

    key_s = split(key)
    key_t = jnp.transpose(key)
    key_ts = split(key_t)

    def system(rows, cols):
        return masked_gram(key_s, key_ts, doc_col, doc_row, rows, cols, scale=beta)

    quarter = [slice(128 * i, 128 * i + 128) for i in range(4)]
    rows128 = lax.broadcasted_iota(jnp.int32, (128, 128), 0)
    cols128 = lax.broadcasted_iota(jnp.int32, (128, 128), 1)
    eye128 = (rows128 == cols128).astype(F32)
    diag = [system(s, s) for s in quarter]
    inv = []
    for a in diag:
        m = ((rows128 >> 1) == (cols128 >> 1)) & (rows128 != cols128)
        inv.append(eye128 - jnp.where(m, a, 0.0))
    for lev in range(1, 7):
        m = ((rows128 >> (lev + 1)) == (cols128 >> (lev + 1))) & (
            (rows128 >> lev) != (cols128 >> lev)
        )
        xs = [split(x) for x in inv]
        ys = [mm3s(x, split(jnp.where(m, a, 0.0))) for x, a in zip(xs, diag)]
        inv = [x - mm3s(split(y), s) for x, y, s in zip(inv, ys, xs)]
    pair_inv = []
    for i in (0, 2):
        off = system(quarter[i + 1], quarter[i])
        low = -mm3(mm3(inv[i + 1], off), inv[i])
        top = jnp.concatenate([inv[i], jnp.zeros((128, 128), F32)], axis=1)
        bottom = jnp.concatenate([low, inv[i + 1]], axis=1)
        pair_inv.append(jnp.concatenate([top, bottom], axis=0))
    lo, hi = slice(0, half), slice(half, TOK)
    right = beta * jnp.concatenate([carry_in * key, value], axis=1)
    cross = system(hi, lo)
    wu_lo = mm3(pair_inv[0], right[lo])
    wu_lo_s = split(wu_lo)
    wu_hi = mm3(pair_inv[1], right[hi] - mm3s(split(cross), wu_lo_s))
    wu_hi_s = split(wu_hi)
    wu_s = tuple(jnp.concatenate([x, y], axis=0) for x, y in zip(wu_lo_s, wu_hi_s))
    tl = mm3s(split(tail_row * key_t), wu_s)
    tl_ref[:, :HD] = last_keep * eye128 - tl[:, :HD]
    tl_ref[:, HD:] = tl[:, HD:]
    tl16_ref[...] = tl_ref[...].astype(BF16)

    query_s = split(query)

    def probs(rows, cols):
        return masked_gram(query_s, key_ts, doc_col, doc_row, rows, cols, inclusive=True)

    out_lo = mm3s(split(probs(lo, lo)), part(wu_s, lo, EVERY))
    out_hi = mm3s(split(probs(hi, slice(0, TOK))), wu_s)
    b_ref[0, lo, :] = carry_in[lo] * query[lo] - out_lo[:, :HD]
    b_ref[0, hi, :] = carry_in[hi] * query[hi] - out_hi[:, :HD]
    b_ref[1, lo, :] = out_lo[:, HD:]
    b_ref[1, hi, :] = out_hi[:, HD:]


def after(later, earlier):
    product = mm3(later[:, :HD], earlier)
    return jnp.concatenate([product[:, :HD], product[:, HD:] + later[:, HD:]], axis=1)


def pair_kernel(tl_ref, one_ref, two_ref):
    two_ref[...] = after(tl_ref[...], one_ref[...].astype(F32)).astype(BF16)


def window_kernel(tl_ref, one_ref, two_ref, pre_ref, four_t_ref, four_l_ref):
    pre = after(one_ref[...].astype(F32), two_ref[...].astype(F32))
    pre_ref[...] = pre
    four = after(tl_ref[...], pre).astype(BF16)
    four_t_ref[...] = four[:, :HD]
    four_l_ref[...] = four[:, HD:]


def finish_kernel(meta_ref, pre_ref, four_ref, extra_ref, b_ref, out_ref):
    first = meta_ref[1] == 0
    half = TOK // 2
    state = four_ref[...].astype(F32) + extra_ref[...]
    state = mm3(pre_ref[:, :HD], state) + pre_ref[:, HD:]
    out = mm3(b_ref[0], state) + b_ref[1]
    out = out * lax.rsqrt(jnp.mean(out * out, axis=-1, keepdims=True) + 1e-05)
    low, high = out[:half], out[half:]
    out_ref[:half, :] = jnp.where(first, high, low).astype(BF16)
    out_ref[half:, :] = jnp.where(first, low, high).astype(BF16)


SMEM = pl.BlockSpec(memory_space=pltpu.SMEM)
VMEM = pl.BlockSpec(memory_space=pltpu.VMEM)


def call(kernel, scalars, arrays, outs, flops):
    return pl.pallas_call(
        kernel,
        out_shape=tuple(jax.ShapeDtypeStruct(s, d) for s, d in outs),
        in_specs=[SMEM] * len(scalars) + [VMEM] * len(arrays),
        out_specs=(VMEM,) * len(outs),
        compiler_params=pltpu.CompilerParams(vmem_limit_bytes=VMEM_LIMIT),
        cost_estimate=pl.CostEstimate(flops=flops, bytes_accessed=1 << 20, transcendentals=0),
    )(*scalars, *arrays)


def swap(value):
    return lax.ppermute(value, "c", [(0, 1), (1, 0)])


def ahead(value, steps):
    chips = lax.axis_size("z")
    return lax.ppermute(value, "z", [(i, i + steps) for i in range(chips - steps)])


def to_f16(value, scale):
    return (value.astype(F32) * scale).astype(F16)


def from_f16(value, scale):
    return (value.astype(F32) * (1.0 / scale)).astype(BF16)


def per_device(hidden_in, w_qkv, doc_starts, beta_codes, w_out):
    z = lax.axis_index("z")
    c = lax.axis_index("c")
    first = c == 0
    chips = lax.axis_size("z")
    heads = lax.axis_size("h")
    half = hidden_in.shape[0]
    meta = jnp.stack([z, c]).astype(jnp.int32)
    codes = beta_codes.T

    turned = [
        ((i * 2 + k) * heads + j, (j * 2 + k) * heads + i)
        for i in range(chips)
        for k in range(2)
        for j in range(heads)
    ]
    wo = lax.ppermute(w_out, ("z", "c", "h"), turned)
    give, mine = call(
        pack_kernel,
        (meta,),
        (w_qkv, codes),
        [((HD, 4 * HD), BF16), ((HD, 3 * HD), BF16)],
        1 << 20,
    )
    got = swap(give)
    hidden_sib = swap(hidden_in)

    other = got[:, : 3 * HD]
    w_chip = jnp.concatenate(
        [jnp.where(first, mine, other), jnp.where(first, other, mine)], axis=0
    )
    both = jnp.concatenate(
        [to_f16(w_chip, W_SCALE), to_f16(wo, WO_SCALE)], axis=1
    )
    both = lax.all_gather(both, "z", axis=0, tiled=True)
    w_all, wo_all = from_f16(both[:, : 3 * HD], W_SCALE), both[:, 3 * HD :]

    def project(hid):
        return jnp.dot(hid, w_all, preferred_element_type=F32).astype(BF16)

    tl, tl16, b, far = pl.pallas_call(
        functools.partial(local_kernel, chips),
        out_shape=(
            jax.ShapeDtypeStruct((HD, 2 * HD), F32),
            jax.ShapeDtypeStruct((HD, 2 * HD), BF16),
            jax.ShapeDtypeStruct((2, TOK, HD), F32),
            jax.ShapeDtypeStruct((1,), jnp.int32),
        ),
        in_specs=[SMEM, SMEM, VMEM, VMEM, VMEM, VMEM],
        out_specs=(VMEM, VMEM, VMEM, SMEM),
        compiler_params=pltpu.CompilerParams(vmem_limit_bytes=VMEM_LIMIT),
        cost_estimate=pl.CostEstimate(flops=3 << 30, bytes_accessed=1 << 20, transcendentals=0),
    )(meta, doc_starts, project(hidden_in), project(hidden_sib), codes, got)
    one = ahead(tl16, 1)
    (two,) = call(pair_kernel, (), (tl, one), [((HD, 2 * HD), BF16)], 1 << 26)
    two = ahead(two, 2)
    wo_all, _ = lax.optimization_barrier((wo_all, one))
    wo_all = wo_all.reshape(chips, 2, HD, HD)
    wo_keep = from_f16(jnp.where(first, wo_all[:, 0], wo_all[:, 1]), WO_SCALE)
    wo_sent = from_f16(jnp.where(first, wo_all[:, 1], wo_all[:, 0]), WO_SCALE)
    wo_got = swap(wo_sent)
    wo_cols = jnp.concatenate(
        [jnp.where(first, wo_keep, wo_got), jnp.where(first, wo_got, wo_keep)], axis=2
    )
    pre, four_t, four_l = call(
        window_kernel,
        (),
        (tl, one, two),
        [((HD, 2 * HD), F32), ((HD, HD), BF16), ((HD, HD), BF16)],
        1 << 26,
    )

    def fetch_far(t, add):
        eight_t, eight_l, twelve = ahead(t, 8), ahead(add, 8), ahead(add, 12)
        state = jnp.dot(eight_t, twelve, preferred_element_type=F32) + eight_l.astype(F32)
        return jnp.dot(ahead(t, 4).astype(F32), state, precision=lax.Precision.HIGHEST)

    extra = lax.cond(
        far[0] > 0, fetch_far, lambda t, add: jnp.zeros((HD, HD), F32), four_t, four_l
    )
    (normed,) = call(
        finish_kernel,
        (meta,),
        (pre, ahead(four_l, 4), extra, b),
        [((TOK, HD), BF16)],
        1 << 28,
    )
    normed_all = lax.all_gather(to_f16(normed, N_SCALE), "h", axis=0)
    def output(rows):
        rows = from_f16(rows, N_SCALE)
        return jnp.einsum("htf,hfn->tn", rows, wo_cols, preferred_element_type=F32)

    sent = swap(output(normed_all[:, :half]))
    return (output(normed_all[:, half:]) + sent).astype(BF16)


def solution(mesh):
    seq, head = mesh.devices.shape
    fine = Mesh(mesh.devices.reshape(seq // 2, 2, head), ("z", "c", "h"))
    tokens = ("z", "c")
    in_specs = (P(tokens, None), P(None, tokens, "h"), P(), P(tokens, "h"), P("h", tokens))
    return jax.shard_map(
        per_device, mesh=fine, in_specs=in_specs, out_specs=P(tokens, "h"), check_vma=False
    )
```

```python
import functools

import jax
import jax.numpy as jnp
from jax import lax
from jax.experimental import pallas as pl
from jax.experimental.pallas import tpu as pltpu
from jax.sharding import Mesh
from jax.sharding import PartitionSpec as P

F32 = jnp.float32
BF16 = jnp.bfloat16
F16 = jnp.float16
HD = 128
VMEM_LIMIT = 12 << 20
TOK_BITS = 9
TOK = 1 << TOK_BITS
W_SCALE = 2.0**19
WO_SCALE = 2.0**18
N_SCALE = 2.0**12
NN = (((1,), (0,)), ((), ()))


def split(a):
    hi = a.astype(BF16)
    return hi, (a - hi.astype(F32)).astype(BF16)


def dot(a, b):
    return lax.dot_general(a, b, NN, preferred_element_type=F32)


def mm3s(a, b):
    (ah, al), (bh, bl) = a, b
    return dot(
        jnp.concatenate([ah, ah, al], axis=1), jnp.concatenate([bh, bl, bh], axis=0)
    )


def mm3(a, b):
    return mm3s(split(a), split(b))


def unit_rows(m):
    return m * lax.rsqrt(jnp.sum(m * m, axis=-1, keepdims=True) + 1e-06)


def count_le(ds_ref, pos):
    total = jnp.zeros(jnp.shape(pos), jnp.int32)
    for j in range(ds_ref.shape[0]):
        total = total + (ds_ref[j] <= pos).astype(jnp.int32)
    return total


def doc_info(meta_ref, ds_ref):
    pos0 = meta_ref[0] * TOK
    doc_col = count_le(ds_ref, pos0 + lax.broadcasted_iota(jnp.int32, (TOK, 1), 0))
    doc_row = count_le(ds_ref, pos0 + lax.broadcasted_iota(jnp.int32, (1, TOK), 1))
    return doc_col, doc_row, count_le(ds_ref, pos0 - 1), count_le(ds_ref, pos0 + TOK - 1)


def in_order(first, own, sib):
    return jnp.concatenate([jnp.where(first, own, sib), jnp.where(first, sib, own)], axis=0)


def part(pair, rows, cols):
    return pair[0][rows, cols], pair[1][rows, cols]


EVERY = slice(None)


def masked_gram(left, right_t, doc_col, doc_row, rows, cols, inclusive=False, scale=None):
    gram = mm3s(part(left, rows, EVERY), part(right_t, EVERY, cols))
    r = lax.broadcasted_iota(jnp.int32, gram.shape, 0) + rows.start
    c = lax.broadcasted_iota(jnp.int32, gram.shape, 1) + cols.start
    keep = (c <= r) if inclusive else (c < r)
    keep = keep & (doc_col[rows] == doc_row[:, cols])
    if scale is not None:
        gram = scale[rows] * gram
    return jnp.where(keep, gram, 0.0)


def pack_kernel(meta_ref, w_ref, codes_ref, give_ref, mine_ref):
    first = meta_ref[1] == 0
    codes = codes_ref[...].astype(F32)
    other = jnp.where(first, codes[1:2], codes[0:1])
    row = lax.broadcasted_iota(jnp.int32, (HD, HD), 0)
    give_ref[:, 3 * HD :] = jnp.where(row == 0, other[:, :HD], other[:, HD:]).astype(BF16)
    for p in range(3):
        cols = slice(HD * p, HD * p + HD)
        left = w_ref[p, :, :HD].astype(F32)
        right = w_ref[p, :, HD:].astype(F32)
        mine_ref[:, cols] = jnp.where(first, left, right).astype(BF16)
        give_ref[:, cols] = jnp.where(first, right, left).astype(BF16)


def far_reach(ds_ref, chips):
    count = ds_ref.shape[0]
    blocks = [ds_ref[j] >> TOK_BITS for j in range(count)]
    gap = chips - 1 - blocks[count - 1]
    for j in range(count - 1):
        gap = jnp.maximum(gap, blocks[j + 1] - blocks[j])
    return (gap > 7).astype(jnp.int32)


def local_kernel(
    chips, meta_ref, ds_ref, own_ref, sib_ref, codes_ref, got_ref, tl_ref, tl16_ref, b_ref, far_ref
):
    far_ref[0] = far_reach(ds_ref, chips)
    first = meta_ref[1] == 0
    half = TOK // 2
    qkv = in_order(first, own_ref[...].astype(F32), sib_ref[...].astype(F32))
    query = unit_rows(qkv[:, :HD])
    key = unit_rows(qkv[:, HD : 2 * HD])
    value = qkv[:, 2 * HD :]
    codes = codes_ref[...].astype(F32)
    own_codes = jnp.where(first, codes[0:1], codes[1:2])
    got = got_ref[0:8, 3 * HD :].astype(F32)
    sib_codes = jnp.concatenate([got[0:1], got[1:2]], axis=1)
    codes = jnp.concatenate(
        [jnp.where(first, own_codes, sib_codes), jnp.where(first, sib_codes, own_codes)], axis=1
    )
    beta = 1.6 + 0.1 * jnp.transpose(jnp.broadcast_to(codes, (8, TOK)))[:, 0:1]
    doc_col, doc_row, prev_doc, last_doc = doc_info(meta_ref, ds_ref)
    carry_in = (doc_col == prev_doc).astype(F32)
    tail_row = (doc_row == last_doc).astype(F32)
    last_keep = (last_doc == prev_doc).astype(F32)

    key_s = split(key)
    key_t = jnp.transpose(key)
    key_ts = split(key_t)

    def system(rows, cols):
        return masked_gram(key_s, key_ts, doc_col, doc_row, rows, cols, scale=beta)

    quarter = [slice(128 * i, 128 * i + 128) for i in range(4)]
    rows128 = lax.broadcasted_iota(jnp.int32, (128, 128), 0)
    cols128 = lax.broadcasted_iota(jnp.int32, (128, 128), 1)
    eye128 = (rows128 == cols128).astype(F32)
    diag = [system(s, s) for s in quarter]
    inv = []
    for a in diag:
        m = ((rows128 >> 1) == (cols128 >> 1)) & (rows128 != cols128)
        inv.append(eye128 - jnp.where(m, a, 0.0))
    for lev in range(1, 7):
        m = ((rows128 >> (lev + 1)) == (cols128 >> (lev + 1))) & (
            (rows128 >> lev) != (cols128 >> lev)
        )
        xs = [split(x) for x in inv]
        ys = [mm3s(x, split(jnp.where(m, a, 0.0))) for x, a in zip(xs, diag)]
        inv = [x - mm3s(split(y), s) for x, y, s in zip(inv, ys, xs)]
    pair_inv = []
    for i in (0, 2):
        off = system(quarter[i + 1], quarter[i])
        low = -mm3(mm3(inv[i + 1], off), inv[i])
        top = jnp.concatenate([inv[i], jnp.zeros((128, 128), F32)], axis=1)
        bottom = jnp.concatenate([low, inv[i + 1]], axis=1)
        pair_inv.append(jnp.concatenate([top, bottom], axis=0))
    lo, hi = slice(0, half), slice(half, TOK)
    right = beta * jnp.concatenate([carry_in * key, value], axis=1)
    cross = system(hi, lo)
    wu_lo = mm3(pair_inv[0], right[lo])
    wu_lo_s = split(wu_lo)
    wu_hi = mm3(pair_inv[1], right[hi] - mm3s(split(cross), wu_lo_s))
    wu_hi_s = split(wu_hi)
    wu_s = tuple(jnp.concatenate([x, y], axis=0) for x, y in zip(wu_lo_s, wu_hi_s))
    tl = mm3s(split(tail_row * key_t), wu_s)
    tl_ref[:, :HD] = last_keep * eye128 - tl[:, :HD]
    tl_ref[:, HD:] = tl[:, HD:]
    tl16_ref[...] = tl_ref[...].astype(BF16)

    query_s = split(query)

    def probs(rows, cols):
        return masked_gram(query_s, key_ts, doc_col, doc_row, rows, cols, inclusive=True)

    out_lo = mm3s(split(probs(lo, lo)), part(wu_s, lo, EVERY))
    out_hi = mm3s(split(probs(hi, slice(0, TOK))), wu_s)
    b_ref[0, lo, :] = carry_in[lo] * query[lo] - out_lo[:, :HD]
    b_ref[0, hi, :] = carry_in[hi] * query[hi] - out_hi[:, :HD]
    b_ref[1, lo, :] = out_lo[:, HD:]
    b_ref[1, hi, :] = out_hi[:, HD:]


def after(later, earlier):
    product = mm3(later[:, :HD], earlier)
    return jnp.concatenate([product[:, :HD], product[:, HD:] + later[:, HD:]], axis=1)


def pair_kernel(tl_ref, one_ref, two_ref):
    two_ref[...] = after(tl_ref[...], one_ref[...].astype(F32)).astype(BF16)


def window_kernel(tl_ref, one_ref, two_ref, pre_ref, four_t_ref, four_l_ref):
    pre = after(one_ref[...].astype(F32), two_ref[...].astype(F32))
    pre_ref[...] = pre
    four = after(tl_ref[...], pre).astype(BF16)
    four_t_ref[...] = four[:, :HD]
    four_l_ref[...] = four[:, HD:]


def finish_kernel(meta_ref, pre_ref, four_ref, extra_ref, b_ref, out_ref):
    first = meta_ref[1] == 0
    half = TOK // 2
    state = four_ref[...].astype(F32) + extra_ref[...]
    state = mm3(pre_ref[:, :HD], state) + pre_ref[:, HD:]
    out = mm3(b_ref[0], state) + b_ref[1]
    out = out * lax.rsqrt(jnp.mean(out * out, axis=-1, keepdims=True) + 1e-05)
    low, high = out[:half], out[half:]
    out_ref[:half, :] = jnp.where(first, high, low).astype(BF16)
    out_ref[half:, :] = jnp.where(first, low, high).astype(BF16)


SMEM = pl.BlockSpec(memory_space=pltpu.SMEM)
VMEM = pl.BlockSpec(memory_space=pltpu.VMEM)


def call(kernel, scalars, arrays, outs, flops):
    return pl.pallas_call(
        kernel,
        out_shape=tuple(jax.ShapeDtypeStruct(s, d) for s, d in outs),
        in_specs=[SMEM] * len(scalars) + [VMEM] * len(arrays),
        out_specs=(VMEM,) * len(outs),
        compiler_params=pltpu.CompilerParams(vmem_limit_bytes=VMEM_LIMIT),
        cost_estimate=pl.CostEstimate(flops=flops, bytes_accessed=1 << 20, transcendentals=0),
    )(*scalars, *arrays)


def swap(value):
    return lax.ppermute(value, "c", [(0, 1), (1, 0)])


def ahead(value, steps):
    chips = lax.axis_size("z")
    return lax.ppermute(value, "z", [(i, i + steps) for i in range(chips - steps)])


def to_f16(value, scale):
    return (value.astype(F32) * scale).astype(F16)


def from_f16(value, scale):
    return (value.astype(F32) * (1.0 / scale)).astype(BF16)


def per_device(hidden_in, w_qkv, doc_starts, beta_codes, w_out):
    z = lax.axis_index("z")
    c = lax.axis_index("c")
    first = c == 0
    chips = lax.axis_size("z")
    heads = lax.axis_size("h")
    half = hidden_in.shape[0]
    meta = jnp.stack([z, c]).astype(jnp.int32)
    codes = beta_codes.T

    turned = [
        ((i * 2 + k) * heads + j, (j * 2 + k) * heads + i)
        for i in range(chips)
        for k in range(2)
        for j in range(heads)
    ]
    wo = lax.ppermute(w_out, ("z", "c", "h"), turned)
    give, mine = call(
        pack_kernel,
        (meta,),
        (w_qkv, codes),
        [((HD, 4 * HD), BF16), ((HD, 3 * HD), BF16)],
        1 << 20,
    )
    got = swap(give)
    hidden_sib = swap(hidden_in)

    other = got[:, : 3 * HD]
    w_chip = jnp.concatenate(
        [jnp.where(first, mine, other), jnp.where(first, other, mine)], axis=0
    )
    both = jnp.concatenate(
        [to_f16(w_chip, W_SCALE), to_f16(wo, WO_SCALE)], axis=1
    )
    both = lax.all_gather(both, "z", axis=0, tiled=True)
    w_all, wo_all = from_f16(both[:, : 3 * HD], W_SCALE), both[:, 3 * HD :]

    def project(hid):
        return jnp.dot(hid, w_all, preferred_element_type=F32).astype(BF16)

    tl, tl16, b, far = pl.pallas_call(
        functools.partial(local_kernel, chips),
        out_shape=(
            jax.ShapeDtypeStruct((HD, 2 * HD), F32),
            jax.ShapeDtypeStruct((HD, 2 * HD), BF16),
            jax.ShapeDtypeStruct((2, TOK, HD), F32),
            jax.ShapeDtypeStruct((1,), jnp.int32),
        ),
        in_specs=[SMEM, SMEM, VMEM, VMEM, VMEM, VMEM],
        out_specs=(VMEM, VMEM, VMEM, SMEM),
        compiler_params=pltpu.CompilerParams(vmem_limit_bytes=VMEM_LIMIT),
        cost_estimate=pl.CostEstimate(flops=3 << 30, bytes_accessed=1 << 20, transcendentals=0),
    )(meta, doc_starts, project(hidden_in), project(hidden_sib), codes, got)
    one = ahead(tl16, 1)
    (two,) = call(pair_kernel, (), (tl, one), [((HD, 2 * HD), BF16)], 1 << 26)
    two = ahead(two, 2)
    wo_all, _ = lax.optimization_barrier((wo_all, tl16))
    wo_all = wo_all.reshape(chips, 2, HD, HD)
    wo_keep = from_f16(jnp.where(first, wo_all[:, 0], wo_all[:, 1]), WO_SCALE)
    wo_sent = from_f16(jnp.where(first, wo_all[:, 1], wo_all[:, 0]), WO_SCALE)
    wo_got = swap(wo_sent)
    wo_cols = jnp.concatenate(
        [jnp.where(first, wo_keep, wo_got), jnp.where(first, wo_got, wo_keep)], axis=2
    )
    pre, four_t, four_l = call(
        window_kernel,
        (),
        (tl, one, two),
        [((HD, 2 * HD), F32), ((HD, HD), BF16), ((HD, HD), BF16)],
        1 << 26,
    )

    def fetch_far(t, add):
        eight_t, eight_l, twelve = ahead(t, 8), ahead(add, 8), ahead(add, 12)
        state = jnp.dot(eight_t, twelve, preferred_element_type=F32) + eight_l.astype(F32)
        return jnp.dot(ahead(t, 4).astype(F32), state, precision=lax.Precision.HIGHEST)

    extra = lax.cond(
        far[0] > 0, fetch_far, lambda t, add: jnp.zeros((HD, HD), F32), four_t, four_l
    )
    (normed,) = call(
        finish_kernel,
        (meta,),
        (pre, ahead(four_l, 4), extra, b),
        [((TOK, HD), BF16)],
        1 << 28,
    )
    normed_all = lax.all_gather(to_f16(normed, N_SCALE), "h", axis=0)
    def output(rows):
        rows = from_f16(rows, N_SCALE)
        return jnp.einsum("htf,hfn->tn", rows, wo_cols, preferred_element_type=F32)

    sent = swap(output(normed_all[:, :half]))
    kept = lax.optimization_barrier(output(normed_all[:, half:]))
    return (kept + sent).astype(BF16)


def solution(mesh):
    seq, head = mesh.devices.shape
    fine = Mesh(mesh.devices.reshape(seq // 2, 2, head), ("z", "c", "h"))
    tokens = ("z", "c")
    in_specs = (P(tokens, None), P(None, tokens, "h"), P(), P(tokens, "h"), P("h", tokens))
    return jax.shard_map(
        per_device, mesh=fine, in_specs=in_specs, out_specs=P(tokens, "h"), check_vma=False
    )
```

```python
import functools

import jax
import jax.numpy as jnp
from jax import lax
from jax.experimental import pallas as pl
from jax.experimental.pallas import tpu as pltpu
from jax.sharding import Mesh
from jax.sharding import PartitionSpec as P

F32 = jnp.float32
BF16 = jnp.bfloat16
F16 = jnp.float16
HD = 128
VMEM_LIMIT = 12 << 20
TOK_BITS = 9
TOK = 1 << TOK_BITS
W_SCALE = 2.0**19
WO_SCALE = 2.0**18
N_SCALE = 2.0**12
NN = (((1,), (0,)), ((), ()))


def split(a):
    hi = a.astype(BF16)
    return hi, (a - hi.astype(F32)).astype(BF16)


def dot(a, b):
    return lax.dot_general(a, b, NN, preferred_element_type=F32)


def mm3s(a, b):
    (ah, al), (bh, bl) = a, b
    return dot(
        jnp.concatenate([ah, ah, al], axis=1), jnp.concatenate([bh, bl, bh], axis=0)
    )


def mm3(a, b):
    return mm3s(split(a), split(b))


def unit_rows(m):
    return m * lax.rsqrt(jnp.sum(m * m, axis=-1, keepdims=True) + 1e-06)


def count_le(ds_ref, pos):
    total = jnp.zeros(jnp.shape(pos), jnp.int32)
    for j in range(ds_ref.shape[0]):
        total = total + (ds_ref[j] <= pos).astype(jnp.int32)
    return total


def doc_info(meta_ref, ds_ref):
    pos0 = meta_ref[0] * TOK
    doc_col = count_le(ds_ref, pos0 + lax.broadcasted_iota(jnp.int32, (TOK, 1), 0))
    doc_row = count_le(ds_ref, pos0 + lax.broadcasted_iota(jnp.int32, (1, TOK), 1))
    return doc_col, doc_row, count_le(ds_ref, pos0 - 1), count_le(ds_ref, pos0 + TOK - 1)


def in_order(first, own, sib):
    return jnp.concatenate([jnp.where(first, own, sib), jnp.where(first, sib, own)], axis=0)


def part(pair, rows, cols):
    return pair[0][rows, cols], pair[1][rows, cols]


EVERY = slice(None)


def masked_gram(left, right_t, doc_col, doc_row, rows, cols, inclusive=False, scale=None):
    gram = mm3s(part(left, rows, EVERY), part(right_t, EVERY, cols))
    r = lax.broadcasted_iota(jnp.int32, gram.shape, 0) + rows.start
    c = lax.broadcasted_iota(jnp.int32, gram.shape, 1) + cols.start
    keep = (c <= r) if inclusive else (c < r)
    keep = keep & (doc_col[rows] == doc_row[:, cols])
    if scale is not None:
        gram = scale[rows] * gram
    return jnp.where(keep, gram, 0.0)


def pack_kernel(meta_ref, w_ref, codes_ref, give_ref, mine_ref):
    first = meta_ref[1] == 0
    codes = codes_ref[...].astype(F32)
    other = jnp.where(first, codes[1:2], codes[0:1])
    row = lax.broadcasted_iota(jnp.int32, (HD, HD), 0)
    give_ref[:, 3 * HD :] = jnp.where(row == 0, other[:, :HD], other[:, HD:]).astype(BF16)
    for p in range(3):
        cols = slice(HD * p, HD * p + HD)
        left = w_ref[p, :, :HD].astype(F32)
        right = w_ref[p, :, HD:].astype(F32)
        mine_ref[:, cols] = jnp.where(first, left, right).astype(BF16)
        give_ref[:, cols] = jnp.where(first, right, left).astype(BF16)


def far_reach(ds_ref, chips):
    count = ds_ref.shape[0]
    blocks = [ds_ref[j] >> TOK_BITS for j in range(count)]
    gap = chips - 1 - blocks[count - 1]
    for j in range(count - 1):
        gap = jnp.maximum(gap, blocks[j + 1] - blocks[j])
    return (gap > 7).astype(jnp.int32)


def local_kernel(
    chips,
    meta_ref,
    ds_ref,
    own_ref,
    sib_ref,
    codes_ref,
    got_ref,
    tl_ref,
    tl16_ref,
    wu_ref,
    kt_ref,
    far_ref,
):
    far_ref[0] = far_reach(ds_ref, chips)
    first = meta_ref[1] == 0
    half = TOK // 2
    qkv = in_order(first, own_ref[...].astype(F32), sib_ref[...].astype(F32))
    key = unit_rows(qkv[:, HD : 2 * HD])
    value = qkv[:, 2 * HD :]
    codes = codes_ref[...].astype(F32)
    own_codes = jnp.where(first, codes[0:1], codes[1:2])
    got = got_ref[0:8, 3 * HD :].astype(F32)
    sib_codes = jnp.concatenate([got[0:1], got[1:2]], axis=1)
    codes = jnp.concatenate(
        [jnp.where(first, own_codes, sib_codes), jnp.where(first, sib_codes, own_codes)], axis=1
    )
    beta = 1.6 + 0.1 * jnp.transpose(jnp.broadcast_to(codes, (8, TOK)))[:, 0:1]
    doc_col, doc_row, prev_doc, last_doc = doc_info(meta_ref, ds_ref)
    carry_in = (doc_col == prev_doc).astype(F32)
    tail_row = (doc_row == last_doc).astype(F32)
    last_keep = (last_doc == prev_doc).astype(F32)

    key_s = split(key)
    key_t = jnp.transpose(key)
    kt_ref[...] = key_t
    key_ts = split(key_t)

    def system(rows, cols):
        return masked_gram(key_s, key_ts, doc_col, doc_row, rows, cols, scale=beta)

    quarter = [slice(128 * i, 128 * i + 128) for i in range(4)]
    rows128 = lax.broadcasted_iota(jnp.int32, (128, 128), 0)
    cols128 = lax.broadcasted_iota(jnp.int32, (128, 128), 1)
    eye128 = (rows128 == cols128).astype(F32)
    diag = [system(s, s) for s in quarter]
    inv = []
    for a in diag:
        m = ((rows128 >> 1) == (cols128 >> 1)) & (rows128 != cols128)
        inv.append(eye128 - jnp.where(m, a, 0.0))
    for lev in range(1, 7):
        m = ((rows128 >> (lev + 1)) == (cols128 >> (lev + 1))) & (
            (rows128 >> lev) != (cols128 >> lev)
        )
        xs = [split(x) for x in inv]
        ys = [mm3s(x, split(jnp.where(m, a, 0.0))) for x, a in zip(xs, diag)]
        inv = [x - mm3s(split(y), s) for x, y, s in zip(inv, ys, xs)]
    pair_inv = []
    for i in (0, 2):
        off = system(quarter[i + 1], quarter[i])
        low = -mm3(mm3(inv[i + 1], off), inv[i])
        top = jnp.concatenate([inv[i], jnp.zeros((128, 128), F32)], axis=1)
        bottom = jnp.concatenate([low, inv[i + 1]], axis=1)
        pair_inv.append(jnp.concatenate([top, bottom], axis=0))
    lo, hi = slice(0, half), slice(half, TOK)
    right = beta * jnp.concatenate([carry_in * key, value], axis=1)
    cross = system(hi, lo)
    wu_lo = mm3(pair_inv[0], right[lo])
    wu_lo_s = split(wu_lo)
    wu_hi = mm3(pair_inv[1], right[hi] - mm3s(split(cross), wu_lo_s))
    wu_hi_s = split(wu_hi)
    wu_s = tuple(jnp.concatenate([x, y], axis=0) for x, y in zip(wu_lo_s, wu_hi_s))
    tl = mm3s(split(tail_row * key_t), wu_s)
    tl_ref[:, :HD] = last_keep * eye128 - tl[:, :HD]
    tl_ref[:, HD:] = tl[:, HD:]
    tl16_ref[...] = tl_ref[...].astype(BF16)
    wu_ref[lo, :] = wu_lo
    wu_ref[hi, :] = wu_hi


def query_kernel(meta_ref, ds_ref, own_ref, sib_ref, kt_ref, wu_ref, b_ref):
    first = meta_ref[1] == 0
    half = TOK // 2
    query = unit_rows(in_order(first, own_ref[:, :HD].astype(F32), sib_ref[:, :HD].astype(F32)))
    doc_col, doc_row, prev_doc, _ = doc_info(meta_ref, ds_ref)
    carry_in = (doc_col == prev_doc).astype(F32)
    query_s = split(query)
    key_ts = split(kt_ref[...])
    wu_s = split(wu_ref[...])
    lo, hi = slice(0, half), slice(half, TOK)

    def probs(rows, cols):
        return masked_gram(query_s, key_ts, doc_col, doc_row, rows, cols, inclusive=True)

    out_lo = mm3s(split(probs(lo, lo)), part(wu_s, lo, EVERY))
    out_hi = mm3s(split(probs(hi, slice(0, TOK))), wu_s)
    b_ref[0, lo, :] = carry_in[lo] * query[lo] - out_lo[:, :HD]
    b_ref[0, hi, :] = carry_in[hi] * query[hi] - out_hi[:, :HD]
    b_ref[1, lo, :] = out_lo[:, HD:]
    b_ref[1, hi, :] = out_hi[:, HD:]


def after(later, earlier):
    product = mm3(later[:, :HD], earlier)
    return jnp.concatenate([product[:, :HD], product[:, HD:] + later[:, HD:]], axis=1)


def pair_kernel(tl_ref, one_ref, two_ref):
    later = tl_ref[...]
    hi, lo = split(later[:, :HD])
    one = one_ref[...]
    product = dot(jnp.concatenate([hi, lo], axis=1), jnp.concatenate([one, one], axis=0))
    two_ref[:, :HD] = product[:, :HD].astype(BF16)
    two_ref[:, HD:] = (product[:, HD:] + later[:, HD:]).astype(BF16)


def window_kernel(tl_ref, one_ref, two_ref, pre_ref, four_t_ref, four_l_ref):
    product = dot(one_ref[:, :HD], two_ref[...])
    pre = jnp.concatenate([product[:, :HD], product[:, HD:] + one_ref[:, HD:].astype(F32)], axis=1)
    pre_ref[...] = pre
    four = after(tl_ref[...], pre).astype(BF16)
    four_t_ref[...] = four[:, :HD]
    four_l_ref[...] = four[:, HD:]


def finish_kernel(meta_ref, pre_ref, four_ref, extra_ref, b_ref, out_ref):
    first = meta_ref[1] == 0
    half = TOK // 2
    state = four_ref[...].astype(F32) + extra_ref[...]
    state = mm3(pre_ref[:, :HD], state) + pre_ref[:, HD:]
    out = mm3(b_ref[0], state) + b_ref[1]
    out = out * lax.rsqrt(jnp.mean(out * out, axis=-1, keepdims=True) + 1e-05)
    low, high = out[:half], out[half:]
    out_ref[:half, :] = jnp.where(first, high, low).astype(BF16)
    out_ref[half:, :] = jnp.where(first, low, high).astype(BF16)


SMEM = pl.BlockSpec(memory_space=pltpu.SMEM)
VMEM = pl.BlockSpec(memory_space=pltpu.VMEM)


def call(kernel, scalars, arrays, outs, flops):
    return pl.pallas_call(
        kernel,
        out_shape=tuple(jax.ShapeDtypeStruct(s, d) for s, d in outs),
        in_specs=[SMEM] * len(scalars) + [VMEM] * len(arrays),
        out_specs=(VMEM,) * len(outs),
        compiler_params=pltpu.CompilerParams(vmem_limit_bytes=VMEM_LIMIT),
        cost_estimate=pl.CostEstimate(flops=flops, bytes_accessed=1 << 20, transcendentals=0),
    )(*scalars, *arrays)


def swap(value):
    return lax.ppermute(value, "c", [(0, 1), (1, 0)])


def ahead(value, steps):
    chips = lax.axis_size("z")
    return lax.ppermute(value, "z", [(i, i + steps) for i in range(chips - steps)])


def to_f16(value, scale):
    return (value.astype(F32) * scale).astype(F16)


def from_f16(value, scale):
    return (value.astype(F32) * (1.0 / scale)).astype(BF16)


def per_device(hidden_in, w_qkv, doc_starts, beta_codes, w_out):
    z = lax.axis_index("z")
    c = lax.axis_index("c")
    first = c == 0
    chips = lax.axis_size("z")
    heads = lax.axis_size("h")
    half = hidden_in.shape[0]
    meta = jnp.stack([z, c]).astype(jnp.int32)
    codes = beta_codes.T

    turned = [
        ((i * 2 + k) * heads + j, (j * 2 + k) * heads + i)
        for i in range(chips)
        for k in range(2)
        for j in range(heads)
    ]
    wo = lax.ppermute(w_out, ("z", "c", "h"), turned)
    give, mine = call(
        pack_kernel,
        (meta,),
        (w_qkv, codes),
        [((HD, 4 * HD), BF16), ((HD, 3 * HD), BF16)],
        1 << 20,
    )
    got = swap(give)
    hidden_sib = swap(hidden_in)

    other = got[:, : 3 * HD]
    w_chip = jnp.concatenate(
        [jnp.where(first, mine, other), jnp.where(first, other, mine)], axis=0
    )
    both = jnp.concatenate(
        [to_f16(w_chip, W_SCALE), to_f16(wo, WO_SCALE)], axis=1
    )
    both = lax.all_gather(both, "z", axis=0, tiled=True)
    w_all, wo_all = from_f16(both[:, : 3 * HD], W_SCALE), both[:, 3 * HD :]

    def project(hid):
        return jnp.dot(hid, w_all, preferred_element_type=F32).astype(BF16)

    own, sib = project(hidden_in), project(hidden_sib)
    tl, tl16, wu, key_t, far = pl.pallas_call(
        functools.partial(local_kernel, chips),
        out_shape=(
            jax.ShapeDtypeStruct((HD, 2 * HD), F32),
            jax.ShapeDtypeStruct((HD, 2 * HD), BF16),
            jax.ShapeDtypeStruct((TOK, 2 * HD), F32),
            jax.ShapeDtypeStruct((HD, TOK), F32),
            jax.ShapeDtypeStruct((1,), jnp.int32),
        ),
        in_specs=[SMEM, SMEM, VMEM, VMEM, VMEM, VMEM],
        out_specs=(VMEM, VMEM, VMEM, VMEM, SMEM),
        compiler_params=pltpu.CompilerParams(vmem_limit_bytes=VMEM_LIMIT),
        cost_estimate=pl.CostEstimate(flops=3 << 30, bytes_accessed=1 << 20, transcendentals=0),
    )(meta, doc_starts, own, sib, codes, got)
    (b,) = call(
        query_kernel,
        (meta, doc_starts),
        (own, sib, key_t, wu),
        [((2, TOK, HD), F32)],
        1 << 30,
    )
    one = ahead(tl16, 1)
    (two,) = call(pair_kernel, (), (tl, one), [((HD, 2 * HD), BF16)], 1 << 26)
    two = ahead(two, 2)
    wo_all, _ = lax.optimization_barrier((wo_all, tl16))
    wo_all = wo_all.reshape(chips, 2, HD, HD)
    wo_keep = from_f16(jnp.where(first, wo_all[:, 0], wo_all[:, 1]), WO_SCALE)
    wo_sent = from_f16(jnp.where(first, wo_all[:, 1], wo_all[:, 0]), WO_SCALE)
    wo_got = swap(wo_sent)
    wo_cols = jnp.concatenate(
        [jnp.where(first, wo_keep, wo_got), jnp.where(first, wo_got, wo_keep)], axis=2
    )
    pre, four_t, four_l = call(
        window_kernel,
        (),
        (tl, one, two),
        [((HD, 2 * HD), F32), ((HD, HD), BF16), ((HD, HD), BF16)],
        1 << 26,
    )

    def fetch_far(t, add):
        eight_t, eight_l, twelve = ahead(t, 8), ahead(add, 8), ahead(add, 12)
        state = jnp.dot(eight_t, twelve, preferred_element_type=F32) + eight_l.astype(F32)
        return jnp.dot(ahead(t, 4).astype(F32), state, precision=lax.Precision.HIGHEST)

    extra = lax.cond(
        far[0] > 0, fetch_far, lambda t, add: jnp.zeros((HD, HD), F32), four_t, four_l
    )
    (normed,) = call(
        finish_kernel,
        (meta,),
        (pre, ahead(four_l, 4), extra, b),
        [((TOK, HD), BF16)],
        1 << 28,
    )
    normed_all = lax.all_gather(to_f16(normed, N_SCALE), "h", axis=0)
    def output(rows):
        rows = from_f16(rows, N_SCALE)
        return jnp.einsum("htf,hfn->tn", rows, wo_cols, preferred_element_type=F32)

    sent = swap(output(normed_all[:, :half]))
    kept = lax.optimization_barrier(output(normed_all[:, half:]))
    return (kept + sent).astype(BF16)


def solution(mesh):
    seq, head = mesh.devices.shape
    fine = Mesh(mesh.devices.reshape(seq // 2, 2, head), ("z", "c", "h"))
    tokens = ("z", "c")
    in_specs = (P(tokens, None), P(None, tokens, "h"), P(), P(tokens, "h"), P("h", tokens))
    return jax.shard_map(
        per_device, mesh=fine, in_specs=in_specs, out_specs=P(tokens, "h"), check_vma=False
    )
```

```python
import functools

import jax
import jax.numpy as jnp
from jax import lax
from jax.experimental import pallas as pl
from jax.experimental.pallas import tpu as pltpu
from jax.sharding import Mesh
from jax.sharding import PartitionSpec as P

F32 = jnp.float32
BF16 = jnp.bfloat16
F16 = jnp.float16
HD = 128
VMEM_LIMIT = 12 << 20
TOK_BITS = 9
TOK = 1 << TOK_BITS
W_SCALE = 2.0**19
WO_SCALE = 2.0**18
N_SCALE = 2.0**12
NN = (((1,), (0,)), ((), ()))


def split(a):
    hi = a.astype(BF16)
    return hi, (a - hi.astype(F32)).astype(BF16)


def dot(a, b):
    return lax.dot_general(a, b, NN, preferred_element_type=F32)


def mm3s(a, b):
    (ah, al), (bh, bl) = a, b
    return dot(
        jnp.concatenate([ah, ah, al], axis=1), jnp.concatenate([bh, bl, bh], axis=0)
    )


def mm3(a, b):
    return mm3s(split(a), split(b))


def unit_rows(m):
    return m * lax.rsqrt(jnp.sum(m * m, axis=-1, keepdims=True) + 1e-06)


def count_le(ds_ref, pos):
    total = jnp.zeros(jnp.shape(pos), jnp.int32)
    for j in range(ds_ref.shape[0]):
        total = total + (ds_ref[j] <= pos).astype(jnp.int32)
    return total


def doc_info(meta_ref, ds_ref):
    pos0 = meta_ref[0] * TOK
    doc_col = count_le(ds_ref, pos0 + lax.broadcasted_iota(jnp.int32, (TOK, 1), 0))
    doc_row = count_le(ds_ref, pos0 + lax.broadcasted_iota(jnp.int32, (1, TOK), 1))
    return doc_col, doc_row, count_le(ds_ref, pos0 - 1), count_le(ds_ref, pos0 + TOK - 1)


def in_order(first, own, sib):
    return jnp.concatenate([jnp.where(first, own, sib), jnp.where(first, sib, own)], axis=0)


def part(pair, rows, cols):
    return pair[0][rows, cols], pair[1][rows, cols]


EVERY = slice(None)


def masked_gram(left, right_t, doc_col, doc_row, rows, cols, inclusive=False, scale=None):
    gram = mm3s(part(left, rows, EVERY), part(right_t, EVERY, cols))
    r = lax.broadcasted_iota(jnp.int32, gram.shape, 0) + rows.start
    c = lax.broadcasted_iota(jnp.int32, gram.shape, 1) + cols.start
    keep = (c <= r) if inclusive else (c < r)
    keep = keep & (doc_col[rows] == doc_row[:, cols])
    if scale is not None:
        gram = scale[rows] * gram
    return jnp.where(keep, gram, 0.0)


def pack_kernel(meta_ref, w_ref, codes_ref, give_ref, mine_ref):
    first = meta_ref[1] == 0
    codes = codes_ref[...].astype(F32)
    other = jnp.where(first, codes[1:2], codes[0:1])
    row = lax.broadcasted_iota(jnp.int32, (HD, HD), 0)
    give_ref[:, 3 * HD :] = jnp.where(row == 0, other[:, :HD], other[:, HD:]).astype(BF16)
    for p in range(3):
        cols = slice(HD * p, HD * p + HD)
        left = w_ref[p, :, :HD].astype(F32)
        right = w_ref[p, :, HD:].astype(F32)
        mine_ref[:, cols] = jnp.where(first, left, right).astype(BF16)
        give_ref[:, cols] = jnp.where(first, right, left).astype(BF16)


def far_reach(ds_ref, chips):
    count = ds_ref.shape[0]
    blocks = [ds_ref[j] >> TOK_BITS for j in range(count)]
    gap = chips - 1 - blocks[count - 1]
    for j in range(count - 1):
        gap = jnp.maximum(gap, blocks[j + 1] - blocks[j])
    return (gap > 7).astype(jnp.int32)


def local_kernel(
    chips,
    meta_ref,
    ds_ref,
    own_ref,
    sib_ref,
    codes_ref,
    got_ref,
    tl_ref,
    tl16_ref,
    wu_ref,
    kt_ref,
    far_ref,
):
    far_ref[0] = far_reach(ds_ref, chips)
    first = meta_ref[1] == 0
    half = TOK // 2
    kv = in_order(first, own_ref[...].astype(F32), sib_ref[...].astype(F32))
    key = unit_rows(kv[:, :HD])
    value = kv[:, HD:]
    codes = codes_ref[...].astype(F32)
    own_codes = jnp.where(first, codes[0:1], codes[1:2])
    got = got_ref[0:8, 3 * HD :].astype(F32)
    sib_codes = jnp.concatenate([got[0:1], got[1:2]], axis=1)
    codes = jnp.concatenate(
        [jnp.where(first, own_codes, sib_codes), jnp.where(first, sib_codes, own_codes)], axis=1
    )
    beta = 1.6 + 0.1 * jnp.transpose(jnp.broadcast_to(codes, (8, TOK)))[:, 0:1]
    doc_col, doc_row, prev_doc, last_doc = doc_info(meta_ref, ds_ref)
    carry_in = (doc_col == prev_doc).astype(F32)
    tail_row = (doc_row == last_doc).astype(F32)
    last_keep = (last_doc == prev_doc).astype(F32)

    key_s = split(key)
    key_t = jnp.transpose(key)
    kt_ref[...] = key_t
    key_ts = split(key_t)

    def system(rows, cols):
        return masked_gram(key_s, key_ts, doc_col, doc_row, rows, cols, scale=beta)

    quarter = [slice(128 * i, 128 * i + 128) for i in range(4)]
    rows128 = lax.broadcasted_iota(jnp.int32, (128, 128), 0)
    cols128 = lax.broadcasted_iota(jnp.int32, (128, 128), 1)
    eye128 = (rows128 == cols128).astype(F32)
    diag = [system(s, s) for s in quarter]
    inv = []
    for a in diag:
        m = ((rows128 >> 1) == (cols128 >> 1)) & (rows128 != cols128)
        inv.append(eye128 - jnp.where(m, a, 0.0))
    for lev in range(1, 7):
        m = ((rows128 >> (lev + 1)) == (cols128 >> (lev + 1))) & (
            (rows128 >> lev) != (cols128 >> lev)
        )
        xs = [split(x) for x in inv]
        ys = [mm3s(x, split(jnp.where(m, a, 0.0))) for x, a in zip(xs, diag)]
        inv = [x - mm3s(split(y), s) for x, y, s in zip(inv, ys, xs)]
    pair_inv = []
    for i in (0, 2):
        off = system(quarter[i + 1], quarter[i])
        low = -mm3(mm3(inv[i + 1], off), inv[i])
        top = jnp.concatenate([inv[i], jnp.zeros((128, 128), F32)], axis=1)
        bottom = jnp.concatenate([low, inv[i + 1]], axis=1)
        pair_inv.append(jnp.concatenate([top, bottom], axis=0))
    lo, hi = slice(0, half), slice(half, TOK)
    right = beta * jnp.concatenate([carry_in * key, value], axis=1)
    cross = system(hi, lo)
    wu_lo = mm3(pair_inv[0], right[lo])
    wu_lo_s = split(wu_lo)
    wu_hi = mm3(pair_inv[1], right[hi] - mm3s(split(cross), wu_lo_s))
    wu_hi_s = split(wu_hi)
    wu_s = tuple(jnp.concatenate([x, y], axis=0) for x, y in zip(wu_lo_s, wu_hi_s))
    tl = mm3s(split(tail_row * key_t), wu_s)
    tl_ref[:, :HD] = last_keep * eye128 - tl[:, :HD]
    tl_ref[:, HD:] = tl[:, HD:]
    tl16_ref[...] = tl_ref[...].astype(BF16)
    wu_ref[lo, :] = wu_lo
    wu_ref[hi, :] = wu_hi


def query_kernel(meta_ref, ds_ref, own_ref, sib_ref, kt_ref, wu_ref, b_ref):
    first = meta_ref[1] == 0
    half = TOK // 2
    query = unit_rows(in_order(first, own_ref[...].astype(F32), sib_ref[...].astype(F32)))
    doc_col, doc_row, prev_doc, _ = doc_info(meta_ref, ds_ref)
    carry_in = (doc_col == prev_doc).astype(F32)
    query_s = split(query)
    key_ts = split(kt_ref[...])
    wu_s = split(wu_ref[...])
    lo, hi = slice(0, half), slice(half, TOK)

    def probs(rows, cols):
        return masked_gram(query_s, key_ts, doc_col, doc_row, rows, cols, inclusive=True)

    out_lo = mm3s(split(probs(lo, lo)), part(wu_s, lo, EVERY))
    out_hi = mm3s(split(probs(hi, slice(0, TOK))), wu_s)
    b_ref[0, lo, :] = carry_in[lo] * query[lo] - out_lo[:, :HD]
    b_ref[0, hi, :] = carry_in[hi] * query[hi] - out_hi[:, :HD]
    b_ref[1, lo, :] = out_lo[:, HD:]
    b_ref[1, hi, :] = out_hi[:, HD:]


def after(later, earlier):
    product = mm3(later[:, :HD], earlier)
    return jnp.concatenate([product[:, :HD], product[:, HD:] + later[:, HD:]], axis=1)


def pair_kernel(tl_ref, one_ref, two_ref):
    later = tl_ref[...]
    hi, lo = split(later[:, :HD])
    one = one_ref[...]
    product = dot(jnp.concatenate([hi, lo], axis=1), jnp.concatenate([one, one], axis=0))
    two_ref[:, :HD] = product[:, :HD].astype(BF16)
    two_ref[:, HD:] = (product[:, HD:] + later[:, HD:]).astype(BF16)


def window_kernel(tl_ref, one_ref, two_ref, pre_ref, four_t_ref, four_l_ref):
    product = dot(one_ref[:, :HD], two_ref[...])
    pre = jnp.concatenate([product[:, :HD], product[:, HD:] + one_ref[:, HD:].astype(F32)], axis=1)
    pre_ref[...] = pre
    four = after(tl_ref[...], pre).astype(BF16)
    four_t_ref[...] = four[:, :HD]
    four_l_ref[...] = four[:, HD:]


def finish_kernel(meta_ref, pre_ref, four_ref, extra_ref, b_ref, out_ref):
    first = meta_ref[1] == 0
    half = TOK // 2
    state = four_ref[...].astype(F32) + extra_ref[...]
    state = mm3(pre_ref[:, :HD], state) + pre_ref[:, HD:]
    out = mm3(b_ref[0], state) + b_ref[1]
    out = out * lax.rsqrt(jnp.mean(out * out, axis=-1, keepdims=True) + 1e-05)
    low, high = out[:half], out[half:]
    out_ref[:half, :] = jnp.where(first, high, low).astype(BF16)
    out_ref[half:, :] = jnp.where(first, low, high).astype(BF16)


SMEM = pl.BlockSpec(memory_space=pltpu.SMEM)
VMEM = pl.BlockSpec(memory_space=pltpu.VMEM)


def call(kernel, scalars, arrays, outs, flops):
    return pl.pallas_call(
        kernel,
        out_shape=tuple(jax.ShapeDtypeStruct(s, d) for s, d in outs),
        in_specs=[SMEM] * len(scalars) + [VMEM] * len(arrays),
        out_specs=(VMEM,) * len(outs),
        compiler_params=pltpu.CompilerParams(vmem_limit_bytes=VMEM_LIMIT),
        cost_estimate=pl.CostEstimate(flops=flops, bytes_accessed=1 << 20, transcendentals=0),
    )(*scalars, *arrays)


def swap(value):
    return lax.ppermute(value, "c", [(0, 1), (1, 0)])


def ahead(value, steps):
    chips = lax.axis_size("z")
    return lax.ppermute(value, "z", [(i, i + steps) for i in range(chips - steps)])


def to_f16(value, scale):
    return (value.astype(F32) * scale).astype(F16)


def from_f16(value, scale):
    return (value.astype(F32) * (1.0 / scale)).astype(BF16)


def per_device(hidden_in, w_qkv, doc_starts, beta_codes, w_out):
    z = lax.axis_index("z")
    c = lax.axis_index("c")
    first = c == 0
    chips = lax.axis_size("z")
    heads = lax.axis_size("h")
    half = hidden_in.shape[0]
    meta = jnp.stack([z, c]).astype(jnp.int32)
    codes = beta_codes.T

    turned = [
        ((i * 2 + k) * heads + j, (j * 2 + k) * heads + i)
        for i in range(chips)
        for k in range(2)
        for j in range(heads)
    ]
    wo = lax.ppermute(w_out, ("z", "c", "h"), turned)
    give, mine = call(
        pack_kernel,
        (meta,),
        (w_qkv, codes),
        [((HD, 4 * HD), BF16), ((HD, 3 * HD), BF16)],
        1 << 20,
    )
    got = swap(give)
    hidden_sib = swap(hidden_in)

    other = got[:, : 3 * HD]
    w_chip = jnp.concatenate(
        [jnp.where(first, mine, other), jnp.where(first, other, mine)], axis=0
    )
    both = jnp.concatenate(
        [to_f16(w_chip, W_SCALE), to_f16(wo, WO_SCALE)], axis=1
    )
    both = lax.all_gather(both, "z", axis=0, tiled=True)
    q_all, kv_all, wo_all = both[:, :HD], both[:, HD : 3 * HD], both[:, 3 * HD :]

    def project(hid, weights):
        weights = from_f16(weights, W_SCALE)
        return jnp.dot(hid, weights, preferred_element_type=F32).astype(BF16)

    tl, tl16, wu, key_t, far = pl.pallas_call(
        functools.partial(local_kernel, chips),
        out_shape=(
            jax.ShapeDtypeStruct((HD, 2 * HD), F32),
            jax.ShapeDtypeStruct((HD, 2 * HD), BF16),
            jax.ShapeDtypeStruct((TOK, 2 * HD), F32),
            jax.ShapeDtypeStruct((HD, TOK), F32),
            jax.ShapeDtypeStruct((1,), jnp.int32),
        ),
        in_specs=[SMEM, SMEM, VMEM, VMEM, VMEM, VMEM],
        out_specs=(VMEM, VMEM, VMEM, VMEM, SMEM),
        compiler_params=pltpu.CompilerParams(vmem_limit_bytes=VMEM_LIMIT),
        cost_estimate=pl.CostEstimate(flops=3 << 30, bytes_accessed=1 << 20, transcendentals=0),
    )(
        meta,
        doc_starts,
        project(hidden_in, kv_all),
        project(hidden_sib, kv_all),
        codes,
        got,
    )
    q_all, _ = lax.optimization_barrier((q_all, tl16))
    (b,) = call(
        query_kernel,
        (meta, doc_starts),
        (project(hidden_in, q_all), project(hidden_sib, q_all), key_t, wu),
        [((2, TOK, HD), F32)],
        1 << 30,
    )
    one = ahead(tl16, 1)
    (two,) = call(pair_kernel, (), (tl, one), [((HD, 2 * HD), BF16)], 1 << 26)
    two = ahead(two, 2)
    wo_all, _ = lax.optimization_barrier((wo_all, one))
    wo_all = wo_all.reshape(chips, 2, HD, HD)
    wo_keep = from_f16(jnp.where(first, wo_all[:, 0], wo_all[:, 1]), WO_SCALE)
    wo_sent = from_f16(jnp.where(first, wo_all[:, 1], wo_all[:, 0]), WO_SCALE)
    wo_got = swap(wo_sent)
    wo_cols = jnp.concatenate(
        [jnp.where(first, wo_keep, wo_got), jnp.where(first, wo_got, wo_keep)], axis=2
    )
    pre, four_t, four_l = call(
        window_kernel,
        (),
        (tl, one, two),
        [((HD, 2 * HD), F32), ((HD, HD), BF16), ((HD, HD), BF16)],
        1 << 26,
    )

    def fetch_far(t, add):
        eight_t, eight_l, twelve = ahead(t, 8), ahead(add, 8), ahead(add, 12)
        state = jnp.dot(eight_t, twelve, preferred_element_type=F32) + eight_l.astype(F32)
        return jnp.dot(ahead(t, 4).astype(F32), state, precision=lax.Precision.HIGHEST)

    extra = lax.cond(
        far[0] > 0, fetch_far, lambda t, add: jnp.zeros((HD, HD), F32), four_t, four_l
    )
    (normed,) = call(
        finish_kernel,
        (meta,),
        (pre, ahead(four_l, 4), extra, b),
        [((TOK, HD), BF16)],
        1 << 28,
    )
    normed_all = lax.all_gather(to_f16(normed, N_SCALE), "h", axis=0)
    def output(rows):
        rows = from_f16(rows, N_SCALE)
        return jnp.einsum("htf,hfn->tn", rows, wo_cols, preferred_element_type=F32)

    sent = swap(output(normed_all[:, :half]))
    kept = lax.optimization_barrier(output(normed_all[:, half:]))
    return (kept + sent).astype(BF16)


def solution(mesh):
    seq, head = mesh.devices.shape
    fine = Mesh(mesh.devices.reshape(seq // 2, 2, head), ("z", "c", "h"))
    tokens = ("z", "c")
    in_specs = (P(tokens, None), P(None, tokens, "h"), P(), P(tokens, "h"), P("h", tokens))
    return jax.shard_map(
        per_device, mesh=fine, in_specs=in_specs, out_specs=P(tokens, "h"), check_vma=False
    )
```

```python
import functools

import jax
import jax.numpy as jnp
from jax import lax
from jax.experimental import pallas as pl
from jax.experimental.pallas import tpu as pltpu
from jax.sharding import Mesh
from jax.sharding import PartitionSpec as P

F32 = jnp.float32
BF16 = jnp.bfloat16
F16 = jnp.float16
HD = 128
VMEM_LIMIT = 12 << 20
TOK_BITS = 9
TOK = 1 << TOK_BITS
W_SCALE = 2.0**19
WO_SCALE = 2.0**18
N_SCALE = 2.0**12
NN = (((1,), (0,)), ((), ()))


def split(a):
    hi = a.astype(BF16)
    return hi, (a - hi.astype(F32)).astype(BF16)


def dot(a, b):
    return lax.dot_general(a, b, NN, preferred_element_type=F32)


def mm3s(a, b):
    (ah, al), (bh, bl) = a, b
    return dot(
        jnp.concatenate([ah, ah, al], axis=1), jnp.concatenate([bh, bl, bh], axis=0)
    )


def mm3(a, b):
    return mm3s(split(a), split(b))


def unit_rows(m):
    return m * lax.rsqrt(jnp.sum(m * m, axis=-1, keepdims=True) + 1e-06)


def count_le(ds_ref, pos):
    total = jnp.zeros(jnp.shape(pos), jnp.int32)
    for j in range(ds_ref.shape[0]):
        total = total + (ds_ref[j] <= pos).astype(jnp.int32)
    return total


def doc_info(meta_ref, ds_ref):
    pos0 = meta_ref[0] * TOK
    doc_col = count_le(ds_ref, pos0 + lax.broadcasted_iota(jnp.int32, (TOK, 1), 0))
    doc_row = count_le(ds_ref, pos0 + lax.broadcasted_iota(jnp.int32, (1, TOK), 1))
    return doc_col, doc_row, count_le(ds_ref, pos0 - 1), count_le(ds_ref, pos0 + TOK - 1)


def in_order(first, own, sib):
    return jnp.concatenate([jnp.where(first, own, sib), jnp.where(first, sib, own)], axis=0)


def part(pair, rows, cols):
    return pair[0][rows, cols], pair[1][rows, cols]


EVERY = slice(None)


def masked_gram(left, right_t, doc_col, doc_row, rows, cols, inclusive=False, scale=None):
    gram = mm3s(part(left, rows, EVERY), part(right_t, EVERY, cols))
    r = lax.broadcasted_iota(jnp.int32, gram.shape, 0) + rows.start
    c = lax.broadcasted_iota(jnp.int32, gram.shape, 1) + cols.start
    keep = (c <= r) if inclusive else (c < r)
    keep = keep & (doc_col[rows] == doc_row[:, cols])
    if scale is not None:
        gram = scale[rows] * gram
    return jnp.where(keep, gram, 0.0)


def pack_kernel(meta_ref, w_ref, codes_ref, give_ref, mine_ref):
    first = meta_ref[1] == 0
    codes = codes_ref[...].astype(F32)
    other = jnp.where(first, codes[1:2], codes[0:1])
    row = lax.broadcasted_iota(jnp.int32, (HD, HD), 0)
    give_ref[:, 3 * HD :] = jnp.where(row == 0, other[:, :HD], other[:, HD:]).astype(BF16)
    for p in range(3):
        cols = slice(HD * p, HD * p + HD)
        left = w_ref[p, :, :HD].astype(F32)
        right = w_ref[p, :, HD:].astype(F32)
        mine_ref[:, cols] = jnp.where(first, left, right).astype(BF16)
        give_ref[:, cols] = jnp.where(first, right, left).astype(BF16)


def far_reach(ds_ref, chips):
    count = ds_ref.shape[0]
    blocks = [ds_ref[j] >> TOK_BITS for j in range(count)]
    gap = chips - 1 - blocks[count - 1]
    for j in range(count - 1):
        gap = jnp.maximum(gap, blocks[j + 1] - blocks[j])
    return (gap > 7).astype(jnp.int32) + (gap > 11).astype(jnp.int32)


def local_kernel(
    chips,
    meta_ref,
    ds_ref,
    own_ref,
    sib_ref,
    codes_ref,
    got_ref,
    tl_ref,
    tl16_ref,
    wu_ref,
    kt_ref,
    far_ref,
):
    far_ref[0] = far_reach(ds_ref, chips)
    first = meta_ref[1] == 0
    half = TOK // 2
    qkv = in_order(first, own_ref[...].astype(F32), sib_ref[...].astype(F32))
    key = unit_rows(qkv[:, HD : 2 * HD])
    value = qkv[:, 2 * HD :]
    codes = codes_ref[...].astype(F32)
    own_codes = jnp.where(first, codes[0:1], codes[1:2])
    got = got_ref[0:8, 3 * HD :].astype(F32)
    sib_codes = jnp.concatenate([got[0:1], got[1:2]], axis=1)
    codes = jnp.concatenate(
        [jnp.where(first, own_codes, sib_codes), jnp.where(first, sib_codes, own_codes)], axis=1
    )
    beta = 1.6 + 0.1 * jnp.transpose(jnp.broadcast_to(codes, (8, TOK)))[:, 0:1]
    doc_col, doc_row, prev_doc, last_doc = doc_info(meta_ref, ds_ref)
    carry_in = (doc_col == prev_doc).astype(F32)
    tail_row = (doc_row == last_doc).astype(F32)
    last_keep = (last_doc == prev_doc).astype(F32)

    key_s = split(key)
    key_t = jnp.transpose(key)
    kt_ref[...] = key_t
    key_ts = split(key_t)

    def system(rows, cols):
        return masked_gram(key_s, key_ts, doc_col, doc_row, rows, cols, scale=beta)

    quarter = [slice(128 * i, 128 * i + 128) for i in range(4)]
    rows128 = lax.broadcasted_iota(jnp.int32, (128, 128), 0)
    cols128 = lax.broadcasted_iota(jnp.int32, (128, 128), 1)
    eye128 = (rows128 == cols128).astype(F32)
    diag = [system(s, s) for s in quarter]
    inv = []
    for a in diag:
        m = ((rows128 >> 1) == (cols128 >> 1)) & (rows128 != cols128)
        inv.append(eye128 - jnp.where(m, a, 0.0))
    for lev in range(1, 7):
        m = ((rows128 >> (lev + 1)) == (cols128 >> (lev + 1))) & (
            (rows128 >> lev) != (cols128 >> lev)
        )
        xs = [split(x) for x in inv]
        ys = [mm3s(x, split(jnp.where(m, a, 0.0))) for x, a in zip(xs, diag)]
        inv = [x - mm3s(split(y), s) for x, y, s in zip(inv, ys, xs)]
    pair_inv = []
    for i in (0, 2):
        off = system(quarter[i + 1], quarter[i])
        low = -mm3(mm3(inv[i + 1], off), inv[i])
        top = jnp.concatenate([inv[i], jnp.zeros((128, 128), F32)], axis=1)
        bottom = jnp.concatenate([low, inv[i + 1]], axis=1)
        pair_inv.append(jnp.concatenate([top, bottom], axis=0))
    lo, hi = slice(0, half), slice(half, TOK)
    right = beta * jnp.concatenate([carry_in * key, value], axis=1)
    cross = system(hi, lo)
    wu_lo = mm3(pair_inv[0], right[lo])
    wu_lo_s = split(wu_lo)
    wu_hi = mm3(pair_inv[1], right[hi] - mm3s(split(cross), wu_lo_s))
    wu_hi_s = split(wu_hi)
    wu_s = tuple(jnp.concatenate([x, y], axis=0) for x, y in zip(wu_lo_s, wu_hi_s))
    tl = mm3s(split(tail_row * key_t), wu_s)
    tl_ref[:, :HD] = last_keep * eye128 - tl[:, :HD]
    tl_ref[:, HD:] = tl[:, HD:]
    tl16_ref[...] = tl_ref[...].astype(BF16)
    wu_ref[lo, :] = wu_lo
    wu_ref[hi, :] = wu_hi


def query_kernel(meta_ref, ds_ref, own_ref, sib_ref, kt_ref, wu_ref, b_ref):
    first = meta_ref[1] == 0
    half = TOK // 2
    query = unit_rows(in_order(first, own_ref[:, :HD].astype(F32), sib_ref[:, :HD].astype(F32)))
    doc_col, doc_row, prev_doc, _ = doc_info(meta_ref, ds_ref)
    carry_in = (doc_col == prev_doc).astype(F32)
    query_s = split(query)
    key_ts = split(kt_ref[...])
    wu_s = split(wu_ref[...])
    lo, hi = slice(0, half), slice(half, TOK)

    def probs(rows, cols):
        return masked_gram(query_s, key_ts, doc_col, doc_row, rows, cols, inclusive=True)

    out_lo = mm3s(split(probs(lo, lo)), part(wu_s, lo, EVERY))
    out_hi = mm3s(split(probs(hi, slice(0, TOK))), wu_s)
    b_ref[0, lo, :] = carry_in[lo] * query[lo] - out_lo[:, :HD]
    b_ref[0, hi, :] = carry_in[hi] * query[hi] - out_hi[:, :HD]
    b_ref[1, lo, :] = out_lo[:, HD:]
    b_ref[1, hi, :] = out_hi[:, HD:]


def after(later, earlier):
    product = mm3(later[:, :HD], earlier)
    return jnp.concatenate([product[:, :HD], product[:, HD:] + later[:, HD:]], axis=1)


def pair_kernel(tl_ref, one_ref, two_ref):
    later = tl_ref[...]
    hi, lo = split(later[:, :HD])
    one = one_ref[...]
    product = dot(jnp.concatenate([hi, lo], axis=1), jnp.concatenate([one, one], axis=0))
    two_ref[:, :HD] = product[:, :HD].astype(BF16)
    two_ref[:, HD:] = (product[:, HD:] + later[:, HD:]).astype(BF16)


def window_kernel(tl_ref, one_ref, two_ref, pre_ref, four_t_ref, four_l_ref):
    product = dot(one_ref[:, :HD], two_ref[...])
    pre = jnp.concatenate([product[:, :HD], product[:, HD:] + one_ref[:, HD:].astype(F32)], axis=1)
    pre_ref[...] = pre
    four = after(tl_ref[...], pre).astype(BF16)
    four_t_ref[...] = four[:, :HD]
    four_l_ref[...] = four[:, HD:]


def finish_kernel(meta_ref, pre_ref, four_ref, extra_ref, b_ref, out_ref):
    first = meta_ref[1] == 0
    half = TOK // 2
    state = four_ref[...].astype(F32) + extra_ref[...]
    state = mm3(pre_ref[:, :HD], state) + pre_ref[:, HD:]
    out = mm3(b_ref[0], state) + b_ref[1]
    out = out * lax.rsqrt(jnp.mean(out * out, axis=-1, keepdims=True) + 1e-05)
    low, high = out[:half], out[half:]
    out_ref[:half, :] = jnp.where(first, high, low).astype(BF16)
    out_ref[half:, :] = jnp.where(first, low, high).astype(BF16)


SMEM = pl.BlockSpec(memory_space=pltpu.SMEM)
VMEM = pl.BlockSpec(memory_space=pltpu.VMEM)


def call(kernel, scalars, arrays, outs, flops):
    return pl.pallas_call(
        kernel,
        out_shape=tuple(jax.ShapeDtypeStruct(s, d) for s, d in outs),
        in_specs=[SMEM] * len(scalars) + [VMEM] * len(arrays),
        out_specs=(VMEM,) * len(outs),
        compiler_params=pltpu.CompilerParams(vmem_limit_bytes=VMEM_LIMIT),
        cost_estimate=pl.CostEstimate(flops=flops, bytes_accessed=1 << 20, transcendentals=0),
    )(*scalars, *arrays)


def swap(value):
    return lax.ppermute(value, "c", [(0, 1), (1, 0)])


def ahead(value, steps):
    chips = lax.axis_size("z")
    return lax.ppermute(value, "z", [(i, i + steps) for i in range(chips - steps)])


def to_f16(value, scale):
    return (value.astype(F32) * scale).astype(F16)


def from_f16(value, scale):
    return (value.astype(F32) * (1.0 / scale)).astype(BF16)


def per_device(hidden_in, w_qkv, doc_starts, beta_codes, w_out):
    z = lax.axis_index("z")
    c = lax.axis_index("c")
    first = c == 0
    chips = lax.axis_size("z")
    heads = lax.axis_size("h")
    half = hidden_in.shape[0]
    meta = jnp.stack([z, c]).astype(jnp.int32)
    codes = beta_codes.T

    turned = [
        ((i * 2 + k) * heads + j, (j * 2 + k) * heads + i)
        for i in range(chips)
        for k in range(2)
        for j in range(heads)
    ]
    wo = lax.ppermute(w_out, ("z", "c", "h"), turned)
    give, mine = call(
        pack_kernel,
        (meta,),
        (w_qkv, codes),
        [((HD, 4 * HD), BF16), ((HD, 3 * HD), BF16)],
        1 << 20,
    )
    got = swap(give)
    hidden_sib = swap(hidden_in)

    other = got[:, : 3 * HD]
    w_chip = jnp.concatenate(
        [jnp.where(first, mine, other), jnp.where(first, other, mine)], axis=0
    )
    both = jnp.concatenate(
        [to_f16(w_chip, W_SCALE), to_f16(wo, WO_SCALE)], axis=1
    )
    both = lax.all_gather(both, "z", axis=0, tiled=True)
    w_all, wo_all = from_f16(both[:, : 3 * HD], W_SCALE), both[:, 3 * HD :]

    def project(hid):
        return jnp.dot(hid, w_all, preferred_element_type=F32).astype(BF16)

    own, sib = project(hidden_in), project(hidden_sib)
    tl, tl16, wu, key_t, far = pl.pallas_call(
        functools.partial(local_kernel, chips),
        out_shape=(
            jax.ShapeDtypeStruct((HD, 2 * HD), F32),
            jax.ShapeDtypeStruct((HD, 2 * HD), BF16),
            jax.ShapeDtypeStruct((TOK, 2 * HD), F32),
            jax.ShapeDtypeStruct((HD, TOK), F32),
            jax.ShapeDtypeStruct((1,), jnp.int32),
        ),
        in_specs=[SMEM, SMEM, VMEM, VMEM, VMEM, VMEM],
        out_specs=(VMEM, VMEM, VMEM, VMEM, SMEM),
        compiler_params=pltpu.CompilerParams(vmem_limit_bytes=VMEM_LIMIT),
        cost_estimate=pl.CostEstimate(flops=3 << 30, bytes_accessed=1 << 20, transcendentals=0),
    )(meta, doc_starts, own, sib, codes, got)
    (b,) = call(
        query_kernel,
        (meta, doc_starts),
        (own, sib, key_t, wu),
        [((2, TOK, HD), F32)],
        1 << 30,
    )
    one = ahead(tl16, 1)
    (two,) = call(pair_kernel, (), (tl, one), [((HD, 2 * HD), BF16)], 1 << 26)
    two = ahead(two, 2)
    wo_all, _ = lax.optimization_barrier((wo_all, tl16))
    wo_all = wo_all.reshape(chips, 2, HD, HD)
    wo_keep = from_f16(jnp.where(first, wo_all[:, 0], wo_all[:, 1]), WO_SCALE)
    wo_sent = from_f16(jnp.where(first, wo_all[:, 1], wo_all[:, 0]), WO_SCALE)
    wo_got = swap(wo_sent)
    wo_cols = jnp.concatenate(
        [jnp.where(first, wo_keep, wo_got), jnp.where(first, wo_got, wo_keep)], axis=2
    )
    pre, four_t, four_l = call(
        window_kernel,
        (),
        (tl, one, two),
        [((HD, 2 * HD), F32), ((HD, HD), BF16), ((HD, HD), BF16)],
        1 << 26,
    )

    def through_four(t, state):
        return jnp.dot(ahead(t, 4).astype(F32), state, precision=lax.Precision.HIGHEST)

    def fetch_none(t, add):
        return jnp.zeros((HD, HD), F32)

    def fetch_eight(t, add):
        return through_four(t, ahead(add, 8).astype(F32))

    def fetch_twelve(t, add):
        eight_t, eight_l, twelve = ahead(t, 8), ahead(add, 8), ahead(add, 12)
        state = jnp.dot(eight_t, twelve, preferred_element_type=F32) + eight_l.astype(F32)
        return through_four(t, state)

    extra = lax.switch(far[0], (fetch_none, fetch_eight, fetch_twelve), four_t, four_l)
    (normed,) = call(
        finish_kernel,
        (meta,),
        (pre, ahead(four_l, 4), extra, b),
        [((TOK, HD), BF16)],
        1 << 28,
    )
    normed_all = lax.all_gather(to_f16(normed, N_SCALE), "h", axis=0)
    def output(rows):
        rows = from_f16(rows, N_SCALE)
        return jnp.einsum("htf,hfn->tn", rows, wo_cols, preferred_element_type=F32)

    sent = swap(output(normed_all[:, :half]))
    kept = lax.optimization_barrier(output(normed_all[:, half:]))
    return (kept + sent).astype(BF16)


def solution(mesh):
    seq, head = mesh.devices.shape
    fine = Mesh(mesh.devices.reshape(seq // 2, 2, head), ("z", "c", "h"))
    tokens = ("z", "c")
    in_specs = (P(tokens, None), P(None, tokens, "h"), P(), P(tokens, "h"), P("h", tokens))
    return jax.shard_map(
        per_device, mesh=fine, in_specs=in_specs, out_specs=P(tokens, "h"), check_vma=False
    )
```

```python
import functools

import jax
import jax.numpy as jnp
from jax import lax
from jax.experimental import pallas as pl
from jax.experimental.pallas import tpu as pltpu
from jax.sharding import Mesh
from jax.sharding import PartitionSpec as P

F32 = jnp.float32
BF16 = jnp.bfloat16
F16 = jnp.float16
HD = 128
VMEM_LIMIT = 12 << 20
TOK_BITS = 9
TOK = 1 << TOK_BITS
W_SCALE = 2.0**19
WO_SCALE = 2.0**18
N_SCALE = 2.0**12
NN = (((1,), (0,)), ((), ()))


def split(a):
    hi = a.astype(BF16)
    return hi, (a - hi.astype(F32)).astype(BF16)


def dot(a, b):
    return lax.dot_general(a, b, NN, preferred_element_type=F32)


def mm3s(a, b):
    (ah, al), (bh, bl) = a, b
    return dot(
        jnp.concatenate([ah, ah, al], axis=1), jnp.concatenate([bh, bl, bh], axis=0)
    )


def mm3(a, b):
    return mm3s(split(a), split(b))


def unit_rows(m):
    return m * lax.rsqrt(jnp.sum(m * m, axis=-1, keepdims=True) + 1e-06)


def count_le(ds_ref, pos):
    total = jnp.zeros(jnp.shape(pos), jnp.int32)
    for j in range(ds_ref.shape[0]):
        total = total + (ds_ref[j] <= pos).astype(jnp.int32)
    return total


def doc_info(meta_ref, ds_ref):
    pos0 = meta_ref[0] * TOK
    doc_col = count_le(ds_ref, pos0 + lax.broadcasted_iota(jnp.int32, (TOK, 1), 0))
    doc_row = count_le(ds_ref, pos0 + lax.broadcasted_iota(jnp.int32, (1, TOK), 1))
    return doc_col, doc_row, count_le(ds_ref, pos0 - 1), count_le(ds_ref, pos0 + TOK - 1)


def in_order(first, own, sib):
    return jnp.concatenate([jnp.where(first, own, sib), jnp.where(first, sib, own)], axis=0)


def part(pair, rows, cols):
    return pair[0][rows, cols], pair[1][rows, cols]


EVERY = slice(None)


def masked_gram(left, right_t, doc_col, doc_row, rows, cols, inclusive=False, scale=None):
    gram = mm3s(part(left, rows, EVERY), part(right_t, EVERY, cols))
    r = lax.broadcasted_iota(jnp.int32, gram.shape, 0) + rows.start
    c = lax.broadcasted_iota(jnp.int32, gram.shape, 1) + cols.start
    keep = (c <= r) if inclusive else (c < r)
    keep = keep & (doc_col[rows] == doc_row[:, cols])
    if scale is not None:
        gram = scale[rows] * gram
    return jnp.where(keep, gram, 0.0)


def pack_kernel(meta_ref, w_ref, codes_ref, give_ref, mine_ref):
    first = meta_ref[1] == 0
    codes = codes_ref[...].astype(F32)
    other = jnp.where(first, codes[1:2], codes[0:1])
    row = lax.broadcasted_iota(jnp.int32, (HD, HD), 0)
    give_ref[:, 3 * HD :] = jnp.where(row == 0, other[:, :HD], other[:, HD:]).astype(BF16)
    for p in range(3):
        cols = slice(HD * p, HD * p + HD)
        left = w_ref[p, :, :HD].astype(F32)
        right = w_ref[p, :, HD:].astype(F32)
        mine_ref[:, cols] = jnp.where(first, left, right).astype(BF16)
        give_ref[:, cols] = jnp.where(first, right, left).astype(BF16)


def far_reach(ds_ref, chips):
    count = ds_ref.shape[0]
    blocks = [ds_ref[j] >> TOK_BITS for j in range(count)]
    gap = chips - 1 - blocks[count - 1]
    for j in range(count - 1):
        gap = jnp.maximum(gap, blocks[j + 1] - blocks[j])
    return (gap > 7).astype(jnp.int32)


def local_kernel(
    chips,
    meta_ref,
    ds_ref,
    own_ref,
    sib_ref,
    codes_ref,
    got_ref,
    tl_ref,
    tl16_ref,
    wu_ref,
    kt_ref,
    far_ref,
):
    far_ref[0] = far_reach(ds_ref, chips)
    first = meta_ref[1] == 0
    half = TOK // 2
    qkv = in_order(first, own_ref[...].astype(F32), sib_ref[...].astype(F32))
    key = unit_rows(qkv[:, HD : 2 * HD])
    value = qkv[:, 2 * HD :]
    codes = codes_ref[...].astype(F32)
    own_codes = jnp.where(first, codes[0:1], codes[1:2])
    got = got_ref[0:8, 3 * HD :].astype(F32)
    sib_codes = jnp.concatenate([got[0:1], got[1:2]], axis=1)
    codes = jnp.concatenate(
        [jnp.where(first, own_codes, sib_codes), jnp.where(first, sib_codes, own_codes)], axis=1
    )
    beta = 1.6 + 0.1 * jnp.transpose(jnp.broadcast_to(codes, (8, TOK)))[:, 0:1]
    doc_col, doc_row, prev_doc, last_doc = doc_info(meta_ref, ds_ref)
    carry_in = (doc_col == prev_doc).astype(F32)
    tail_row = (doc_row == last_doc).astype(F32)
    last_keep = (last_doc == prev_doc).astype(F32)

    key_s = split(key)
    key_t = jnp.transpose(key)
    kt_ref[...] = key_t
    key_ts = split(key_t)

    def system(rows, cols):
        return masked_gram(key_s, key_ts, doc_col, doc_row, rows, cols, scale=beta)

    quarter = [slice(128 * i, 128 * i + 128) for i in range(4)]
    rows128 = lax.broadcasted_iota(jnp.int32, (128, 128), 0)
    cols128 = lax.broadcasted_iota(jnp.int32, (128, 128), 1)
    eye128 = (rows128 == cols128).astype(F32)
    diag = [system(s, s) for s in quarter]
    inv = []
    for a in diag:
        m = ((rows128 >> 1) == (cols128 >> 1)) & (rows128 != cols128)
        inv.append(eye128 - jnp.where(m, a, 0.0))
    for lev in range(1, 7):
        m = ((rows128 >> (lev + 1)) == (cols128 >> (lev + 1))) & (
            (rows128 >> lev) != (cols128 >> lev)
        )
        xs = [split(x) for x in inv]
        ys = [mm3s(x, split(jnp.where(m, a, 0.0))) for x, a in zip(xs, diag)]
        inv = [x - mm3s(split(y), s) for x, y, s in zip(inv, ys, xs)]
    pair_inv = []
    for i in (0, 2):
        off = system(quarter[i + 1], quarter[i])
        low = -mm3(mm3(inv[i + 1], off), inv[i])
        top = jnp.concatenate([inv[i], jnp.zeros((128, 128), F32)], axis=1)
        bottom = jnp.concatenate([low, inv[i + 1]], axis=1)
        pair_inv.append(jnp.concatenate([top, bottom], axis=0))
    lo, hi = slice(0, half), slice(half, TOK)
    right = beta * jnp.concatenate([carry_in * key, value], axis=1)
    cross = system(hi, lo)
    wu_lo = mm3(pair_inv[0], right[lo])
    wu_lo_s = split(wu_lo)
    wu_hi = mm3(pair_inv[1], right[hi] - mm3s(split(cross), wu_lo_s))
    wu_hi_s = split(wu_hi)
    wu_s = tuple(jnp.concatenate([x, y], axis=0) for x, y in zip(wu_lo_s, wu_hi_s))
    tl = mm3s(split(tail_row * key_t), wu_s)
    tl_ref[:, :HD] = last_keep * eye128 - tl[:, :HD]
    tl_ref[:, HD:] = tl[:, HD:]
    tl16_ref[...] = tl_ref[...].astype(BF16)
    wu_ref[lo, :] = wu_lo
    wu_ref[hi, :] = wu_hi


def query_kernel(meta_ref, ds_ref, own_ref, sib_ref, kt_ref, wu_ref, b_ref):
    first = meta_ref[1] == 0
    half = TOK // 2
    query = unit_rows(in_order(first, own_ref[:, :HD].astype(F32), sib_ref[:, :HD].astype(F32)))
    doc_col, doc_row, prev_doc, _ = doc_info(meta_ref, ds_ref)
    carry_in = (doc_col == prev_doc).astype(F32)
    query_s = split(query)
    key_ts = split(kt_ref[...])
    wu_s = split(wu_ref[...])
    lo, hi = slice(0, half), slice(half, TOK)

    def probs(rows, cols):
        return masked_gram(query_s, key_ts, doc_col, doc_row, rows, cols, inclusive=True)

    out_lo = mm3s(split(probs(lo, lo)), part(wu_s, lo, EVERY))
    out_hi = mm3s(split(probs(hi, slice(0, TOK))), wu_s)
    b_ref[0, lo, :] = carry_in[lo] * query[lo] - out_lo[:, :HD]
    b_ref[0, hi, :] = carry_in[hi] * query[hi] - out_hi[:, :HD]
    b_ref[1, lo, :] = out_lo[:, HD:]
    b_ref[1, hi, :] = out_hi[:, HD:]


def after(later, earlier):
    product = mm3(later[:, :HD], earlier)
    return jnp.concatenate([product[:, :HD], product[:, HD:] + later[:, HD:]], axis=1)


def pair_kernel(tl_ref, one_ref, two_ref):
    later = tl_ref[...]
    hi, lo = split(later[:, :HD])
    one = one_ref[...]
    product = dot(jnp.concatenate([hi, lo], axis=1), jnp.concatenate([one, one], axis=0))
    two_ref[:, :HD] = product[:, :HD].astype(BF16)
    two_ref[:, HD:] = (product[:, HD:] + later[:, HD:]).astype(BF16)


def window_kernel(tl_ref, one_ref, two_ref, pre_ref, four_t_ref, four_l_ref):
    product = dot(one_ref[:, :HD], two_ref[...])
    pre = jnp.concatenate([product[:, :HD], product[:, HD:] + one_ref[:, HD:].astype(F32)], axis=1)
    pre_ref[...] = pre
    four = after(tl_ref[...], pre).astype(BF16)
    four_t_ref[...] = four[:, :HD]
    four_l_ref[...] = four[:, HD:]


def finish_kernel(meta_ref, pre_ref, four_ref, extra_ref, b_ref, out_ref):
    first = meta_ref[1] == 0
    half = TOK // 2
    state = four_ref[...].astype(F32) + extra_ref[...]
    state = mm3(pre_ref[:, :HD], state) + pre_ref[:, HD:]
    out = mm3(b_ref[0], state) + b_ref[1]
    out = out * lax.rsqrt(jnp.mean(out * out, axis=-1, keepdims=True) + 1e-05)
    low, high = out[:half], out[half:]
    out_ref[:half, :] = jnp.where(first, high, low).astype(BF16)
    out_ref[half:, :] = jnp.where(first, low, high).astype(BF16)


SMEM = pl.BlockSpec(memory_space=pltpu.SMEM)
VMEM = pl.BlockSpec(memory_space=pltpu.VMEM)


def call(kernel, scalars, arrays, outs, flops):
    return pl.pallas_call(
        kernel,
        out_shape=tuple(jax.ShapeDtypeStruct(s, d) for s, d in outs),
        in_specs=[SMEM] * len(scalars) + [VMEM] * len(arrays),
        out_specs=(VMEM,) * len(outs),
        compiler_params=pltpu.CompilerParams(vmem_limit_bytes=VMEM_LIMIT),
        cost_estimate=pl.CostEstimate(flops=flops, bytes_accessed=1 << 20, transcendentals=0),
    )(*scalars, *arrays)


def swap(value):
    return lax.ppermute(value, "c", [(0, 1), (1, 0)])


def ahead(value, steps):
    chips = lax.axis_size("z")
    return lax.ppermute(value, "z", [(i, i + steps) for i in range(chips - steps)])


def to_f16(value, scale):
    return (value.astype(F32) * scale).astype(F16)


def from_f16(value, scale):
    return (value.astype(F32) * (1.0 / scale)).astype(BF16)


def per_device(hidden_in, w_qkv, doc_starts, beta_codes, w_out):
    z = lax.axis_index("z")
    c = lax.axis_index("c")
    first = c == 0
    chips = lax.axis_size("z")
    heads = lax.axis_size("h")
    half = hidden_in.shape[0]
    meta = jnp.stack([z, c]).astype(jnp.int32)
    codes = beta_codes.T

    turned = [
        ((i * 2 + k) * heads + j, (j * 2 + k) * heads + i)
        for i in range(chips)
        for k in range(2)
        for j in range(heads)
    ]
    wo = lax.ppermute(w_out, ("z", "c", "h"), turned)
    give, mine = call(
        pack_kernel,
        (meta,),
        (w_qkv, codes),
        [((HD, 4 * HD), BF16), ((HD, 3 * HD), BF16)],
        1 << 20,
    )
    got = swap(give)
    hidden_sib = swap(hidden_in)

    other = got[:, : 3 * HD]
    w_chip = jnp.concatenate(
        [jnp.where(first, mine, other), jnp.where(first, other, mine)], axis=0
    )
    both = jnp.concatenate(
        [to_f16(w_chip, W_SCALE), to_f16(wo, WO_SCALE)], axis=1
    )
    both = lax.all_gather(both, "z", axis=0, tiled=True)
    w_all, wo_all = from_f16(both[:, : 3 * HD], W_SCALE), both[:, 3 * HD :]

    def project(hid):
        return jnp.dot(hid, w_all, preferred_element_type=F32).astype(BF16)

    own, sib = project(hidden_in), project(hidden_sib)
    tl, tl16, wu, key_t, far = pl.pallas_call(
        functools.partial(local_kernel, chips),
        out_shape=(
            jax.ShapeDtypeStruct((HD, 2 * HD), F32),
            jax.ShapeDtypeStruct((HD, 2 * HD), BF16),
            jax.ShapeDtypeStruct((TOK, 2 * HD), F32),
            jax.ShapeDtypeStruct((HD, TOK), F32),
            jax.ShapeDtypeStruct((1,), jnp.int32),
        ),
        in_specs=[SMEM, SMEM, VMEM, VMEM, VMEM, VMEM],
        out_specs=(VMEM, VMEM, VMEM, VMEM, SMEM),
        compiler_params=pltpu.CompilerParams(vmem_limit_bytes=VMEM_LIMIT),
        cost_estimate=pl.CostEstimate(flops=3 << 30, bytes_accessed=1 << 20, transcendentals=0),
    )(meta, doc_starts, own, sib, codes, got)
    (b,) = call(
        query_kernel,
        (meta, doc_starts),
        (own, sib, key_t, wu),
        [((2, TOK, HD), F32)],
        1 << 30,
    )
    one = ahead(tl16, 1)
    (two,) = call(pair_kernel, (), (tl, one), [((HD, 2 * HD), BF16)], 1 << 26)
    two = ahead(two, 2)
    wo_all, _ = lax.optimization_barrier((wo_all, tl16))
    wo_all = wo_all.reshape(chips, 2, HD, HD)
    wo_keep = from_f16(jnp.where(first, wo_all[:, 0], wo_all[:, 1]), WO_SCALE)
    wo_sent = from_f16(jnp.where(first, wo_all[:, 1], wo_all[:, 0]), WO_SCALE)
    wo_got = swap(wo_sent)
    wo_cols = jnp.concatenate(
        [jnp.where(first, wo_keep, wo_got), jnp.where(first, wo_got, wo_keep)], axis=2
    )
    pre, four_t, four_l = call(
        window_kernel,
        (),
        (tl, one, two),
        [((HD, 2 * HD), F32), ((HD, HD), BF16), ((HD, HD), BF16)],
        1 << 26,
    )

    def fetch_far(t, add):
        eight_t, eight_l, twelve = ahead(t, 8), ahead(add, 8), ahead(add, 12)
        state = jnp.dot(eight_t, twelve, preferred_element_type=F32) + eight_l.astype(F32)
        return jnp.dot(ahead(t, 4).astype(F32), state, precision=lax.Precision.HIGHEST)

    extra = lax.cond(
        far[0] > 0, fetch_far, lambda t, add: jnp.zeros((HD, HD), F32), four_t, four_l
    )
    (normed,) = call(
        finish_kernel,
        (meta,),
        (pre, ahead(four_l, 4), extra, b),
        [((TOK, HD), BF16)],
        1 << 28,
    )
    normed_all = lax.all_gather(to_f16(normed, N_SCALE), "h", axis=0)
    def output(rows):
        rows = from_f16(rows, N_SCALE)
        return jnp.einsum("htf,hfn->tn", rows, wo_cols, preferred_element_type=F32)

    sent = swap(output(normed_all[:, :half]).astype(BF16)).astype(F32)
    kept = lax.optimization_barrier(output(normed_all[:, half:]))
    return (kept + sent).astype(BF16)


def solution(mesh):
    seq, head = mesh.devices.shape
    fine = Mesh(mesh.devices.reshape(seq // 2, 2, head), ("z", "c", "h"))
    tokens = ("z", "c")
    in_specs = (P(tokens, None), P(None, tokens, "h"), P(), P(tokens, "h"), P("h", tokens))
    return jax.shard_map(
        per_device, mesh=fine, in_specs=in_specs, out_specs=P(tokens, "h"), check_vma=False
    )
```
